128 devices in a mesh: row: 8 (over x_hi, y), col: 16 (over x_lo, z, core).
Axes of the slice: x: 4 (x_hi: 2, x_lo: 2; x = x_hi * 2 + x_lo), y: 4, z: 4, core: 2. Of those that a mesh axis runs over, the one named last changes fastest.
Arguments:
- activations: bfloat16 [48, 512, 2048], P('row', 'col'), may hold values from -6 to 6
- targets: int32 [48, 512], P('row', 'col'), may hold values from 0 to 255
- candidates: int32 [1024], replicated, may hold values from 0 to 24575
- mix_gain: float32 [2048], replicated, may hold values from 0.1 to 1.9
- project_weight: bfloat16 [3, 2048, 2048], P(None, None, 'col'), may hold values from -0.1875 to 0.1875
- output_weight: bfloat16 [2048, 2048], P('col'), may hold values from -0.25 to 0.25
- up_weight: bfloat16 [2048, 8192], P(None, 'col'), as said below
- down_weight: bfloat16 [8192, 2048], P('col'), as said below
- pattern_bias: float32 [16], P('col'), may hold values from 1 to 5
- head_gain: float32 [2048], replicated, may hold values from 0.1 to 1.9
- head_weight: bfloat16 [2048, 256], replicated, may hold values from -0.375 to 0.375
Outputs:
- layer_out: bfloat16 [48, 512, 2048], P('row', 'col')
- chosen: float32 [1024], replicated
The draws below stay inside these ranges and needn't reach their ends.
Inputs may be any that keep to these rules, and one draw needn't show every extreme that they name: `up_weight`: Real-valued weights of fan-in scale. `down_weight`: Real-valued weights of fan-in scale.
All inputs are finite; a program needn't handle non-finite values.
Results may differ from the reference program's by a relative error of at most 0.018.
Values may be sent and summed in bfloat16 or wider, within the bound.
No kernel may reach another device: no remote copies, remote signals or barrier semaphores. Data moves between devices by JAX's collectives and lax.ppermute only.
A program may use at most 128 MiB of HBM per device.

```python
import math
import jax
import jax.numpy as jnp
import numpy as np
from jax import lax

D = 2048
HEADS = 16
HD = 128
FF = 8192
VOCAB = 256
COLS = 512
NCAND = 1024
ROWS = 48
N_COL = 16


def ramp_scale(count, power):
    ramp_steps = jnp.arange(count, dtype=jnp.float32) / (count - 1)
    return jnp.exp(power * math.log(3.0) * ramp_steps)


def draw_up_weight(key, part):
    normal_base = jnp.clip(jax.random.normal(jax.random.fold_in(key, 11), (D, FF), jnp.float32), -6.0, 6.0)
    rise_factor = ramp_scale(FF, 0.5)
    return (normal_base * rise_factor[None, :] / math.sqrt(D)).astype(jnp.bfloat16)


def draw_down_weight(key, part):
    normal_base = jnp.clip(jax.random.normal(jax.random.fold_in(key, 23), (FF, D), jnp.float32), -6.0, 6.0)
    rise_factor = ramp_scale(FF, 0.5)
    return (normal_base / rise_factor[:, None] / math.sqrt(FF)).astype(jnp.bfloat16)


def place_ends(result, stream_key, low, high):
    dims = result.shape
    spot = [jax.random.randint(jax.random.fold_in(stream_key, axis), (), 0, dims[axis]) for axis in range(len(dims))]
    result = result.at[tuple(spot)].set(low)
    longest = dims.index(max(dims))
    spot[longest] = (spot[longest] + 1) % dims[longest]
    return result.at[tuple(spot)].set(high)


def block_levels(key, shape, cuts, smallest, high):
    def one(position, parts):
        draws = jax.random.uniform(jax.random.fold_in(jax.random.fold_in(key, 6), position), (parts,), jnp.float32, smallest / len(cuts), high / len(cuts))
        return jnp.repeat(jnp.exp(draws), shape[position] // parts).reshape((-1,) + (1,) * (len(shape) - position - 1))

    gain = one(*cuts[0])
    for cut in cuts[1:]:
        gain = gain * one(*cut)
    return gain


def rank_table(amount, lean):
    loads = [(1 << 20) // math.isqrt(grade ** lean) + 1 for grade in range(1, amount + 1)]
    width = 1 + sum(loads) // (1 << 30)
    return np.cumsum(np.array([max(1, weight // width) for weight in loads]))


def skewed_ids(stream_key, extent, amount, slope):
    table = rank_table(amount, slope)
    ticket = jax.random.randint(jax.random.fold_in(stream_key, 1), extent, 0, int(table[amount - 1]))
    grade = jnp.searchsorted(jnp.asarray(table, jnp.int32), ticket, side="right")
    return jax.random.permutation(jax.random.fold_in(stream_key, 2), amount)[grade].astype(jnp.int32)


def noise(stream_key, extent, deviation, bound, shards=(), kind=jnp.bfloat16):
    entries = jax.random.normal(stream_key, extent, jnp.float32) * deviation
    if len(shards) > 0:
        entries = block_levels(stream_key, extent, shards, -0.22, 0.18) * entries
    return jnp.clip(entries, min=-bound, max=bound).astype(kind)


def setup_inputs(seed: int = 0) -> dict:
    key_list = jax.random.split(jax.random.key(seed), 12)
    return {
        "activations": noise(key_list[0], (ROWS, COLS, D), 1.0, 6.0, ((0, 8), (1, 16))),
        "targets": place_ends(skewed_ids(key_list[1], (ROWS, COLS), VOCAB, 2), jax.random.fold_in(key_list[1], 3), 0, VOCAB - 1).astype(jnp.int32),
        "candidates": place_ends(jax.random.randint(key_list[2], (NCAND,), 0, ROWS * COLS), jax.random.fold_in(key_list[2], 1), 0, (ROWS * COLS) - 1).astype(jnp.int32),
        "mix_gain": jnp.clip(1.0 + 0.18 * jax.random.normal(key_list[3], (D,), jnp.float32), 0.1, 1.9),
        "project_weight": noise(key_list[4], (3, D, HEADS * HD), (D // 2) ** -0.5, 0.1875, ((2, 16),)),
        "output_weight": noise(key_list[5], (HEADS * HD, D), (D // 4) ** -0.5, 0.25, ((0, 16),)),
        "up_weight": draw_up_weight(jax.random.fold_in(key_list[11], 71), 0),
        "down_weight": draw_down_weight(jax.random.fold_in(key_list[11], 71), 0),
        "pattern_bias": jnp.clip(1.0 + 4.0 * jax.random.uniform(key_list[8], (HEADS,), jnp.float32) ** block_levels(key_list[8], (HEADS,), ((0, 16),), -0.2, 0.2), 1.0, 5.0),
        "head_gain": jnp.clip(1.0 + 0.18 * jax.random.normal(key_list[9], (D,), jnp.float32), 0.1, 1.9),
        "head_weight": noise(key_list[10], (D, VOCAB), (D // 9) ** -0.5, 0.375),
    }


EPS = 1e-06

def rms_scale(values):
    return lax.rsqrt(lax.optimization_barrier(jnp.mean(values * values, axis=-1, keepdims=True)) + EPS)

def round_half(values):
    return lax.optimization_barrier(values.astype(jnp.bfloat16)).astype(jnp.float32)

def attend_head(query_one, key_one, value_one, bias_one):
    inv_root = 1.0 / math.sqrt(HD)
    query_f = query_one.astype(jnp.float32)
    key_f = key_one.astype(jnp.float32)
    value_f = value_one.astype(jnp.float32)
    zero_row = jnp.zeros_like(key_f[:1])
    prev_key = jnp.concatenate([zero_row, key_f[:-1]], axis=0)
    prev_value = jnp.concatenate([zero_row, value_f[:-1]], axis=0)
    col_index = jnp.arange(COLS)
    row_index = jnp.arange(ROWS)
    same_allowed = (col_index[None, :] <= col_index[:, None])[None]
    prev_allowed = (col_index[None, :] > col_index[:, None])[None] & (row_index > 0)[:, None, None]
    same_scores = jnp.einsum('rqe,rke->rqk', query_f, key_f, precision=lax.Precision.HIGHEST) * inv_root
    same_weights = jnp.where(same_allowed, jnp.exp(same_scores), 0.0)
    prev_scores = jnp.einsum('rqe,rke->rqk', query_f, prev_key, precision=lax.Precision.HIGHEST) * inv_root
    prev_weights = jnp.where(prev_allowed, jnp.exp(prev_scores), 0.0)
    col_scores = jnp.einsum('rce,sce->rsc', query_f, key_f, precision=lax.Precision.HIGHEST) * inv_root + bias_one
    col_allowed = (row_index[None, :] < row_index[:, None])[:, :, None]
    col_weights = jnp.where(col_allowed, jnp.exp(col_scores), 0.0)
    denom = lax.optimization_barrier(jnp.sum(same_weights, -1)) + lax.optimization_barrier(jnp.sum(prev_weights, -1)) + lax.optimization_barrier(jnp.sum(col_weights, 1))
    accumulated = jnp.einsum('rqk,rke->rqe', round_half(same_weights), value_f, precision=lax.Precision.HIGHEST)
    accumulated = accumulated + jnp.einsum('rqk,rke->rqe', round_half(prev_weights), prev_value, precision=lax.Precision.HIGHEST)
    accumulated = accumulated + jnp.einsum('rsc,sce->rce', round_half(col_weights), value_f, precision=lax.Precision.HIGHEST)
    return (accumulated / denom[..., None]).astype(jnp.bfloat16)

def reference(activations, targets, candidates, mix_gain, project_weight, output_weight, up_weight, down_weight, pattern_bias, head_gain, head_weight):
    input_f = activations.astype(jnp.float32)
    normed = (input_f * rms_scale(input_f) * mix_gain).astype(jnp.bfloat16)
    normed_flat = normed.reshape(ROWS * COLS, D)
    heads_dev = HEADS // N_COL
    hidden_dev = FF // N_COL
    zero_index = jnp.zeros((), jnp.int32)

    def group_step(group_index, totals):
        mixed_sum, spread = totals
        group_index = group_index.astype(jnp.int32)
        partial_sum = jnp.zeros((ROWS * COLS, D), jnp.float32)
        for offset in range(heads_dev):
            head_index = group_index * heads_dev + offset
            head_start = (head_index * HD).astype(jnp.int32)
            head_proj = lax.dynamic_slice(project_weight, (zero_index, zero_index, head_start), (3, D, HD))
            query_one = jnp.dot(normed_flat, head_proj[0], preferred_element_type=jnp.float32).astype(jnp.bfloat16)
            key_one = jnp.dot(normed_flat, head_proj[1], preferred_element_type=jnp.float32).astype(jnp.bfloat16)
            value_one = jnp.dot(normed_flat, head_proj[2], preferred_element_type=jnp.float32).astype(jnp.bfloat16)
            bias_one = lax.dynamic_index_in_dim(pattern_bias, head_index, keepdims=False)
            attended = attend_head(query_one.reshape(ROWS, COLS, HD), key_one.reshape(ROWS, COLS, HD), value_one.reshape(ROWS, COLS, HD), bias_one)
            attended_flat = attended.reshape(ROWS * COLS, HD)
            out_rows = lax.dynamic_slice_in_dim(output_weight, head_start, HD, 0)
            partial_sum = partial_sum + jnp.dot(attended_flat, out_rows, preferred_element_type=jnp.float32)
            spread = spread + lax.optimization_barrier(jnp.sum(jnp.square(attended_flat.astype(jnp.float32)), -1))
        unit_start = (group_index * hidden_dev).astype(jnp.int32)
        up_cols = lax.dynamic_slice_in_dim(up_weight, unit_start, hidden_dev, 1)
        down_rows = lax.dynamic_slice_in_dim(down_weight, unit_start, hidden_dev, 0)
        hidden = jax.nn.gelu(jnp.dot(normed_flat, up_cols, preferred_element_type=jnp.float32), approximate=True).astype(jnp.bfloat16)
        partial_sum = partial_sum + jnp.dot(hidden, down_rows, preferred_element_type=jnp.float32)
        spread = spread + lax.optimization_barrier(jnp.sum(jnp.square(hidden.astype(jnp.float32)), -1))
        mixed_sum = mixed_sum + round_half(partial_sum)
        return (mixed_sum, spread)
    mixed_sum, spread = lax.fori_loop(0, N_COL, group_step, (jnp.zeros((ROWS * COLS, D), jnp.float32), jnp.zeros((ROWS * COLS,), jnp.float32)))
    layer_out = (input_f + mixed_sum.reshape(ROWS, COLS, D)).astype(jnp.bfloat16)
    layer_back = layer_out.reshape(ROWS * COLS, D).astype(jnp.float32)
    inv_norm = rms_scale(layer_back)
    head_in = (layer_back * inv_norm * head_gain).astype(jnp.bfloat16)
    logits = jnp.dot(head_in, head_weight, preferred_element_type=jnp.float32)
    raised = jnp.exp(logits)
    probabilities = raised / lax.optimization_barrier(jnp.sum(raised, axis=-1, keepdims=True))
    onehot = (targets.reshape(ROWS * COLS, 1) == jnp.arange(VOCAB)[None, :]).astype(jnp.float32)
    logit_grad = probabilities - onehot
    head_grad = jnp.dot(logit_grad.astype(jnp.bfloat16), head_weight.T, preferred_element_type=jnp.float32)
    scaled = head_gain * head_grad
    layer_grad = inv_norm * scaled - layer_back * inv_norm ** 3 * lax.optimization_barrier(jnp.mean(layer_back * scaled, axis=-1, keepdims=True))
    out_sq = lax.optimization_barrier(jnp.sum(jnp.square(head_in.astype(jnp.float32)), -1)) * lax.optimization_barrier(jnp.sum(logit_grad * logit_grad, -1))
    norms = jnp.sqrt(out_sq + spread * lax.optimization_barrier(jnp.sum(layer_grad * layer_grad, -1)))
    picked = norms[candidates]
    chosen = NCAND * picked / jnp.sum(picked)
    return (layer_out, chosen)
```

```python
import math

import jax
import jax.numpy as jnp
from jax import lax
from jax.experimental import pallas as pl
from jax.experimental.pallas import tpu as pltpu
from jax.sharding import Mesh
from jax.sharding import PartitionSpec as P

COL = ("col_0", "col_1", "col_2")
ROW = ("row_0", "row_1")
ALL = ("row_0", "row_1", "col_0", "col_1", "col_2")
XL, Z, CORE = COL

EPS = 1e-06
F32 = jnp.float32
BF16 = jnp.bfloat16


def permuted(array, axis, by):
    n = lax.axis_size(axis)
    return lax.ppermute(array, axis, [(i, (i + by) % n) for i in range(n)])


def up_z(array):
    return permuted(array, Z, 1)


def down_z(array):
    return permuted(array, Z, -1)


def swap_x(array):
    return permuted(array, XL, 1)


def swap_core(array):
    return permuted(array, CORE, 1)


def next_row(array):
    n = lax.axis_size(ROW)
    return lax.ppermute(array, ROW, [(i, i + 1) for i in range(n - 1)])


def dot(a, b):
    return jnp.dot(a, b, preferred_element_type=F32)


def dot_t(a, b):
    return lax.dot_general(a, b, (((1,), (1,)), ((), ())), preferred_element_type=F32)


def row_body(inv_root, hs, top_ref, qcol, kcol, cur, prv, pcur, pprv, edge, pedge, acc, den):
    r = pl.program_id(0)
    first = r == 0
    shape = (qcol.shape[0], hs)
    mask = kcol[...] <= qcol[...]
    open_prev = jnp.logical_not(jnp.logical_and(first, top_ref[0] == 1))
    used = jnp.logical_or(mask, jnp.broadcast_to(open_prev, mask.shape))
    for h in range(2):
        g = 1 - h

        def part(ref, at):
            return ref[:, 0, :, at : at + hs].reshape(shape)

        def edge_part(ref, at):
            return ref[:, :, at : at + hs].reshape(shape)

        def pair(base):
            mine, theirs = base + 2 * hs * h, base + 2 * hs * g
            same = jnp.concatenate([part(cur, 2 * hs + mine), part(pcur, 2 * hs + theirs)], axis=0)
            prev = jnp.concatenate(
                [
                    jnp.where(first, edge_part(edge, mine), part(prv, 2 * hs + mine)),
                    jnp.where(first, edge_part(pedge, theirs), part(pprv, 2 * hs + theirs)),
                ],
                axis=0,
            )
            return same, prev

        q = part(cur, h * hs)
        k_same, k_prev = pair(0)
        v_same, v_prev = pair(hs)
        scores = jnp.where(mask, dot_t(q, k_same), dot_t(q, k_prev)) * inv_root
        w = jnp.where(used, jnp.exp(scores), 0.0)
        total = jnp.sum(w, axis=-1, keepdims=True)
        w_same = jnp.where(mask, w, 0.0).astype(BF16)
        w_prev = jnp.where(mask, 0.0, w).astype(BF16)
        out = dot(w_same, v_same) + dot(w_prev, v_prev)
        slots, _, cols, _ = cur.shape
        acc[:, 0, :, h * hs : (h + 1) * hs] = out.reshape(slots, cols, hs)
        den[:, 0, :, h * hs : (h + 1) * hs] = jnp.broadcast_to(total, out.shape).reshape(
            slots, cols, hs
        )


def row_attention(top, qcol, kcol, qkv, pqkv, edge, pedge, hs, inv_root):
    slots, rows, cols, width = qkv.shape
    now = pl.BlockSpec((slots, 1, cols, width), lambda r: (0, r, 0, 0))
    before = pl.BlockSpec((slots, 1, cols, width), lambda r: (0, jnp.maximum(r - 1, 0), 0, 0))
    whole = lambda a: pl.BlockSpec(a.shape, lambda r: (0,) * a.ndim)
    out = jax.ShapeDtypeStruct((slots, rows, cols, 2 * hs), F32)
    out_spec = pl.BlockSpec((slots, 1, cols, 2 * hs), lambda r: (0, r, 0, 0))
    return pl.pallas_call(
        lambda *refs: row_body(inv_root, hs, *refs),
        grid=(rows,),
        in_specs=[
            pl.BlockSpec(memory_space=pltpu.SMEM),
            whole(qcol),
            whole(kcol),
            now,
            before,
            now,
            before,
            whole(edge),
            whole(pedge),
        ],
        out_specs=[out_spec, out_spec],
        out_shape=[out, out],
        name="row_attention",
    )(top, qcol, kcol, qkv, qkv, pqkv, pqkv, edge, pedge)


def col_body(inv_root, hs, own_rows, bias, x, out):
    rows, cols, _ = x.shape
    half = 16
    chunk = 16
    spots = rows * half
    step = chunk * half
    dens = []
    for g in range(cols // half):
        den_rows = jnp.zeros((rows, 128), F32)
        for h in range(2):

            def part(at):
                return x[:, g * half : (g + 1) * half, at : at + hs].reshape(spots, hs)

            q, k, v = part(h * hs), part(2 * hs + 2 * hs * h), part(3 * hs + 2 * hs * h)
            accs, sums = [], []
            for i in range(rows // chunk):
                n = step * (i + 1)
                s = dot_t(q[step * i : step * (i + 1)], k[:n]) * inv_root + bias[h]
                qi = lax.broadcasted_iota(jnp.int32, s.shape, 0) + step * i
                ki = lax.broadcasted_iota(jnp.int32, s.shape, 1)
                keep = jnp.logical_and(((qi - ki) & (half - 1)) == 0, ki < qi)
                w = jnp.where(keep, jnp.exp(s), 0.0)
                accs.append(dot(w.astype(BF16), v[:n]))
                sums.append(jnp.sum(w, axis=-1, keepdims=True))
            a = jnp.concatenate(accs, axis=0).astype(BF16)
            d = jnp.concatenate(sums, axis=0)
            lane = lax.broadcasted_iota(jnp.int32, (spots, 128), 1)
            spot = lax.broadcasted_iota(jnp.int32, (spots, 128), 0)
            hit = lane == (spot & (half - 1)) + half * h
            spread = jnp.where(hit, jnp.broadcast_to(d, (spots, 128)), 0.0)
            den_rows = den_rows + jnp.sum(spread.reshape(rows, half, 128), axis=1)
            a = a.reshape(rows, half, hs)
            for r in range(rows):
                out[r // own_rows, (r % own_rows) * 2 + g, :, h * hs : (h + 1) * hs] = a[r]
        dens.append(den_rows)
    fill = jnp.zeros((8 - own_rows, 128), F32)
    for b in range(rows // own_rows):
        at = slice(own_rows * b, own_rows * (b + 1))
        block = jnp.concatenate([dens[0][at], fill, dens[1][at], fill], axis=0)
        out[b, 2 * own_rows, :, 0:128] = block.astype(BF16)
        out[b, 2 * own_rows, :, 128:256] = jnp.zeros((16, 128), BF16)


def column_attention(bias, x, own_rows, hs, inv_root):
    rows, cols, _ = x.shape
    return pl.pallas_call(
        lambda *refs: col_body(inv_root, hs, own_rows, *refs),
        in_specs=[
            pl.BlockSpec(memory_space=pltpu.SMEM),
            pl.BlockSpec(memory_space=pltpu.VMEM),
        ],
        out_specs=pl.BlockSpec(memory_space=pltpu.VMEM),
        out_shape=jax.ShapeDtypeStruct((rows // own_rows, 2 * own_rows + 1, 16, 2 * hs), BF16),
        name="column_attention",
    )(bias, x)


def merge_body(hs, own_rows, got, acc, den, out):
    half = 16
    lane = lax.broadcasted_iota(jnp.int32, (half, 128), 1)
    spot = lax.broadcasted_iota(jnp.int32, (half, 128), 0)
    table = got[0, 2 * own_rows, :, 0:128].astype(F32)
    for r in range(own_rows):
        for g in range(2):
            line = table[8 * g + r : 8 * g + r + 1]
            for h in range(2):
                at = slice(h * hs, (h + 1) * hs)
                hit = lane == spot + half * h
                col_den = jnp.sum(jnp.where(hit, line, 0.0), axis=-1, keepdims=True)
                cols = slice(half * g, half * (g + 1))
                total = acc[0, r, cols, at] + got[0, 2 * r + g, :, at].astype(F32)
                out[0, r, cols, at] = (total / (den[0, r, cols, at] + col_den)).astype(BF16)


def merge(got, acc, den, hs, own_rows):
    slots, rows, cols, width = acc.shape
    spec = pl.BlockSpec((1, rows, cols, width), lambda s: (s, 0, 0, 0))
    return pl.pallas_call(
        lambda *refs: merge_body(hs, own_rows, *refs),
        grid=(slots,),
        in_specs=[pl.BlockSpec((1,) + got.shape[1:], lambda s: (s, 0, 0, 0)), spec, spec],
        out_specs=spec,
        out_shape=jax.ShapeDtypeStruct(acc.shape, BF16),
        name="merge",
    )(got, acc, den)


def head_body(x, mine, m0, m1, m2, targets, spread, gain, weight, layer_out, line):
    mixed = mine[...] + m0[...].astype(F32) + m1[...].astype(F32) + m2[...].astype(F32)
    lo = (x[...].astype(F32) + mixed).astype(BF16)
    layer_out[...] = lo
    back = lo.astype(F32)
    width = back.shape[1]
    inv_norm = lax.rsqrt(jnp.sum(back * back, axis=-1, keepdims=True) / width + EPS)
    head_in = (back * inv_norm * gain[...]).astype(BF16)
    raised = jnp.exp(dot(head_in, weight[...]))
    prob = raised / jnp.sum(raised, axis=-1, keepdims=True)
    levels = lax.broadcasted_iota(jnp.int32, prob.shape, 1)
    grad = prob - jnp.where(levels == targets[...], 1.0, 0.0)
    scaled = gain[...] * dot_t(grad.astype(BF16), weight[...])
    lean = jnp.sum(back * scaled, axis=-1, keepdims=True) / width
    layer_grad = inv_norm * scaled - back * (inv_norm * inv_norm * inv_norm) * lean
    head_f = head_in.astype(F32)
    out_sq = jnp.sum(head_f * head_f, axis=-1, keepdims=True) * jnp.sum(
        grad * grad, axis=-1, keepdims=True
    )
    layer_sq = jnp.sum(layer_grad * layer_grad, axis=-1, keepdims=True)
    tokens = back.shape[0]
    lane = lax.broadcasted_iota(jnp.int32, (tokens, 256), 1)
    spot = lax.broadcasted_iota(jnp.int32, (tokens, 256), 0)

    def laid(v):
        return jnp.sum(jnp.where(lane == spot, v, 0.0), axis=0, keepdims=True)

    norm = jnp.sqrt(laid(out_sq) + spread[...] * laid(layer_sq))
    line[...] = jnp.broadcast_to(norm, line.shape)


def head(x, mine, m0, m1, m2, targets, spread, gain, weight):
    return pl.pallas_call(
        head_body,
        in_specs=[pl.BlockSpec(memory_space=pltpu.VMEM)] * 9,
        out_specs=[pl.BlockSpec(memory_space=pltpu.VMEM)] * 2,
        out_shape=[
            jax.ShapeDtypeStruct(x.shape, BF16),
            jax.ShapeDtypeStruct((8, 256), F32),
        ],
        name="head",
    )(x, mine, m0, m1, m2, targets, spread, gain, weight)


def pick_body(table, where, spot, out):
    devices = table.shape[0]
    count = where.shape[1]
    hit = lax.broadcasted_iota(jnp.int32, (devices, count), 0) == where[...]
    hot = jnp.where(hit, 1.0, 0.0).astype(BF16)

    def take(part):
        return lax.dot_general(part, hot, (((0,), (0,)), ((), ())), preferred_element_type=F32)

    full = table[...]
    high = full.astype(BF16)
    rest = full - high.astype(F32)
    mid = rest.astype(BF16)
    low = (rest - mid.astype(F32)).astype(BF16)
    lines = take(high) + take(mid) + take(low)
    mine = lax.broadcasted_iota(jnp.int32, lines.shape, 0) == spot[...]
    picked = jnp.sum(jnp.where(mine, lines, 0.0), axis=0, keepdims=True)
    out[...] = count * picked / jnp.sum(picked, axis=-1, keepdims=True)


def pick(table, where, spot):
    return pl.pallas_call(
        pick_body,
        in_specs=[pl.BlockSpec(memory_space=pltpu.VMEM)] * 3,
        out_specs=pl.BlockSpec(memory_space=pltpu.VMEM),
        out_shape=jax.ShapeDtypeStruct(where.shape, F32),
        name="pick",
    )(table, where, spot)


def per_device(
    activations,
    targets,
    candidates,
    mix_gain,
    project_weight,
    output_weight,
    up_weight,
    down_weight,
    pattern_bias,
    head_gain,
    head_weight,
):
    rows, cols, width = activations.shape
    hs = project_weight.shape[2]
    tokens = rows * cols
    row_peers = lax.axis_size(ROW)
    inv_root = 1.0 / math.sqrt(hs)
    third = tokens // 3

    x = activations.reshape(tokens, width)
    x_f = x.astype(F32)
    scale = lax.rsqrt(jnp.mean(x_f * x_f, axis=-1, keepdims=True) + EPS)
    own = (x_f * scale * mix_gain).astype(BF16)

    their_project = swap_core(project_weight)
    their_up = swap_core(up_weight)
    their_down = swap_core(down_weight)
    their_output = swap_core(output_weight)
    bias = jnp.concatenate([pattern_bias, swap_core(pattern_bias)])

    s_a, s_b, s_p = up_z(own), down_z(own), swap_x(own)
    s_aa, s_pb, s_pa = up_z(s_a), down_z(s_p), swap_x(s_a)
    s_far = jnp.concatenate(
        [
            swap_x(s_aa[:third]),
            up_z(s_pa[third : 2 * third]),
            down_z(s_pb[2 * third :]),
        ],
        axis=0,
    )
    shards = (own, s_a, s_b, s_p, s_aa, s_pa, s_pb, s_far)

    attn_weight = jnp.concatenate(
        [
            project_weight[0],
            their_project[0],
            project_weight[1],
            project_weight[2],
            their_project[1],
            their_project[2],
        ],
        axis=1,
    )
    qkv = jnp.stack([dot(s, attn_weight).astype(BF16) for s in shards])
    slots = len(shards)
    split = (slots, rows, cols, 6 * hs)
    qkv4 = qkv.reshape(split)

    above = next_row(qkv4[:, -1, :, 2 * hs :])
    col_in = lax.all_to_all(qkv, ROW, split_axis=0, concat_axis=0, tiled=True)
    their_qkv4 = swap_core(qkv).reshape(split)
    their_above = swap_core(above)

    xl, z, core = lax.axis_index(XL), lax.axis_index(Z), lax.axis_index(CORE)
    n_z = lax.axis_size(Z)
    shift_x = jnp.array([0, 0, 0, 1, 0, 1, 1, 1], jnp.int32)
    shift_z = jnp.array([0, 3, 1, 0, 2, 3, 1, 2], jnp.int32)
    chip = ((xl + shift_x) % 2) * n_z + (z + shift_z) % n_z
    starts = chip * 2 * cols
    offs = jnp.arange(cols, dtype=jnp.int32)
    mine = (starts[:, None] + core * cols + offs[None, :]).reshape(-1)
    theirs = (starts[:, None] + (1 - core) * cols + offs[None, :]).reshape(-1)
    qcol = mine[:, None]
    kcol = jnp.concatenate([mine, theirs])[None, :]
    top = (lax.axis_index(ROW) == 0).astype(jnp.int32)[None]
    acc, den = row_attention(
        top, qcol, kcol, qkv4, their_qkv4, above, their_above, hs, inv_root
    )

    back = column_attention(
        bias, col_in.reshape(row_peers * rows, cols, 6 * hs), rows, hs, inv_root
    )
    got = lax.all_to_all(back, ROW, split_axis=0, concat_axis=0, tiled=True)
    attended = merge(got, acc, den, hs, rows).reshape(slots, tokens, 2 * hs)

    hidden = [
        [
            jax.nn.gelu(dot(s, w), approximate=True).astype(BF16)
            for w in (up_weight, their_up)
        ]
        for s in shards
    ]

    def term(i):
        a = attended[i]
        return (
            dot(a[:, :hs], output_weight)
            + dot(a[:, hs:], their_output)
            + dot(hidden[i][0], down_weight)
            + dot(hidden[i][1], their_down)
        )

    def sent(v):
        return v.astype(BF16)

    def plus(v, *more):
        for m in more:
            v = v + m.astype(F32)
        return v

    far = sent(term(7))
    g0, g1, g2 = swap_x(far[:third]), down_z(far[third : 2 * third]), up_z(far[2 * third :])
    none = jnp.zeros((third, width), BF16)
    from_b = up_z(sent(term(2)))
    t_aa = sent(plus(term(4), jnp.concatenate([g0, none, none], axis=0)))
    t_pa = sent(plus(term(5), jnp.concatenate([none, g1, none], axis=0)))
    t_pb = sent(plus(term(6), jnp.concatenate([none, none, g2], axis=0)))
    r_aa, r_pa, r_pb = down_z(t_aa), swap_x(t_pa), up_z(t_pb)
    t_a = sent(plus(term(1), r_aa, r_pa))
    t_p = sent(plus(term(3), r_pb))
    from_a, from_p = down_z(t_a), swap_x(t_p)
    mine_sum = term(0)

    spread_part = jnp.stack(
        [
            jnp.sum(jnp.square(attended[i].astype(F32)), -1)
            + jnp.sum(jnp.square(hidden[i][0].astype(F32)), -1)
            + jnp.sum(jnp.square(hidden[i][1].astype(F32)), -1)
            for i in range(slots)
        ]
    )
    place = jnp.array([[0, 2, 4, 1], [3, 6, 7, 5]], jnp.int32).reshape(-1)
    k = jnp.arange(slots, dtype=jnp.int32)
    dx = (k // n_z - xl) % 2
    dz = (k % n_z - z) % n_z
    spread_abs = spread_part[place[dx * n_z + dz]]
    spread = jnp.sum(
        lax.all_to_all(spread_abs, (XL, Z), split_axis=0, concat_axis=0, tiled=True), axis=0
    )
    spread = jnp.pad(spread, (0, 256 - tokens))[None, :]

    layer_out, line = head(
        x,
        mine_sum,
        from_a,
        from_b,
        from_p,
        targets.reshape(tokens, 1),
        spread,
        head_gain[None, :],
        head_weight,
    )
    devices = lax.axis_size(ALL)
    table = lax.all_to_all(
        jnp.broadcast_to(line[None, :1], (devices, 1, 256)),
        ALL,
        split_axis=0,
        concat_axis=0,
        tiled=True,
    ).reshape(devices, 256)
    full_cols = cols * lax.axis_size(COL)
    c_row, c_col = candidates // full_cols, candidates % full_cols
    where = (c_row // rows) * lax.axis_size(COL) + c_col // cols
    spot = (c_row % rows) * cols + c_col % cols
    chosen = pick(table, where[None, :], spot[None, :])
    return (layer_out.reshape(rows, cols, width), chosen.reshape(-1))


def solution(mesh):
    split = Mesh(mesh.devices.reshape(2, 4, 2, 4, 2), ("row_0", "row_1", "col_0", "col_1", "col_2"))
    return jax.shard_map(
        per_device,
        mesh=split,
        in_specs=(
            P(ROW, COL, None),
            P(ROW, COL),
            P(),
            P(),
            P(None, None, COL),
            P(COL, None),
            P(None, COL),
            P(COL, None),
            P(COL),
            P(),
            P(),
        ),
        out_specs=(P(ROW, COL, None), P()),
        check_vma=False,
    )
```

```python
import math

import jax
import jax.numpy as jnp
from jax import lax
from jax.experimental import pallas as pl
from jax.experimental.pallas import tpu as pltpu
from jax.sharding import Mesh
from jax.sharding import PartitionSpec as P

COL = ("col_0", "col_1", "col_2")
ROW = ("row_0", "row_1")
ALL = ("row_0", "row_1", "col_0", "col_1", "col_2")
XL, Z, CORE = COL

EPS = 1e-06
F32 = jnp.float32
BF16 = jnp.bfloat16


def permuted(array, axis, by):
    n = lax.axis_size(axis)
    return lax.ppermute(array, axis, [(i, (i + by) % n) for i in range(n)])


def up_z(array):
    return permuted(array, Z, 1)


def down_z(array):
    return permuted(array, Z, -1)


def swap_x(array):
    return permuted(array, XL, 1)


def swap_core(array):
    return permuted(array, CORE, 1)


def next_row(array):
    n = lax.axis_size(ROW)
    return lax.ppermute(array, ROW, [(i, i + 1) for i in range(n - 1)])


def dot(a, b):
    return jnp.dot(a, b, preferred_element_type=F32)


def dot_t(a, b):
    return lax.dot_general(a, b, (((1,), (1,)), ((), ())), preferred_element_type=F32)


def cost(flops, bytes_accessed, exps=0):
    return pl.CostEstimate(flops=flops, bytes_accessed=bytes_accessed, transcendentals=exps)


VMEM = pl.BlockSpec(memory_space=pltpu.VMEM)
SMEM = pl.BlockSpec(memory_space=pltpu.SMEM)
HALF = 16


def laid(column, lanes=256):
    shape = (column.shape[0], lanes)
    hit = lax.broadcasted_iota(jnp.int32, shape, 1) == lax.broadcasted_iota(jnp.int32, shape, 0)
    return jnp.sum(jnp.where(hit, column, 0.0), axis=0, keepdims=True)


def norm_body(x, gain, out):
    v = x[...].astype(F32)
    scale = lax.rsqrt(jnp.sum(v * v, axis=-1, keepdims=True) / v.shape[1] + EPS)
    out[...] = (v * scale * gain[...]).astype(BF16)


def normalize(x, gain):
    return pl.pallas_call(
        norm_body,
        in_specs=[VMEM, VMEM],
        out_specs=VMEM,
        out_shape=jax.ShapeDtypeStruct(x.shape, BF16),
        cost_estimate=cost(5 * x.size, 4 * x.size),
        name="normalize",
    )(x, gain)


def stacked(refs):
    return jnp.concatenate([ref[...] for ref in refs], axis=0)


def project_body(rows, n, *refs):
    mine, theirs, out = refs[n:]
    x = stacked(refs[:n])
    w = jnp.concatenate([mine[0], theirs[0]], axis=1)
    y = dot(x, w).astype(BF16).reshape(4, rows, 2, HALF, w.shape[1])
    for g in range(2):
        out[:, g] = y[:, :, g]


def project(shards, mine, theirs, rows):
    n = len(shards)
    total = sum(v.shape[0] for v in shards)
    _, width, hs = mine.shape
    whole = [pl.BlockSpec(v.shape, lambda j: (0, 0)) for v in shards]
    weight = pl.BlockSpec((1, width, hs), lambda j: (j, 0, 0))
    return pl.pallas_call(
        lambda *refs: project_body(rows, n, *refs),
        grid=(3,),
        in_specs=whole + [weight] * 2,
        out_specs=pl.BlockSpec((4, 2, rows, HALF, 2 * hs), lambda j: (0, 0, 0, 0, j)),
        out_shape=jax.ShapeDtypeStruct((4, 2, rows, HALF, 6 * hs), BF16),
        cost_estimate=cost(2 * total * width * 6 * hs, 2 * total * width + 12 * width * hs),
        name="project",
    )(*shards, mine, theirs)


def forward_body(n, *refs):
    up, their_up, down, their_down = refs[n : n + 4]
    outs, (acc, sums) = refs[n + 4 : -2], refs[-2:]
    step = pl.program_id(0)
    x = stacked(refs[:n])
    h = dot(x, jnp.concatenate([up[...], their_up[...]], axis=1))
    h = jax.nn.gelu(h, approximate=True).astype(BF16)
    h_f = h.astype(F32)
    part = jnp.sum(h_f * h_f, axis=-1, keepdims=True)
    term = dot(h, jnp.concatenate([down[...], their_down[...]], axis=0))

    @pl.when(step == 0)
    def _():
        acc[...] = term
        sums[...] = jnp.broadcast_to(part, sums.shape)

    @pl.when(step == 1)
    def _():
        width = acc.shape[1]
        total = (acc[...] + term).astype(BF16)
        squares = (sums[...] + part).astype(BF16)
        tokens = outs[0].shape[0]
        for i, out in enumerate(outs):
            at = slice(tokens * i, tokens * (i + 1))
            out[:, 0:width] = total[at]
            out[:, width : width + 128] = squares[at]


def feed_forward(shards, slots, up, their_up, down, their_down):
    n = len(shards)
    total = sum(v.shape[0] for v in shards)
    tokens, width = total // slots, shards[0].shape[1]
    units = up.shape[1] // 2
    whole = [pl.BlockSpec(v.shape, lambda j: (0, 0)) for v in shards]
    rise = pl.BlockSpec((width, units), lambda j: (0, j))
    fall = pl.BlockSpec((units, width), lambda j: (j, 0))
    return pl.pallas_call(
        lambda *refs: forward_body(n, *refs),
        grid=(2,),
        in_specs=whole + [rise, rise, fall, fall],
        out_specs=[pl.BlockSpec((tokens, width + 128), lambda j: (0, 0))] * slots,
        out_shape=[jax.ShapeDtypeStruct((tokens, width + 128), BF16)] * slots,
        scratch_shapes=[pltpu.VMEM((total, width), F32), pltpu.VMEM((total, 128), F32)],
        cost_estimate=cost(16 * total * width * units, 4 * total * width + 16 * width * units),
        name="feed_forward",
    )(*shards, up, their_up, down, their_down)


def row_body(inv_root, hs, top_ref, qcol, kcol, *refs):
    (cur0, cur1, prv0, prv1, pcur0, pcur1, pprv0, pprv1) = refs[:8]
    (edge0, edge1, pedge0, pedge1) = refs[8:12]
    accs, dens = refs[12:14], refs[14:16]
    r = pl.program_id(0)
    first = r == 0
    n = qcol.shape[0] // 2
    mask = kcol[...] <= qcol[...]
    open_prev = jnp.logical_not(jnp.logical_and(first, top_ref[0] == 1))
    used = jnp.logical_or(mask, jnp.broadcast_to(open_prev, mask.shape))

    def part(ref, at):
        return ref[:, :, 0, :, at : at + hs].reshape(n, hs)

    def edge_part(ref, at):
        return ref[:, :, :, at : at + hs].reshape(n, hs)

    def either(prv, edge, at):
        return jnp.where(first, edge_part(edge, at), part(prv, 2 * hs + at))

    for h in range(2):
        q = jnp.concatenate([part(cur0, h * hs), part(cur1, h * hs)], axis=0)

        def pair(base):
            a, b = base + hs * h, base + hs * (1 - h)
            same = [part(cur0, 2 * hs + a), part(cur1, 2 * hs + a)]
            same += [part(pcur0, 2 * hs + b), part(pcur1, 2 * hs + b)]
            prev = [either(prv0, edge0, a), either(prv1, edge1, a)]
            prev += [either(pprv0, pedge0, b), either(pprv1, pedge1, b)]
            return jnp.concatenate(same, axis=0), jnp.concatenate(prev, axis=0)

        k_same, k_prev = pair(0)
        v_same, v_prev = pair(2 * hs)
        scores = jnp.where(mask, dot_t(q, k_same), dot_t(q, k_prev)) * inv_root
        w = jnp.where(used, jnp.exp(scores), 0.0)
        total = jnp.sum(w, axis=-1, keepdims=True)
        w_same = jnp.where(mask, w, 0.0).astype(BF16)
        w_prev = jnp.where(mask, 0.0, w).astype(BF16)
        out = dot(w_same, v_same) + dot(w_prev, v_prev)
        total = jnp.broadcast_to(total, out.shape)
        for i in range(2):
            at = slice(h * hs, (h + 1) * hs)
            shape = (4, 2, HALF, hs)
            accs[i][:, :, 0, :, at] = out[n * i : n * (i + 1)].reshape(shape)
            dens[i][:, :, 0, :, at] = total[n * i : n * (i + 1)].reshape(shape)


def row_attention(top, qcol, kcol, qkv, their_qkv, edge, their_edge, hs, inv_root):
    rows = qkv[0].shape[2]
    width = 6 * hs
    now = pl.BlockSpec((4, 2, 1, HALF, width), lambda r: (0, 0, r, 0, 0))
    before = pl.BlockSpec(
        (4, 2, 1, HALF, width), lambda r: (0, 0, jnp.maximum(r - 1, 0), 0, 0)
    )
    whole = lambda a: pl.BlockSpec(a.shape, lambda r: (0,) * a.ndim)
    out = jax.ShapeDtypeStruct((4, 2, rows, HALF, 2 * hs), F32)
    out_spec = pl.BlockSpec((4, 2, 1, HALF, 2 * hs), lambda r: (0, 0, r, 0, 0))
    n = qcol.shape[0]
    outs = pl.pallas_call(
        lambda *refs: row_body(inv_root, hs, *refs),
        grid=(rows,),
        in_specs=[SMEM, whole(qcol), whole(kcol)]
        + [now, now, before, before] * 2
        + [whole(e) for e in (*edge, *their_edge)],
        out_specs=[out_spec] * 4,
        out_shape=[out] * 4,
        cost_estimate=cost(rows * 32 * n * n * hs, rows * 32 * n * hs, rows * 4 * n * n),
        name="row_attention",
    )(top, qcol, kcol, *qkv, *qkv, *their_qkv, *their_qkv, *edge, *their_edge)
    return outs[:2], outs[2:]


def col_body(inv_root, hs, own_rows, bias, x, *refs):
    out = refs[-1]
    rows, cols, _ = x.shape
    chunk = 16
    spots = rows * cols
    step = chunk * cols
    den_rows = jnp.zeros((rows, 128), F32)
    lane = lax.broadcasted_iota(jnp.int32, (spots, 128), 1)
    spot = lax.broadcasted_iota(jnp.int32, (spots, 128), 0)
    for h in range(2):

        def part(at):
            return x[:, :, at * hs : (at + 1) * hs].reshape(spots, hs)

        q, k, v = part(h), part(2 + h), part(4 + h)
        accs, sums = [], []
        for i in range(rows // chunk):
            n = step * (i + 1)
            s = dot_t(q[step * i : step * (i + 1)], k[:n]) * inv_root + bias[h]
            qi = lax.broadcasted_iota(jnp.int32, s.shape, 0) + step * i
            ki = lax.broadcasted_iota(jnp.int32, s.shape, 1)
            keep = jnp.logical_and(((qi - ki) & (cols - 1)) == 0, ki < qi)
            w = jnp.where(keep, jnp.exp(s), 0.0)
            accs.append(dot(w.astype(BF16), v[:n]))
            sums.append(jnp.sum(w, axis=-1, keepdims=True))
        a = jnp.concatenate(accs, axis=0).astype(BF16).reshape(rows, cols, hs)
        d = jnp.concatenate(sums, axis=0)
        spread = jnp.where(lane == (spot & (cols - 1)) + cols * h, d, 0.0)
        den_rows = den_rows + jnp.sum(spread.reshape(rows, cols, 128), axis=1)
        for r in range(rows):
            out[r // own_rows, 0, r % own_rows, :, h * hs : (h + 1) * hs] = a[r]
    fill = jnp.zeros((cols - own_rows, 128), F32)
    for b in range(rows // own_rows):
        block = jnp.concatenate([den_rows[own_rows * b : own_rows * (b + 1)], fill], axis=0)
        out[b, 0, own_rows, :, 0:128] = block.astype(BF16)
        out[b, 0, own_rows, :, 128:256] = jnp.zeros((cols, 128), BF16)


def column_attention(group, bias, x, own_rows, hs, inv_root, earlier=()):
    rows, cols, _ = x.shape
    spots = rows * cols
    peers = rows // own_rows
    return pl.pallas_call(
        lambda *refs: col_body(inv_root, hs, own_rows, *refs),
        grid=(1,),
        in_specs=[SMEM, pl.BlockSpec(x.shape, lambda i: (0, 0, 0))]
        + [pl.BlockSpec(memory_space=pl.ANY)] * len(earlier),
        out_specs=pl.BlockSpec(
            (peers, 1, own_rows + 1, cols, 2 * hs), lambda i: (0, group, 0, 0, 0)
        ),
        out_shape=jax.ShapeDtypeStruct((peers, 2, own_rows + 1, cols, 2 * hs), BF16),
        input_output_aliases={2: 0} if earlier else {},
        cost_estimate=cost(6 * spots * spots * hs, 16 * spots * hs, 2 * spots * spots),
        name="column_attention",
    )(bias, x, *earlier)


def term_body(hs, rows, group, splits, got, acc, den, f0, f1, f2, f3, w_mine, w_their, *outs):
    spots = 8 * rows * HALF
    unit = lax.broadcasted_iota(jnp.int32, (spots, 128), 0) // HALF
    line = lax.broadcasted_iota(jnp.int32, (spots, 128), 1)
    hit = jnp.logical_and(unit == (line // HALF) * rows + line % HALF, line % HALF < rows)
    table = got[:, group, rows, :, 0:128].reshape(128, 128)
    table = dot(jnp.where(hit, 1.0, 0.0).astype(BF16), table)
    spot = lax.broadcasted_iota(jnp.int32, (spots, 128), 0) % HALF
    ones = jnp.ones((128, 128), BF16)
    parts = []
    for h in range(2):
        at = slice(h * hs, (h + 1) * hs)
        col_den = dot(jnp.where(line == spot + HALF * h, table, 0.0).astype(BF16), ones)
        total = acc[:, :, :, :, at].reshape(spots, hs)
        total = total + got[:, group, 0:rows, :, at].reshape(spots, hs).astype(F32)
        parts.append((total / (den[:, :, :, :, at].reshape(spots, hs) + col_den)).astype(BF16))
    halves = jnp.concatenate(parts, axis=1).reshape(4, 2, rows, HALF, 2 * hs)
    blocks = [halves[s, g, r] for s in range(4) for r in range(rows) for g in range(2)]
    attended = jnp.concatenate(blocks, axis=0)
    att_f = attended.astype(F32)
    squares = jnp.sum(att_f * att_f, axis=-1, keepdims=True)
    weight = jnp.concatenate([w_mine[...], w_their[...]], axis=0)
    term = dot(attended, weight)
    width = term.shape[1]
    for out, (slot, low, high) in zip(outs, splits):
        f = (f0, f1, f2, f3)[slot]
        tokens = f.shape[0]
        at = slice(tokens * slot + low, tokens * slot + high)
        out[:, 0:width] = (f[low:high, 0:width].astype(F32) + term[at]).astype(BF16)
        out[:, width:] = (f[low:high, width:].astype(F32) + squares[at]).astype(BF16)


def terms(group, got, acc, den, ff, w_mine, w_their, hs, rows, splits):
    tokens, full = ff[0].shape
    return pl.pallas_call(
        lambda *refs: term_body(hs, rows, group, splits, *refs),
        in_specs=[VMEM] * 9,
        out_specs=[VMEM] * len(splits),
        out_shape=[jax.ShapeDtypeStruct((b - a, full), BF16) for _, a, b in splits],
        cost_estimate=cost(16 * tokens * hs * full, 20 * tokens * full),
        name="terms",
    )(got, acc, den, *ff, w_mine, w_their)


def thirds_body(t0, t1, t2, o0, o1, o2):
    o0[...] = t0[...]
    o1[...] = t1[...]
    o2[...] = t2[...]


def thirds_of(arrays):
    rows, width = arrays[0].shape
    third = rows // 3
    block = lambda at: pl.BlockSpec((third, width), lambda i: (at, 0))
    return pl.pallas_call(
        thirds_body,
        grid=(1,),
        in_specs=[block(0), block(1), block(2)],
        out_specs=[block(0)] * 3,
        out_shape=[jax.ShapeDtypeStruct((third, width), BF16)] * 3,
        cost_estimate=cost(0, 4 * rows * width),
        name="thirds",
    )(*arrays)


def far_body(t0, t1, t2, g0, g1, g2, o0, o1, o2):
    for t, g, o in ((t0, g0, o0), (t1, g1, o1), (t2, g2, o2)):
        o[...] = (t[...].astype(F32) + g[...].astype(F32)).astype(BF16)


def add_far(arrays, parts):
    third, width = parts[0].shape
    block = lambda at: pl.BlockSpec((third, width), lambda i: (at, 0))
    spread = [block(0), block(1), block(2)]
    return pl.pallas_call(
        far_body,
        grid=(1,),
        in_specs=spread + [block(0)] * 3,
        out_specs=spread,
        out_shape=[jax.ShapeDtypeStruct(arrays[0].shape, BF16)] * 3,
        input_output_aliases={0: 0, 1: 1, 2: 2},
        cost_estimate=cost(6 * third * width, 18 * third * width),
        name="add_far",
    )(*arrays, *parts)


def near_body(t0, t1, r0, r1, r2, o0, o1):
    o0[...] = (t0[...].astype(F32) + r0[...].astype(F32) + r1[...].astype(F32)).astype(BF16)
    o1[...] = (t1[...].astype(F32) + r2[...].astype(F32)).astype(BF16)


def add_near(*arrays):
    rows, width = arrays[0].shape
    block = pl.BlockSpec((rows // 3, width), lambda i: (i, 0))
    return pl.pallas_call(
        near_body,
        grid=(3,),
        in_specs=[block] * 5,
        out_specs=[block] * 2,
        out_shape=[jax.ShapeDtypeStruct((rows, width), BF16)] * 2,
        cost_estimate=cost(3 * rows * width, 14 * rows * width),
        name="add_near",
    )(*arrays)


def head_body(x, mine, m0, m1, m2, targets, gain, weight, layer_out, line):
    width = x.shape[1]
    mixed, spread = 0.0, 0.0
    for m in (mine, m0, m1, m2):
        mixed = mixed + m[:, :width].astype(F32)
        spread = spread + m[:, width : width + 1].astype(F32)
    lo = (x[...].astype(F32) + mixed).astype(BF16)
    layer_out[...] = lo
    back = lo.astype(F32)
    inv_norm = lax.rsqrt(jnp.sum(back * back, axis=-1, keepdims=True) / width + EPS)
    head_in = (back * inv_norm * gain[...]).astype(BF16)
    raised = jnp.exp(dot(head_in, weight[...]))
    prob = raised / jnp.sum(raised, axis=-1, keepdims=True)
    levels = lax.broadcasted_iota(jnp.int32, prob.shape, 1)
    grad = prob - jnp.where(levels == targets[...], 1.0, 0.0)
    scaled = gain[...] * dot_t(grad.astype(BF16), weight[...])
    lean = jnp.sum(back * scaled, axis=-1, keepdims=True) / width
    layer_grad = inv_norm * scaled - back * (inv_norm * inv_norm * inv_norm) * lean
    head_f = head_in.astype(F32)
    out_sq = jnp.sum(head_f * head_f, axis=-1, keepdims=True) * jnp.sum(
        grad * grad, axis=-1, keepdims=True
    )
    layer_sq = jnp.sum(layer_grad * layer_grad, axis=-1, keepdims=True)
    norm = jnp.sqrt(laid(out_sq + spread * layer_sq))
    line[...] = jnp.broadcast_to(norm[None], line.shape)


def head(x, mine, m0, m1, m2, targets, gain, weight, devices):
    return pl.pallas_call(
        head_body,
        in_specs=[VMEM] * 8,
        out_specs=[pl.BlockSpec(memory_space=pltpu.VMEM)] * 2,
        out_shape=[
            jax.ShapeDtypeStruct(x.shape, BF16),
            jax.ShapeDtypeStruct((devices, 1, 256), F32),
        ],
        name="head",
    )(x, mine, m0, m1, m2, targets, gain, weight)


def pick_body(table, where, spot, out):
    devices = table.shape[0]
    count = where.shape[1]
    hit = lax.broadcasted_iota(jnp.int32, (devices, count), 0) == where[...]
    hot = jnp.where(hit, 1.0, 0.0).astype(BF16)

    def take(part):
        return lax.dot_general(part, hot, (((0,), (0,)), ((), ())), preferred_element_type=F32)

    full = table[...]
    high = full.astype(BF16)
    rest = full - high.astype(F32)
    mid = rest.astype(BF16)
    low = (rest - mid.astype(F32)).astype(BF16)
    lines = take(high) + take(mid) + take(low)
    mine = lax.broadcasted_iota(jnp.int32, lines.shape, 0) == spot[...]
    picked = jnp.sum(jnp.where(mine, lines, 0.0), axis=0, keepdims=True)
    out[...] = count * picked / jnp.sum(picked, axis=-1, keepdims=True)


def pick(table, where, spot):
    return pl.pallas_call(
        pick_body,
        in_specs=[pl.BlockSpec(memory_space=pltpu.VMEM)] * 3,
        out_specs=pl.BlockSpec(memory_space=pltpu.VMEM),
        out_shape=jax.ShapeDtypeStruct(where.shape, F32),
        name="pick",
    )(table, where, spot)


def per_device(
    activations,
    targets,
    candidates,
    mix_gain,
    project_weight,
    output_weight,
    up_weight,
    down_weight,
    pattern_bias,
    head_gain,
    head_weight,
):
    rows, cols, width = activations.shape
    hs = project_weight.shape[2]
    tokens = rows * cols
    row_peers = lax.axis_size(ROW)
    inv_root = 1.0 / math.sqrt(hs)
    third = tokens // 3

    devices = lax.axis_size(ALL)

    their_project = swap_core(project_weight)
    their_up = swap_core(up_weight)
    their_down = swap_core(down_weight)
    their_output = swap_core(output_weight)
    bias = jnp.concatenate([pattern_bias, swap_core(pattern_bias)])

    x = activations.reshape(tokens, width)
    own = normalize(x, mix_gain[None, :])

    def after(first, values):
        return lax.optimization_barrier((first, values))[1]

    def ffn(shards, slots):
        return feed_forward(shards, slots, up_weight, their_up, down_weight, their_down)

    near = (up_z(own), down_z(own), swap_x(own))
    (ff_own,) = ffn((own,), 1)
    s_a, s_b, s_p = after((ff_own, their_project), near)
    s_aa, s_pb, s_pa = up_z(s_a), down_z(s_p), swap_x(s_a)

    def columns(shards):
        qkv = project(shards, project_weight, their_project, rows)
        got = lax.all_to_all(
            qkv.reshape(row_peers, rows * HALF, 6 * hs), ROW, split_axis=0, concat_axis=0, tiled=True
        )
        return qkv, got

    def attend_columns(group, got, *earlier):
        x = got.reshape(row_peers * rows, HALF, 6 * hs)
        return column_attention(group, bias, x, rows, hs, inv_root, earlier)

    def edge_of(qkv):
        return next_row(qkv[:, :, -1, :, 2 * hs :])

    qkv0, got0 = columns((own, s_a, s_b, s_p))
    their_qkv0 = swap_core(qkv0)
    edge0 = edge_of(qkv0)
    their_edge0 = swap_core(edge0)
    s_aa, s_pa, s_pb = after(qkv0, (s_aa, s_pa, s_pb))
    h_aa, h_pa, h_pb = thirds_of((s_aa, s_pa, s_pb))
    far = (swap_x(h_aa), up_z(h_pa), down_z(h_pb))
    back = attend_columns(0, after((s_aa, s_pa, s_pb), got0))
    away = after((back, their_qkv0), (s_aa, s_pa, s_pb, *far))
    qkv1, got1 = columns(away)
    their_qkv1 = swap_core(qkv1)
    edge1 = edge_of(qkv1)
    their_edge1 = swap_core(edge1)
    ff1 = ffn(after(qkv1, away), 4)
    back = attend_columns(1, after((ff1, their_qkv1), got1), back)
    again = lax.all_to_all(back, ROW, split_axis=0, concat_axis=0, tiled=True)

    xl, z, core = lax.axis_index(XL), lax.axis_index(Z), lax.axis_index(CORE)
    n_z = lax.axis_size(Z)
    shift_x = jnp.array([0, 0, 0, 1, 0, 1, 1, 1], jnp.int32)
    shift_z = jnp.array([0, 3, 1, 0, 2, 3, 1, 2], jnp.int32)
    chip = ((xl + shift_x) % 2) * n_z + (z + shift_z) % n_z
    starts = chip * 2 * cols
    offs = jnp.arange(cols, dtype=jnp.int32)
    mine = (starts[:, None] + core * cols + offs[None, :]).reshape(-1)
    theirs = (starts[:, None] + (1 - core) * cols + offs[None, :]).reshape(-1)
    top = (lax.axis_index(ROW) == 0).astype(jnp.int32)[None]
    acc, den = row_attention(
        after(back, top),
        mine[:, None],
        jnp.concatenate([mine, theirs])[None, :],
        (qkv0, qkv1),
        (their_qkv0, their_qkv1),
        (edge0, edge1),
        (their_edge0, their_edge1),
        hs,
        inv_root,
    )
    thirds = [(3, third * i, third * (i + 1)) for i in range(3)]
    t_aa, t_pa, t_pb, f0, f1, f2 = terms(
        1, again, acc[1], den[1], ff1, output_weight, their_output, hs, rows,
        [(i, 0, tokens) for i in range(3)] + thirds,
    )

    t_aa, t_pa, t_pb = add_far((t_aa, t_pa, t_pb), (swap_x(f0), down_z(f1), up_z(f2)))
    r_aa, r_pa, r_pb = down_z(t_aa), swap_x(t_pa), up_z(t_pb)
    ff0 = ffn(after(t_pb, (s_a, s_b, s_p)), 3)
    t_own, t_a, t_b, t_p = terms(
        0, again, acc[0], den[0], (ff_own, *ff0), output_weight, their_output, hs, rows,
        [(i, 0, tokens) for i in range(4)],
    )
    from_b = up_z(t_b)
    t_a, t_p = add_near(t_a, t_p, r_aa, r_pa, r_pb)
    from_a, from_p = down_z(t_a), swap_x(t_p)

    layer_out, line = head(
        x,
        t_own,
        from_a,
        from_b,
        from_p,
        targets.reshape(tokens, 1),
        head_gain[None, :],
        head_weight,
        devices,
    )
    table = lax.all_to_all(
        line,
        ALL,
        split_axis=0,
        concat_axis=0,
        tiled=True,
    ).reshape(devices, 256)
    full_cols = cols * lax.axis_size(COL)
    c_row, c_col = candidates // full_cols, candidates % full_cols
    where = (c_row // rows) * lax.axis_size(COL) + c_col // cols
    spot = (c_row % rows) * cols + c_col % cols
    chosen = pick(table, where[None, :], spot[None, :])
    return (layer_out.reshape(rows, cols, width), chosen.reshape(-1))


def solution(mesh):
    split = Mesh(mesh.devices.reshape(2, 4, 2, 4, 2), ("row_0", "row_1", "col_0", "col_1", "col_2"))

    return jax.shard_map(
        per_device,
        mesh=split,
        in_specs=(
            P(ROW, COL, None),
            P(ROW, COL),
            P(),
            P(),
            P(None, None, COL),
            P(COL, None),
            P(None, COL),
            P(COL, None),
            P(COL),
            P(),
            P(),
        ),
        out_specs=(P(ROW, COL, None), P()),
        check_vma=False,
    )
```

```python
import math

import jax
import jax.numpy as jnp
from jax import lax
from jax.experimental import pallas as pl
from jax.experimental.pallas import tpu as pltpu
from jax.sharding import Mesh
from jax.sharding import PartitionSpec as P

COL = ("col_0", "col_1", "col_2")
ROW = ("row_0", "row_1")
ALL = ("row_0", "row_1", "col_0", "col_1", "col_2")
XL, Z, CORE = COL

EPS = 1e-06
F32 = jnp.float32
BF16 = jnp.bfloat16


def permuted(array, axis, by):
    n = lax.axis_size(axis)
    return lax.ppermute(array, axis, [(i, (i + by) % n) for i in range(n)])


def up_z(array):
    return permuted(array, Z, 1)


def down_z(array):
    return permuted(array, Z, -1)


def swap_x(array):
    return permuted(array, XL, 1)


def swap_core(array):
    return permuted(array, CORE, 1)


def next_row(array):
    n = lax.axis_size(ROW)
    return lax.ppermute(array, ROW, [(i, i + 1) for i in range(n - 1)])


def dot(a, b):
    return jnp.dot(a, b, preferred_element_type=F32)


def dot_t(a, b):
    return lax.dot_general(a, b, (((1,), (1,)), ((), ())), preferred_element_type=F32)


def cost(flops, bytes_accessed, exps=0):
    return pl.CostEstimate(flops=flops, bytes_accessed=bytes_accessed, transcendentals=exps)


VMEM = pl.BlockSpec(memory_space=pltpu.VMEM)
SMEM = pl.BlockSpec(memory_space=pltpu.SMEM)
HALF = 16


def laid(column, lanes=256):
    shape = (column.shape[0], lanes)
    hit = lax.broadcasted_iota(jnp.int32, shape, 1) == lax.broadcasted_iota(jnp.int32, shape, 0)
    return jnp.sum(jnp.where(hit, column, 0.0), axis=0, keepdims=True)


def norm_body(x, gain, out):
    v = x[...].astype(F32)
    scale = lax.rsqrt(jnp.sum(v * v, axis=-1, keepdims=True) / v.shape[1] + EPS)
    out[...] = (v * scale * gain[...]).astype(BF16)


def normalize(x, gain):
    return pl.pallas_call(
        norm_body,
        in_specs=[VMEM, VMEM],
        out_specs=VMEM,
        out_shape=jax.ShapeDtypeStruct(x.shape, BF16),
        cost_estimate=cost(5 * x.size, 4 * x.size),
        name="normalize",
    )(x, gain)


def stacked(refs):
    return jnp.concatenate([ref[...] for ref in refs], axis=0)


def project_body(rows, n, *refs):
    mine, theirs, out, edge = refs[n:]
    x = stacked(refs[:n])
    w = jnp.concatenate([mine[0], theirs[0]], axis=1)
    y = dot(x, w).astype(BF16).reshape(4, rows, 2, HALF, w.shape[1])
    for g in range(2):
        out[:, g] = y[:, :, g]
        edge[:, g] = y[:, rows - 1, g]


def project(shards, mine, theirs, rows):
    n = len(shards)
    total = sum(v.shape[0] for v in shards)
    _, width, hs = mine.shape
    whole = [pl.BlockSpec(v.shape, lambda j: (0, 0)) for v in shards]
    weight = pl.BlockSpec((1, width, hs), lambda j: (j, 0, 0))
    return pl.pallas_call(
        lambda *refs: project_body(rows, n, *refs),
        grid=(3,),
        in_specs=whole + [weight] * 2,
        out_specs=[
            pl.BlockSpec((4, 2, rows, HALF, 2 * hs), lambda j: (0, 0, 0, 0, j)),
            pl.BlockSpec((4, 2, HALF, 2 * hs), lambda j: (0, 0, 0, jnp.maximum(j - 1, 0))),
        ],
        out_shape=[
            jax.ShapeDtypeStruct((4, 2, rows, HALF, 6 * hs), BF16),
            jax.ShapeDtypeStruct((4, 2, HALF, 4 * hs), BF16),
        ],
        cost_estimate=cost(2 * total * width * 6 * hs, 2 * total * width + 12 * width * hs),
        name="project",
    )(*shards, mine, theirs)


def forward_body(n, *refs):
    up, their_up, down, their_down = refs[n : n + 4]
    outs, (acc, sums) = refs[n + 4 : -2], refs[-2:]
    step = pl.program_id(0)
    x = stacked(refs[:n])
    h = dot(x, jnp.concatenate([up[...], their_up[...]], axis=1))
    h = jax.nn.gelu(h, approximate=True).astype(BF16)
    h_f = h.astype(F32)
    part = jnp.sum(h_f * h_f, axis=-1, keepdims=True)
    term = dot(h, jnp.concatenate([down[...], their_down[...]], axis=0))

    @pl.when(step == 0)
    def _():
        acc[...] = term
        sums[...] = jnp.broadcast_to(part, sums.shape)

    @pl.when(step == 1)
    def _():
        width = acc.shape[1]
        total = (acc[...] + term).astype(BF16)
        squares = (sums[...] + part).astype(BF16)
        tokens = outs[0].shape[0]
        for i, out in enumerate(outs):
            at = slice(tokens * i, tokens * (i + 1))
            out[:, 0:width] = total[at]
            out[:, width : width + 128] = squares[at]


def feed_forward(shards, slots, up, their_up, down, their_down):
    n = len(shards)
    total = sum(v.shape[0] for v in shards)
    tokens, width = total // slots, shards[0].shape[1]
    units = up.shape[1] // 2
    whole = [pl.BlockSpec(v.shape, lambda j: (0, 0)) for v in shards]
    rise = pl.BlockSpec((width, units), lambda j: (0, j))
    fall = pl.BlockSpec((units, width), lambda j: (j, 0))
    return pl.pallas_call(
        lambda *refs: forward_body(n, *refs),
        grid=(2,),
        in_specs=whole + [rise, rise, fall, fall],
        out_specs=[pl.BlockSpec((tokens, width + 128), lambda j: (0, 0))] * slots,
        out_shape=[jax.ShapeDtypeStruct((tokens, width + 128), BF16)] * slots,
        scratch_shapes=[pltpu.VMEM((total, width), F32), pltpu.VMEM((total, 128), F32)],
        cost_estimate=cost(16 * total * width * units, 4 * total * width + 16 * width * units),
        name="feed_forward",
    )(*shards, up, their_up, down, their_down)


def row_body(inv_root, hs, top_ref, qcol, kcol, *refs):
    (cur0, cur1, prv0, prv1, pcur0, pcur1, pprv0, pprv1) = refs[:8]
    (edge0, edge1, pedge0, pedge1) = refs[8:12]
    accs, dens = refs[12:14], refs[14:16]
    r = pl.program_id(0)
    first = r == 0
    n = qcol.shape[0] // 2
    mask = kcol[...] <= qcol[...]
    open_prev = jnp.logical_not(jnp.logical_and(first, top_ref[0] == 1))
    used = jnp.logical_or(mask, jnp.broadcast_to(open_prev, mask.shape))

    def part(ref, at):
        return ref[:, :, 0, :, at : at + hs].reshape(n, hs)

    def edge_part(ref, at):
        return ref[:, :, :, at : at + hs].reshape(n, hs)

    def either(prv, edge, at):
        return jnp.where(first, edge_part(edge, at), part(prv, 2 * hs + at))

    for h in range(2):
        q = jnp.concatenate([part(cur0, h * hs), part(cur1, h * hs)], axis=0)

        def pair(base):
            a, b = base + hs * h, base + hs * (1 - h)
            same = [part(cur0, 2 * hs + a), part(cur1, 2 * hs + a)]
            same += [part(pcur0, 2 * hs + b), part(pcur1, 2 * hs + b)]
            prev = [either(prv0, edge0, a), either(prv1, edge1, a)]
            prev += [either(pprv0, pedge0, b), either(pprv1, pedge1, b)]
            return jnp.concatenate(same, axis=0), jnp.concatenate(prev, axis=0)

        k_same, k_prev = pair(0)
        v_same, v_prev = pair(2 * hs)
        scores = jnp.where(mask, dot_t(q, k_same), dot_t(q, k_prev)) * inv_root
        w = jnp.where(used, jnp.exp(scores), 0.0)
        total = jnp.sum(w, axis=-1, keepdims=True)
        w_same = jnp.where(mask, w, 0.0).astype(BF16)
        w_prev = jnp.where(mask, 0.0, w).astype(BF16)
        out = dot(w_same, v_same) + dot(w_prev, v_prev)
        total = jnp.broadcast_to(total, out.shape)
        for i in range(2):
            at = slice(h * hs, (h + 1) * hs)
            shape = (4, 2, HALF, hs)
            accs[i][:, :, 0, :, at] = out[n * i : n * (i + 1)].reshape(shape)
            dens[i][:, :, 0, :, at] = total[n * i : n * (i + 1)].reshape(shape)


def row_attention(top, qcol, kcol, qkv, their_qkv, edge, their_edge, hs, inv_root):
    rows = qkv[0].shape[2]
    width = 6 * hs
    now = pl.BlockSpec((4, 2, 1, HALF, width), lambda r: (0, 0, r, 0, 0))
    before = pl.BlockSpec(
        (4, 2, 1, HALF, width), lambda r: (0, 0, jnp.maximum(r - 1, 0), 0, 0)
    )
    whole = lambda a: pl.BlockSpec(a.shape, lambda r: (0,) * a.ndim)
    out = jax.ShapeDtypeStruct((4, 2, rows, HALF, 2 * hs), F32)
    out_spec = pl.BlockSpec((4, 2, 1, HALF, 2 * hs), lambda r: (0, 0, r, 0, 0))
    n = qcol.shape[0]
    outs = pl.pallas_call(
        lambda *refs: row_body(inv_root, hs, *refs),
        grid=(rows,),
        in_specs=[SMEM, whole(qcol), whole(kcol)]
        + [now, now, before, before] * 2
        + [whole(e) for e in (*edge, *their_edge)],
        out_specs=[out_spec] * 4,
        out_shape=[out] * 4,
        cost_estimate=cost(rows * 32 * n * n * hs, rows * 32 * n * hs, rows * 4 * n * n),
        name="row_attention",
    )(top, qcol, kcol, *qkv, *qkv, *their_qkv, *their_qkv, *edge, *their_edge)
    return outs[:2], outs[2:]


def col_body(inv_root, hs, own_rows, bias, x, *refs):
    out = refs[-1]
    rows, cols, _ = x.shape
    chunk = 16
    spots = rows * cols
    step = chunk * cols
    den_rows = jnp.zeros((rows, 128), F32)
    lane = lax.broadcasted_iota(jnp.int32, (spots, 128), 1)
    spot = lax.broadcasted_iota(jnp.int32, (spots, 128), 0)
    for h in range(2):

        def part(at):
            return x[:, :, at * hs : (at + 1) * hs].reshape(spots, hs)

        q, k, v = part(h), part(2 + h), part(4 + h)
        accs, sums = [], []
        for i in range(rows // chunk):
            n = step * (i + 1)
            s = dot_t(q[step * i : step * (i + 1)], k[:n]) * inv_root + bias[h]
            qi = lax.broadcasted_iota(jnp.int32, s.shape, 0) + step * i
            ki = lax.broadcasted_iota(jnp.int32, s.shape, 1)
            keep = jnp.logical_and(((qi - ki) & (cols - 1)) == 0, ki < qi)
            w = jnp.where(keep, jnp.exp(s), 0.0)
            accs.append(dot(w.astype(BF16), v[:n]))
            sums.append(jnp.sum(w, axis=-1, keepdims=True))
        a = jnp.concatenate(accs, axis=0).astype(BF16).reshape(rows, cols, hs)
        d = jnp.concatenate(sums, axis=0)
        spread = jnp.where(lane == (spot & (cols - 1)) + cols * h, d, 0.0)
        den_rows = den_rows + jnp.sum(spread.reshape(rows, cols, 128), axis=1)
        for r in range(rows):
            out[r // own_rows, 0, r % own_rows, :, h * hs : (h + 1) * hs] = a[r]
    fill = jnp.zeros((cols - own_rows, 128), F32)
    for b in range(rows // own_rows):
        block = jnp.concatenate([den_rows[own_rows * b : own_rows * (b + 1)], fill], axis=0)
        out[b, 0, own_rows, :, 0:128] = block.astype(BF16)
        out[b, 0, own_rows, :, 128:256] = jnp.zeros((cols, 128), BF16)


def column_attention(group, bias, x, own_rows, hs, inv_root, earlier=()):
    rows, cols, _ = x.shape
    spots = rows * cols
    peers = rows // own_rows
    return pl.pallas_call(
        lambda *refs: col_body(inv_root, hs, own_rows, *refs),
        grid=(1,),
        in_specs=[SMEM, pl.BlockSpec(x.shape, lambda i: (0, 0, 0))]
        + [pl.BlockSpec(memory_space=pl.ANY)] * len(earlier),
        out_specs=pl.BlockSpec(
            (peers, 1, own_rows + 1, cols, 2 * hs), lambda i: (0, group, 0, 0, 0)
        ),
        out_shape=jax.ShapeDtypeStruct((peers, 2, own_rows + 1, cols, 2 * hs), BF16),
        input_output_aliases={2: 0} if earlier else {},
        cost_estimate=cost(6 * spots * spots * hs, 16 * spots * hs, 2 * spots * spots),
        name="column_attention",
    )(bias, x, *earlier)


def term_body(hs, rows, group, splits, got, acc, den, f0, f1, f2, f3, w_mine, w_their, *outs):
    spots = 8 * rows * HALF
    unit = lax.broadcasted_iota(jnp.int32, (spots, 128), 0) // HALF
    line = lax.broadcasted_iota(jnp.int32, (spots, 128), 1)
    hit = jnp.logical_and(unit == (line // HALF) * rows + line % HALF, line % HALF < rows)
    table = got[:, group, rows, :, 0:128].reshape(128, 128)
    table = dot(jnp.where(hit, 1.0, 0.0).astype(BF16), table)
    spot = lax.broadcasted_iota(jnp.int32, (spots, 128), 0) % HALF
    ones = jnp.ones((128, 128), BF16)
    parts = []
    for h in range(2):
        at = slice(h * hs, (h + 1) * hs)
        col_den = dot(jnp.where(line == spot + HALF * h, table, 0.0).astype(BF16), ones)
        total = acc[:, :, :, :, at].reshape(spots, hs)
        total = total + got[:, group, 0:rows, :, at].reshape(spots, hs).astype(F32)
        parts.append((total / (den[:, :, :, :, at].reshape(spots, hs) + col_den)).astype(BF16))
    halves = jnp.concatenate(parts, axis=1).reshape(4, 2, rows, HALF, 2 * hs)
    blocks = [halves[s, g, r] for s in range(4) for r in range(rows) for g in range(2)]
    attended = jnp.concatenate(blocks, axis=0)
    att_f = attended.astype(F32)
    squares = jnp.sum(att_f * att_f, axis=-1, keepdims=True)
    weight = jnp.concatenate([w_mine[...], w_their[...]], axis=0)
    term = dot(attended, weight)
    width = term.shape[1]
    for out, (slot, low, high) in zip(outs, splits):
        f = (f0, f1, f2, f3)[slot]
        tokens = f.shape[0]
        at = slice(tokens * slot + low, tokens * slot + high)
        out[:, 0:width] = (f[low:high, 0:width].astype(F32) + term[at]).astype(BF16)
        out[:, width:] = (f[low:high, width:].astype(F32) + squares[at]).astype(BF16)


def terms(group, got, acc, den, ff, w_mine, w_their, hs, rows, splits):
    tokens, full = ff[0].shape
    return pl.pallas_call(
        lambda *refs: term_body(hs, rows, group, splits, *refs),
        in_specs=[VMEM] * 9,
        out_specs=[VMEM] * len(splits),
        out_shape=[jax.ShapeDtypeStruct((b - a, full), BF16) for _, a, b in splits],
        cost_estimate=cost(16 * tokens * hs * full, 20 * tokens * full),
        name="terms",
    )(got, acc, den, *ff, w_mine, w_their)


def thirds_body(t0, t1, t2, o0, o1, o2):
    o0[...] = t0[...]
    o1[...] = t1[...]
    o2[...] = t2[...]


def thirds_of(arrays):
    rows, width = arrays[0].shape
    third = rows // 3
    block = lambda at: pl.BlockSpec((third, width), lambda i: (at, 0))
    return pl.pallas_call(
        thirds_body,
        grid=(1,),
        in_specs=[block(0), block(1), block(2)],
        out_specs=[block(0)] * 3,
        out_shape=[jax.ShapeDtypeStruct((third, width), BF16)] * 3,
        cost_estimate=cost(0, 4 * rows * width),
        name="thirds",
    )(*arrays)


def far_body(t0, t1, t2, g0, g1, g2, o0, o1, o2):
    for t, g, o in ((t0, g0, o0), (t1, g1, o1), (t2, g2, o2)):
        o[...] = (t[...].astype(F32) + g[...].astype(F32)).astype(BF16)


def add_far(arrays, parts):
    third, width = parts[0].shape
    block = lambda at: pl.BlockSpec((third, width), lambda i: (at, 0))
    spread = [block(0), block(1), block(2)]
    return pl.pallas_call(
        far_body,
        grid=(1,),
        in_specs=spread + [block(0)] * 3,
        out_specs=spread,
        out_shape=[jax.ShapeDtypeStruct(arrays[0].shape, BF16)] * 3,
        input_output_aliases={0: 0, 1: 1, 2: 2},
        cost_estimate=cost(6 * third * width, 18 * third * width),
        name="add_far",
    )(*arrays, *parts)


def near_body(t0, t1, r0, r1, r2, o0, o1):
    o0[...] = (t0[...].astype(F32) + r0[...].astype(F32) + r1[...].astype(F32)).astype(BF16)
    o1[...] = (t1[...].astype(F32) + r2[...].astype(F32)).astype(BF16)


def add_near(*arrays):
    rows, width = arrays[0].shape
    block = pl.BlockSpec((rows // 3, width), lambda i: (i, 0))
    return pl.pallas_call(
        near_body,
        grid=(3,),
        in_specs=[block] * 5,
        out_specs=[block] * 2,
        out_shape=[jax.ShapeDtypeStruct((rows, width), BF16)] * 2,
        cost_estimate=cost(3 * rows * width, 14 * rows * width),
        name="add_near",
    )(*arrays)


def head_body(x, mine, m0, m1, m2, targets, gain, weight, layer_out, line):
    width = x.shape[1]
    mixed, spread = 0.0, 0.0
    for m in (mine, m0, m1, m2):
        mixed = mixed + m[:, :width].astype(F32)
        spread = spread + m[:, width : width + 1].astype(F32)
    lo = (x[...].astype(F32) + mixed).astype(BF16)
    layer_out[...] = lo
    back = lo.astype(F32)
    inv_norm = lax.rsqrt(jnp.sum(back * back, axis=-1, keepdims=True) / width + EPS)
    head_in = (back * inv_norm * gain[...]).astype(BF16)
    raised = jnp.exp(dot(head_in, weight[...]))
    prob = raised / jnp.sum(raised, axis=-1, keepdims=True)
    levels = lax.broadcasted_iota(jnp.int32, prob.shape, 1)
    grad = prob - jnp.where(levels == targets[...], 1.0, 0.0)
    scaled = gain[...] * dot_t(grad.astype(BF16), weight[...])
    lean = jnp.sum(back * scaled, axis=-1, keepdims=True) / width
    layer_grad = inv_norm * scaled - back * (inv_norm * inv_norm * inv_norm) * lean
    head_f = head_in.astype(F32)
    out_sq = jnp.sum(head_f * head_f, axis=-1, keepdims=True) * jnp.sum(
        grad * grad, axis=-1, keepdims=True
    )
    layer_sq = jnp.sum(layer_grad * layer_grad, axis=-1, keepdims=True)
    norm = jnp.sqrt(laid(out_sq + spread * layer_sq))
    line[...] = jnp.broadcast_to(norm[None], line.shape)


def head(x, mine, m0, m1, m2, targets, gain, weight, devices):
    return pl.pallas_call(
        head_body,
        in_specs=[VMEM] * 8,
        out_specs=[pl.BlockSpec(memory_space=pltpu.VMEM)] * 2,
        out_shape=[
            jax.ShapeDtypeStruct(x.shape, BF16),
            jax.ShapeDtypeStruct((devices, 1, 256), F32),
        ],
        name="head",
    )(x, mine, m0, m1, m2, targets, gain, weight)


def pick_body(table, where, spot, out):
    devices = table.shape[0]
    count = where.shape[1]
    hit = lax.broadcasted_iota(jnp.int32, (devices, count), 0) == where[...]
    hot = jnp.where(hit, 1.0, 0.0).astype(BF16)

    full = table[...]
    high = full.astype(BF16)
    rest = full - high.astype(F32)
    mid = rest.astype(BF16)
    low = (rest - mid.astype(F32)).astype(BF16)
    parts = jnp.concatenate([high, mid, low], axis=0)
    lines = lax.dot_general(
        parts,
        jnp.concatenate([hot, hot, hot], axis=0),
        (((0,), (0,)), ((), ())),
        preferred_element_type=F32,
    )
    mine = lax.broadcasted_iota(jnp.int32, lines.shape, 0) == spot[...]
    picked = jnp.sum(jnp.where(mine, lines, 0.0), axis=0, keepdims=True)
    out[...] = count * picked / jnp.sum(picked, axis=-1, keepdims=True)


def pick(table, where, spot):
    return pl.pallas_call(
        pick_body,
        in_specs=[pl.BlockSpec(memory_space=pltpu.VMEM)] * 3,
        out_specs=pl.BlockSpec(memory_space=pltpu.VMEM),
        out_shape=jax.ShapeDtypeStruct(where.shape, F32),
        name="pick",
    )(table, where, spot)


def per_device(
    activations,
    targets,
    candidates,
    mix_gain,
    project_weight,
    output_weight,
    up_weight,
    down_weight,
    pattern_bias,
    head_gain,
    head_weight,
):
    rows, cols, width = activations.shape
    hs = project_weight.shape[2]
    tokens = rows * cols
    row_peers = lax.axis_size(ROW)
    inv_root = 1.0 / math.sqrt(hs)
    third = tokens // 3

    devices = lax.axis_size(ALL)

    their_project = swap_core(project_weight)
    their_up = swap_core(up_weight)
    their_down = swap_core(down_weight)
    their_output = swap_core(output_weight)
    bias = jnp.concatenate([pattern_bias, swap_core(pattern_bias)])

    x = activations.reshape(tokens, width)
    own = normalize(x, mix_gain[None, :])

    def after(first, values):
        return lax.optimization_barrier((first, values))[1]

    def ffn(shards, slots):
        return feed_forward(shards, slots, up_weight, their_up, down_weight, their_down)

    near = (up_z(own), down_z(own), swap_x(own))
    (ff_own,) = ffn((own,), 1)
    s_a, s_b, s_p = after((ff_own, their_project), near)
    s_aa, s_pb, s_pa = up_z(s_a), down_z(s_p), swap_x(s_a)

    def columns(shards):
        qkv, edge = project(shards, project_weight, their_project, rows)
        got = lax.all_to_all(
            qkv.reshape(row_peers, rows * HALF, 6 * hs), ROW, split_axis=0, concat_axis=0, tiled=True
        )
        return qkv, edge, got

    def attend_columns(group, got, *earlier):
        x = got.reshape(row_peers * rows, HALF, 6 * hs)
        return column_attention(group, bias, x, rows, hs, inv_root, earlier)

    qkv0, edge0, got0 = columns((own, s_a, s_b, s_p))
    edge0 = next_row(edge0)
    their_edge0 = swap_core(edge0)
    their_qkv0 = swap_core(qkv0)
    s_aa, s_pa, s_pb = after(qkv0, (s_aa, s_pa, s_pb))
    h_aa, h_pa, h_pb = thirds_of((s_aa, s_pa, s_pb))
    far = (swap_x(h_aa), up_z(h_pa), down_z(h_pb))
    back = attend_columns(0, after((s_aa, s_pa, s_pb), got0))
    away = after((back, their_qkv0), (s_aa, s_pa, s_pb, *far))
    qkv1, edge1, got1 = columns(away)
    their_qkv1 = swap_core(qkv1)
    edge1 = next_row(edge1)
    their_edge1 = swap_core(edge1)
    ff1 = ffn(after(qkv1, away), 4)
    back = attend_columns(1, after((ff1, their_qkv1), got1), back)
    again = lax.all_to_all(back, ROW, split_axis=0, concat_axis=0, tiled=True)

    xl, z, core = lax.axis_index(XL), lax.axis_index(Z), lax.axis_index(CORE)
    n_z = lax.axis_size(Z)
    shift_x = jnp.array([0, 0, 0, 1, 0, 1, 1, 1], jnp.int32)
    shift_z = jnp.array([0, 3, 1, 0, 2, 3, 1, 2], jnp.int32)
    chip = ((xl + shift_x) % 2) * n_z + (z + shift_z) % n_z
    starts = chip * 2 * cols
    offs = jnp.arange(cols, dtype=jnp.int32)
    mine = (starts[:, None] + core * cols + offs[None, :]).reshape(-1)
    theirs = (starts[:, None] + (1 - core) * cols + offs[None, :]).reshape(-1)
    top = (lax.axis_index(ROW) == 0).astype(jnp.int32)[None]
    acc, den = row_attention(
        after(back, top),
        mine[:, None],
        jnp.concatenate([mine, theirs])[None, :],
        (qkv0, qkv1),
        (their_qkv0, their_qkv1),
        (edge0, edge1),
        (their_edge0, their_edge1),
        hs,
        inv_root,
    )
    thirds = [(3, third * i, third * (i + 1)) for i in range(3)]
    t_aa, t_pa, t_pb, f0, f1, f2 = terms(
        1, again, acc[1], den[1], ff1, output_weight, their_output, hs, rows,
        [(i, 0, tokens) for i in range(3)] + thirds,
    )

    t_aa, t_pa, t_pb = add_far((t_aa, t_pa, t_pb), (swap_x(f0), down_z(f1), up_z(f2)))
    r_aa, r_pa, r_pb = down_z(t_aa), swap_x(t_pa), up_z(t_pb)
    ff0 = ffn(after(t_pb, (s_a, s_b, s_p)), 3)
    t_own, t_a, t_b, t_p = terms(
        0, again, acc[0], den[0], (ff_own, *ff0), output_weight, their_output, hs, rows,
        [(i, 0, tokens) for i in range(4)],
    )
    from_b = up_z(t_b)
    t_a, t_p = add_near(t_a, t_p, r_aa, r_pa, r_pb)
    from_a, from_p = down_z(t_a), swap_x(t_p)

    layer_out, line = head(
        x,
        t_own,
        from_a,
        from_b,
        from_p,
        targets.reshape(tokens, 1),
        head_gain[None, :],
        head_weight,
        devices,
    )
    table = lax.all_to_all(
        line,
        ALL,
        split_axis=0,
        concat_axis=0,
        tiled=True,
    ).reshape(devices, 256)
    full_cols = cols * lax.axis_size(COL)
    c_row, c_col = candidates // full_cols, candidates % full_cols
    where = (c_row // rows) * lax.axis_size(COL) + c_col // cols
    spot = (c_row % rows) * cols + c_col % cols
    chosen = pick(table, where[None, :], spot[None, :])
    return (layer_out.reshape(rows, cols, width), chosen.reshape(-1))


def solution(mesh):
    split = Mesh(mesh.devices.reshape(2, 4, 2, 4, 2), ("row_0", "row_1", "col_0", "col_1", "col_2"))

    return jax.shard_map(
        per_device,
        mesh=split,
        in_specs=(
            P(ROW, COL, None),
            P(ROW, COL),
            P(),
            P(),
            P(None, None, COL),
            P(COL, None),
            P(None, COL),
            P(COL, None),
            P(COL),
            P(),
            P(),
        ),
        out_specs=(P(ROW, COL, None), P()),
        check_vma=False,
    )
```

```python
import math

import jax
import jax.numpy as jnp
from jax import lax
from jax.experimental import pallas as pl
from jax.experimental.pallas import tpu as pltpu
from jax.sharding import Mesh
from jax.sharding import PartitionSpec as P

COL = ("col_0", "col_1", "col_2")
ROW = ("row_0", "row_1")
ALL = ("row_0", "row_1", "col_0", "col_1", "col_2")
XL, Z, CORE = COL

EPS = 1e-06
F32 = jnp.float32
BF16 = jnp.bfloat16


def permuted(array, axis, by):
    n = lax.axis_size(axis)
    return lax.ppermute(array, axis, [(i, (i + by) % n) for i in range(n)])


def up_z(array):
    return permuted(array, Z, 1)


def down_z(array):
    return permuted(array, Z, -1)


def swap_x(array):
    return permuted(array, XL, 1)


def swap_core(array):
    return permuted(array, CORE, 1)


def next_row(array):
    n = lax.axis_size(ROW)
    return lax.ppermute(array, ROW, [(i, i + 1) for i in range(n - 1)])


def dot(a, b):
    return jnp.dot(a, b, preferred_element_type=F32)


def dot_t(a, b):
    return lax.dot_general(a, b, (((1,), (1,)), ((), ())), preferred_element_type=F32)


def cost(flops, bytes_accessed, exps=0):
    return pl.CostEstimate(flops=flops, bytes_accessed=bytes_accessed, transcendentals=exps)


VMEM = pl.BlockSpec(memory_space=pltpu.VMEM)
SMEM = pl.BlockSpec(memory_space=pltpu.SMEM)
HALF = 16


def laid(column, lanes=256):
    shape = (column.shape[0], lanes)
    hit = lax.broadcasted_iota(jnp.int32, shape, 1) == lax.broadcasted_iota(jnp.int32, shape, 0)
    return jnp.sum(jnp.where(hit, column, 0.0), axis=0, keepdims=True)


def norm_body(x, gain, out):
    v = x[...].astype(F32)
    scale = lax.rsqrt(jnp.sum(v * v, axis=-1, keepdims=True) / v.shape[1] + EPS)
    out[...] = (v * scale * gain[...]).astype(BF16)


def normalize(x, gain):
    return pl.pallas_call(
        norm_body,
        in_specs=[VMEM, VMEM],
        out_specs=VMEM,
        out_shape=jax.ShapeDtypeStruct(x.shape, BF16),
        cost_estimate=cost(5 * x.size, 4 * x.size),
        name="normalize",
    )(x, gain)


def stacked(refs):
    return jnp.concatenate([ref[...] for ref in refs], axis=0)


def project_body(rows, n, *refs):
    mine, theirs, out, edge = refs[n:]
    x = stacked(refs[:n])
    w = jnp.concatenate([mine[0], theirs[0]], axis=1)
    y = dot(x, w).astype(BF16).reshape(4, rows, 2, HALF, w.shape[1])
    for g in range(2):
        out[:, g] = y[:, :, g]
        edge[:, g] = y[:, rows - 1, g]


def project(shards, mine, theirs, rows):
    n = len(shards)
    total = sum(v.shape[0] for v in shards)
    _, width, hs = mine.shape
    whole = [pl.BlockSpec(v.shape, lambda j: (0, 0)) for v in shards]
    weight = pl.BlockSpec((1, width, hs), lambda j: (j, 0, 0))
    return pl.pallas_call(
        lambda *refs: project_body(rows, n, *refs),
        grid=(3,),
        in_specs=whole + [weight] * 2,
        out_specs=[
            pl.BlockSpec((4, 2, rows, HALF, 2 * hs), lambda j: (0, 0, 0, 0, j)),
            pl.BlockSpec((4, 2, HALF, 2 * hs), lambda j: (0, 0, 0, jnp.maximum(j - 1, 0))),
        ],
        out_shape=[
            jax.ShapeDtypeStruct((4, 2, rows, HALF, 6 * hs), BF16),
            jax.ShapeDtypeStruct((4, 2, HALF, 4 * hs), BF16),
        ],
        cost_estimate=cost(2 * total * width * 6 * hs, 2 * total * width + 12 * width * hs),
        name="project",
    )(*shards, mine, theirs)


ANY = pl.BlockSpec(memory_space=pl.ANY)


def forward_body(n, slots, unrolled, *refs):
    shards, (up, their_up, down, their_down) = refs[:n], refs[n : n + 4]
    outs, (x, rise, fall, hidden, done, sems, out_sems) = refs[n + 4 : -7], refs[-7:]
    tokens = x.shape[0] // slots
    width, units = up.shape
    sizes = [ref.shape[0] for ref in shards]
    starts = [sum(sizes[:i]) for i in range(n)]

    def fetch(source, target, i):
        copy = pltpu.make_async_copy(source, target, sems.at[i])
        copy.start()
        return copy

    def shard(i):
        return fetch(shards[i], x.at[starts[i] : starts[i] + sizes[i]], i)

    x_in = [shard(0)]
    ups = [fetch(up, rise.at[:, :units], n), fetch(their_up, rise.at[:, units:], n + 1)]
    x_in += [shard(i) for i in range(1, n)]
    downs = [fetch(down, fall.at[:units], n + 2), fetch(their_down, fall.at[units:], n + 3)]

    def rows_of(s):
        return pl.ds(s * tokens if unrolled else pl.multiple_of(s * tokens, tokens), tokens)

    def each_slot(step):
        if unrolled:
            for s in range(slots):
                step(s, 0)
        else:
            lax.fori_loop(0, slots, step, 0)

    def ascend(s, carry):
        at = rows_of(s)
        for i in range(n):

            @pl.when(s == starts[i] // tokens)
            def _():
                x_in[i].wait()

        total = 0.0
        for c in range(2):

            @pl.when(s == 0)
            def _():
                ups[c].wait()

            lanes = slice(units * c, units * (c + 1))
            h = jax.nn.gelu(dot(x[at, :], rise[:, lanes]), approximate=True).astype(BF16)
            hidden[at, lanes] = h
            h_f = h.astype(F32)
            total = total + jnp.sum(h_f * h_f, axis=-1, keepdims=True)
        done[at, width : width + 128] = jnp.broadcast_to(total, (tokens, 128)).astype(BF16)
        return carry

    each_slot(ascend)
    for copy in downs:
        copy.wait()
    copies = []
    for s in range(slots):
        source = done.at[tokens * s : tokens * (s + 1)]
        copies.append(pltpu.make_async_copy(source, outs[s], out_sems.at[s]))

    def descend(s, carry):
        at = rows_of(s)
        done[at, 0:width] = dot(hidden[at, :], fall[...]).astype(BF16)
        for i in range(slots):

            @pl.when(s == i)
            def _():
                copies[i].start()

        return carry

    each_slot(descend)
    for copy in copies:
        copy.wait()


def feed_forward(shards, slots, up, their_up, down, their_down):
    n = len(shards)
    total = sum(v.shape[0] for v in shards)
    tokens, width = total // slots, shards[0].shape[1]
    units = 2 * up.shape[1]
    return pl.pallas_call(
        lambda *refs: forward_body(n, slots, slots == 4, *refs),
        in_specs=[ANY] * (n + 4),
        out_specs=[ANY] * slots,
        out_shape=[jax.ShapeDtypeStruct((tokens, width + 128), BF16)] * slots,
        scratch_shapes=[
            pltpu.VMEM((total, width), BF16),
            pltpu.VMEM((width, units), BF16),
            pltpu.VMEM((units, width), BF16),
            pltpu.VMEM((total, units), BF16),
            pltpu.VMEM((total, width + 128), BF16),
            pltpu.SemaphoreType.DMA((n + 4,)),
            pltpu.SemaphoreType.DMA((slots,)),
        ],
        cost_estimate=cost(4 * total * width * units, 4 * total * width + 4 * width * units),
        name="feed_forward",
    )(*shards, up, their_up, down, their_down)


def row_body(inv_root, hs, top_ref, qcol, kcol, *refs):
    cur, theirs, edges = refs[:2], refs[2:6], refs[6:10]
    accs, dens, above = refs[10:12], refs[12:14], refs[14:]
    r = pl.program_id(0)
    first = r == 0
    n = qcol.shape[0] // 2
    mask = kcol[...] <= qcol[...]
    closed = jnp.logical_and(first, top_ref[0] == 1)
    same_one = jnp.where(mask, 1.0, 0.0)
    prev_one = jnp.where(closed, 0.0, 1.0 - same_one).astype(BF16)
    same_one = same_one.astype(BF16)
    ones = jnp.ones((kcol.shape[1], hs), BF16)
    scale = inv_root * math.log2(math.e)

    @pl.when(first)
    def _():
        for keep, edge in zip(above, edges):
            keep[...] = edge[...].reshape(n, 4 * hs)

    now = [ref[:, :, 0, :, 2 * hs :].reshape(n, 4 * hs) for ref in cur]
    for i in range(2):
        pair = [ref[:, :, 0].reshape(n, 2 * hs) for ref in theirs[2 * i : 2 * i + 2]]
        now.append(jnp.concatenate(pair, axis=1))
    before = [ref[...] for ref in above]
    for h in range(2):
        at = slice(h * hs, (h + 1) * hs)
        q = jnp.concatenate([ref[:, :, 0, :, at].reshape(n, hs) for ref in cur], axis=0)

        def taken(parts, base):
            lanes = [base + hs * h] * 2 + [base + hs * (1 - h)] * 2
            return jnp.concatenate([p[:, m : m + hs] for p, m in zip(parts, lanes)], axis=0)

        scores = jnp.where(mask, dot_t(q, taken(now, 0)), dot_t(q, taken(before, 0))) * scale
        w = jnp.exp2(scores).astype(BF16)
        out = dot(w * same_one, jnp.concatenate([taken(now, 2 * hs), ones], axis=1))
        out = out + dot(w * prev_one, jnp.concatenate([taken(before, 2 * hs), ones], axis=1))
        shape = (4, 2, HALF, hs)
        for i in range(2):
            half = out[n * i : n * (i + 1)]
            accs[i][:, :, 0, :, at] = half[:, :hs].astype(BF16).reshape(shape)
            dens[i][:, :, 0, :, at] = half[:, hs:].reshape(shape)
    for keep, value in zip(above, now):
        keep[...] = value


def row_attention(top, qcol, kcol, qkv, their_qkv, edge, their_edge, hs, inv_root):
    rows = qkv[0].shape[2]
    now = pl.BlockSpec((4, 2, 1, HALF, 6 * hs), lambda r: (0, 0, r, 0, 0))
    keys = pl.BlockSpec((4, 2, 1, HALF, 2 * hs), lambda r: (0, 0, r, 0, 1))
    values = pl.BlockSpec((4, 2, 1, HALF, 2 * hs), lambda r: (0, 0, r, 0, 2))
    whole = lambda a: pl.BlockSpec(a.shape, lambda r: (0,) * a.ndim)
    out = lambda kind: jax.ShapeDtypeStruct((4, 2, rows, HALF, 2 * hs), kind)
    out_spec = pl.BlockSpec((4, 2, 1, HALF, 2 * hs), lambda r: (0, 0, r, 0, 0))
    n = qcol.shape[0]
    outs = pl.pallas_call(
        lambda *refs: row_body(inv_root, hs, *refs),
        grid=(rows,),
        in_specs=[SMEM, whole(qcol), whole(kcol), now, now, keys, values, keys, values]
        + [whole(e) for e in (*edge, *their_edge)],
        out_specs=[out_spec] * 4,
        out_shape=[out(BF16)] * 2 + [out(F32)] * 2,
        scratch_shapes=[pltpu.VMEM((n // 2, 4 * hs), BF16)] * 4,
        cost_estimate=cost(rows * 32 * n * n * hs, rows * 32 * n * hs, rows * 4 * n * n),
        name="row_attention",
    )(
        top, qcol, kcol, *qkv, their_qkv[0], their_qkv[0], their_qkv[1], their_qkv[1],
        *edge, *their_edge,
    )
    return outs[:2], outs[2:]


def col_body(inv_root, hs, own_rows, bias, their_bias, x, *refs):
    out = refs[-1]
    rows, cols, _ = x.shape
    chunk = 16
    spots = rows * cols
    step = chunk * cols
    log2e = math.log2(math.e)
    lane = lax.broadcasted_iota(jnp.int32, (step, 128), 1)
    spot = lax.broadcasted_iota(jnp.int32, (step, 128), 0) & (cols - 1)
    ones = jnp.ones((spots, hs), BF16)

    def part(at):
        return x[:, :, at * hs : (at + 1) * hs].reshape(spots, hs)

    den_rows = []
    for i in range(rows // chunk):
        n = step * (i + 1)
        qi = lax.broadcasted_iota(jnp.int32, (step, n), 0) + step * i
        ki = lax.broadcasted_iota(jnp.int32, (step, n), 1)
        keep = jnp.logical_and(((qi - ki) & (cols - 1)) == 0, ki < qi)
        laid_out = 0.0
        for h in range(2):
            q, k, v = part(h), part(2 + h), part(4 + h)
            s = dot_t(q[step * i : n], k[:n]) * (inv_root * log2e)
            s = s + (bias, their_bias)[h][0] * log2e
            w = jnp.where(keep, jnp.exp2(s), 0.0).astype(BF16)
            a = dot(w, jnp.concatenate([v[:n], ones[:n]], axis=1))
            laid_out = laid_out + jnp.where(lane == spot + cols * h, a[:, hs:], 0.0)
            a = a[:, :hs].astype(BF16).reshape(chunk, cols, hs)
            for j in range(chunk):
                r = chunk * i + j
                out[r // own_rows, 0, r % own_rows, :, h * hs : (h + 1) * hs] = a[j]
        den_rows.append(jnp.sum(laid_out.reshape(chunk, cols, 128), axis=1))
    den_rows = jnp.concatenate(den_rows, axis=0)
    fill = jnp.zeros((cols - own_rows, 128), F32)
    for b in range(rows // own_rows):
        block = jnp.concatenate([den_rows[own_rows * b : own_rows * (b + 1)], fill], axis=0)
        out[b, 0, own_rows, :, 0:128] = block.astype(BF16)
        out[b, 0, own_rows, :, 128:256] = jnp.zeros((cols, 128), BF16)


def column_attention(group, bias, x, own_rows, hs, inv_root, earlier=()):
    rows, cols, _ = x.shape
    spots = rows * cols
    peers = rows // own_rows
    return pl.pallas_call(
        lambda *refs: col_body(inv_root, hs, own_rows, *refs),
        grid=(1,),
        in_specs=[SMEM, SMEM, pl.BlockSpec(x.shape, lambda i: (0, 0, 0))]
        + [pl.BlockSpec(memory_space=pl.ANY)] * len(earlier),
        out_specs=pl.BlockSpec(
            (peers, 1, own_rows + 1, cols, 2 * hs), lambda i: (0, group, 0, 0, 0)
        ),
        out_shape=jax.ShapeDtypeStruct((peers, 2, own_rows + 1, cols, 2 * hs), BF16),
        input_output_aliases={3: 0} if earlier else {},
        cost_estimate=cost(6 * spots * spots * hs, 16 * spots * hs, 2 * spots * spots),
        name="column_attention",
    )(*bias, x, *earlier)


def term_body(hs, rows, group, base, splits, got, acc, den, *refs):
    count = len({slot for slot, _, _ in splits})
    ffs, (w_mine, w_their), outs = refs[:count], refs[count : count + 2], refs[count + 2 :]
    spots = 2 * count * rows * HALF
    lines = 2 * count * HALF
    pairs = slice(2 * base, 2 * (base + count))
    slots = slice(base, base + count)
    unit = lax.broadcasted_iota(jnp.int32, (spots, lines), 0) // HALF
    line = lax.broadcasted_iota(jnp.int32, (spots, lines), 1)
    hit = jnp.logical_and(unit == (line // HALF) * rows + line % HALF, line % HALF < rows)
    table = got[pairs, group, rows, :, 0:128].reshape(lines, 128)
    table = dot(jnp.where(hit, 1.0, 0.0).astype(BF16), table)
    lane = lax.broadcasted_iota(jnp.int32, (spots, 128), 1)
    spot = lax.broadcasted_iota(jnp.int32, (spots, 128), 0) % HALF
    ones = jnp.ones((128, 128), BF16)
    parts = []
    for h in range(2):
        at = slice(h * hs, (h + 1) * hs)
        col_den = dot(jnp.where(lane == spot + HALF * h, table, 0.0).astype(BF16), ones)
        total = acc[slots, :, :, :, at].reshape(spots, hs).astype(F32)
        total = total + got[pairs, group, 0:rows, :, at].reshape(spots, hs).astype(F32)
        parts.append((total / (den[slots, :, :, :, at].reshape(spots, hs) + col_den)).astype(BF16))
    halves = jnp.concatenate(parts, axis=1).reshape(count, 2, rows, HALF, 2 * hs)
    blocks = [halves[s, g, r] for s in range(count) for r in range(rows) for g in range(2)]
    attended = jnp.concatenate(blocks, axis=0)
    att_f = attended.astype(F32)
    squares = jnp.sum(att_f * att_f, axis=-1, keepdims=True)
    weight = jnp.concatenate([w_mine[...], w_their[...]], axis=0)
    term = dot(attended, weight).astype(BF16)
    width = term.shape[1]
    for out, (slot, low, high) in zip(outs, splits):
        f = ffs[slot]
        tokens = f.shape[0]
        at = slice(tokens * slot + low, tokens * slot + high)
        out[:, 0:width] = f[low:high, 0:width] + term[at]
        out[:, width:] = (f[low:high, width:].astype(F32) + squares[at]).astype(BF16)


def terms(group, base, got, acc, den, ff, w_mine, w_their, hs, rows, splits):
    tokens, full = ff[0].shape
    return pl.pallas_call(
        lambda *refs: term_body(hs, rows, group, base, splits, *refs),
        in_specs=[VMEM] * (5 + len(ff)),
        out_specs=[VMEM] * len(splits),
        out_shape=[jax.ShapeDtypeStruct((b - a, full), BF16) for _, a, b in splits],
        cost_estimate=cost(4 * len(ff) * tokens * hs * full, 5 * len(ff) * tokens * full),
        name="terms",
    )(got, acc, den, *ff, w_mine, w_their)


def thirds_body(t0, t1, t2, o0, o1, o2):
    o0[...] = t0[...]
    o1[...] = t1[...]
    o2[...] = t2[...]


def thirds_of(arrays):
    rows, width = arrays[0].shape
    third = rows // 3
    block = lambda at: pl.BlockSpec((third, width), lambda i: (at, 0))
    return pl.pallas_call(
        thirds_body,
        grid=(1,),
        in_specs=[block(0), block(1), block(2)],
        out_specs=[block(0)] * 3,
        out_shape=[jax.ShapeDtypeStruct((third, width), BF16)] * 3,
        cost_estimate=cost(0, 4 * rows * width),
        name="thirds",
    )(*arrays)


def far_body(t0, t1, t2, g0, g1, g2, o0, o1, o2):
    for t, g, o in ((t0, g0, o0), (t1, g1, o1), (t2, g2, o2)):
        o[...] = t[...] + g[...]


def add_far(arrays, parts):
    third, width = parts[0].shape
    block = lambda at: pl.BlockSpec((third, width), lambda i: (at, 0))
    spread = [block(0), block(1), block(2)]
    return pl.pallas_call(
        far_body,
        grid=(1,),
        in_specs=spread + [block(0)] * 3,
        out_specs=spread,
        out_shape=[jax.ShapeDtypeStruct(arrays[0].shape, BF16)] * 3,
        input_output_aliases={0: 0, 1: 1, 2: 2},
        cost_estimate=cost(6 * third * width, 18 * third * width),
        name="add_far",
    )(*arrays, *parts)


def near_body(t0, t1, r0, r1, r2, o0, o1):
    o0[...] = t0[...] + (r0[...] + r1[...])
    o1[...] = t1[...] + r2[...]


def add_near(*arrays):
    rows, width = arrays[0].shape
    block = pl.BlockSpec((rows // 3, width), lambda i: (i, 0))
    return pl.pallas_call(
        near_body,
        grid=(3,),
        in_specs=[block] * 5,
        out_specs=[block] * 2,
        out_shape=[jax.ShapeDtypeStruct((rows, width), BF16)] * 2,
        cost_estimate=cost(3 * rows * width, 14 * rows * width),
        name="add_near",
    )(*arrays)


def head_body(x, mine, m0, m1, m2, targets, gain, weight, layer_out, line):
    width = x.shape[1]
    mixed, spread = 0.0, 0.0
    for m in (mine, m0, m1, m2):
        mixed = mixed + m[:, :width].astype(F32)
        spread = spread + m[:, width : width + 1].astype(F32)
    lo = (x[...].astype(F32) + mixed).astype(BF16)
    layer_out[...] = lo
    back = lo.astype(F32)
    inv_norm = lax.rsqrt(jnp.sum(back * back, axis=-1, keepdims=True) / width + EPS)
    head_in = (back * inv_norm * gain[...]).astype(BF16)
    raised = jnp.exp(dot(head_in, weight[...]))
    prob = raised / jnp.sum(raised, axis=-1, keepdims=True)
    levels = lax.broadcasted_iota(jnp.int32, prob.shape, 1)
    grad = prob - jnp.where(levels == targets[...], 1.0, 0.0)
    scaled = gain[...] * dot_t(grad.astype(BF16), weight[...])
    lean = jnp.sum(back * scaled, axis=-1, keepdims=True) / width
    layer_grad = inv_norm * scaled - back * (inv_norm * inv_norm * inv_norm) * lean
    head_f = head_in.astype(F32)
    out_sq = jnp.sum(head_f * head_f, axis=-1, keepdims=True) * jnp.sum(
        grad * grad, axis=-1, keepdims=True
    )
    layer_sq = jnp.sum(layer_grad * layer_grad, axis=-1, keepdims=True)
    norm = jnp.sqrt(laid(out_sq + spread * layer_sq))
    line[...] = jnp.broadcast_to(norm[None], line.shape)


def head(x, mine, m0, m1, m2, targets, gain, weight, devices):
    return pl.pallas_call(
        head_body,
        in_specs=[VMEM] * 8,
        out_specs=[pl.BlockSpec(memory_space=pltpu.VMEM)] * 2,
        out_shape=[
            jax.ShapeDtypeStruct(x.shape, BF16),
            jax.ShapeDtypeStruct((devices, 1, 256), F32),
        ],
        name="head",
    )(x, mine, m0, m1, m2, targets, gain, weight)


def pick_body(table, where, spot, out):
    devices = table.shape[0]
    count = where.shape[1]
    hit = lax.broadcasted_iota(jnp.int32, (devices, count), 0) == where[...]
    hot = jnp.where(hit, 1.0, 0.0).astype(BF16)

    full = table[...]
    high = full.astype(BF16)
    rest = full - high.astype(F32)
    mid = rest.astype(BF16)
    low = (rest - mid.astype(F32)).astype(BF16)
    parts = jnp.concatenate([high, mid, low], axis=0)
    lines = lax.dot_general(
        parts,
        jnp.concatenate([hot, hot, hot], axis=0),
        (((0,), (0,)), ((), ())),
        preferred_element_type=F32,
    )
    mine = lax.broadcasted_iota(jnp.int32, lines.shape, 0) == spot[...]
    picked = jnp.sum(jnp.where(mine, lines, 0.0), axis=0, keepdims=True)
    out[...] = count * picked / jnp.sum(picked, axis=-1, keepdims=True)


def pick(table, where, spot):
    return pl.pallas_call(
        pick_body,
        in_specs=[pl.BlockSpec(memory_space=pltpu.VMEM)] * 3,
        out_specs=pl.BlockSpec(memory_space=pltpu.VMEM),
        out_shape=jax.ShapeDtypeStruct(where.shape, F32),
        name="pick",
    )(table, where, spot)


def per_device(
    activations,
    targets,
    candidates,
    mix_gain,
    project_weight,
    output_weight,
    up_weight,
    down_weight,
    pattern_bias,
    head_gain,
    head_weight,
):
    rows, cols, width = activations.shape
    hs = project_weight.shape[2]
    tokens = rows * cols
    row_peers = lax.axis_size(ROW)
    inv_root = 1.0 / math.sqrt(hs)
    third = tokens // 3

    devices = lax.axis_size(ALL)

    their_project = swap_core(project_weight)
    their_up = swap_core(up_weight)
    their_down = swap_core(down_weight)
    their_output = swap_core(output_weight)
    bias = (pattern_bias, swap_core(pattern_bias))

    x = activations.reshape(tokens, width)
    own = normalize(x, mix_gain[None, :])

    def after(first, values):
        return lax.optimization_barrier((first, values))[1]

    def ffn(shards, slots):
        return feed_forward(shards, slots, up_weight, their_up, down_weight, their_down)

    near = (up_z(own), down_z(own), swap_x(own))
    (ff_own,) = ffn((own,), 1)
    s_a, s_b, s_p = after((ff_own, their_project), near)
    s_aa, s_pb, s_pa = up_z(s_a), down_z(s_p), swap_x(s_a)

    def columns(shards):
        qkv, edge = project(shards, project_weight, their_project, rows)
        got = lax.all_to_all(
            qkv.reshape(row_peers, rows * HALF, 6 * hs), ROW, split_axis=0, concat_axis=0, tiled=True
        )
        return qkv, edge, got

    def attend_columns(group, got, *earlier):
        x = got.reshape(row_peers * rows, HALF, 6 * hs)
        return column_attention(group, bias, x, rows, hs, inv_root, earlier)

    qkv0, edge0, got0 = columns((own, s_a, s_b, s_p))
    edge0 = next_row(edge0)
    their_edge0 = swap_core(edge0)
    their_qkv0 = swap_core(qkv0)
    s_aa, s_pa, s_pb = after(qkv0, (s_aa, s_pa, s_pb))
    h_aa, h_pa, h_pb = thirds_of((s_aa, s_pa, s_pb))
    far = (swap_x(h_aa), up_z(h_pa), down_z(h_pb))
    back = attend_columns(0, after((s_aa, s_pa, s_pb), got0))
    away = after((back, their_qkv0), (s_aa, s_pa, s_pb, *far))
    qkv1, edge1, got1 = columns(away)
    their_qkv1 = swap_core(qkv1)
    edge1 = next_row(edge1)
    their_edge1 = swap_core(edge1)
    ff1 = ffn(after(qkv1, away), 4)
    back = attend_columns(1, after((ff1, their_qkv1), got1), back)
    again = lax.all_to_all(back, ROW, split_axis=0, concat_axis=0, tiled=True)

    xl, z, core = lax.axis_index(XL), lax.axis_index(Z), lax.axis_index(CORE)
    n_z = lax.axis_size(Z)
    shift_x = jnp.array([0, 0, 0, 1, 0, 1, 1, 1], jnp.int32)
    shift_z = jnp.array([0, 3, 1, 0, 2, 3, 1, 2], jnp.int32)
    chip = ((xl + shift_x) % 2) * n_z + (z + shift_z) % n_z
    starts = chip * 2 * cols
    offs = jnp.arange(cols, dtype=jnp.int32)
    mine = (starts[:, None] + core * cols + offs[None, :]).reshape(-1)
    theirs = (starts[:, None] + (1 - core) * cols + offs[None, :]).reshape(-1)
    top = (lax.axis_index(ROW) == 0).astype(jnp.int32)[None]
    acc, den = row_attention(
        after(back, top),
        mine[:, None],
        jnp.concatenate([mine, theirs])[None, :],
        (qkv0, qkv1),
        (their_qkv0, their_qkv1),
        (edge0, edge1),
        (their_edge0, their_edge1),
        hs,
        inv_root,
    )
    f0, f1, f2 = terms(
        1, 3, again, acc[1], den[1], ff1[3:], output_weight, their_output, hs, rows,
        [(0, third * i, third * (i + 1)) for i in range(3)],
    )
    g0, g1, g2 = swap_x(f0), down_z(f1), up_z(f2)
    t_aa, t_pa, t_pb = terms(
        1, 0, *after(f0, (again, acc[1], den[1])), ff1[:3], output_weight, their_output, hs, rows,
        [(i, 0, tokens) for i in range(3)],
    )

    t_aa, t_pa, t_pb = add_far((t_aa, t_pa, t_pb), (g0, g1, g2))
    r_aa, r_pa, r_pb = down_z(t_aa), swap_x(t_pa), up_z(t_pb)
    ff0 = ffn(after(t_pb, (s_a, s_b, s_p)), 3)
    t_own, t_a, t_b, t_p = terms(
        0, 0, again, acc[0], den[0], (ff_own, *ff0), output_weight, their_output, hs, rows,
        [(i, 0, tokens) for i in range(4)],
    )
    from_b = up_z(t_b)
    t_a, t_p = add_near(t_a, t_p, r_aa, r_pa, r_pb)
    from_a, from_p = down_z(t_a), swap_x(t_p)

    layer_out, line = head(
        x,
        t_own,
        from_a,
        from_b,
        from_p,
        targets.reshape(tokens, 1),
        head_gain[None, :],
        head_weight,
        devices,
    )
    table = lax.all_to_all(
        line,
        ALL,
        split_axis=0,
        concat_axis=0,
        tiled=True,
    ).reshape(devices, 256)
    full_cols = cols * lax.axis_size(COL)
    c_row, c_col = candidates // full_cols, candidates % full_cols
    where = (c_row // rows) * lax.axis_size(COL) + c_col // cols
    spot = (c_row % rows) * cols + c_col % cols
    chosen = pick(table, where[None, :], spot[None, :])
    return (layer_out.reshape(rows, cols, width), chosen.reshape(-1))


def solution(mesh):
    split = Mesh(mesh.devices.reshape(2, 4, 2, 4, 2), ("row_0", "row_1", "col_0", "col_1", "col_2"))

    return jax.shard_map(
        per_device,
        mesh=split,
        in_specs=(
            P(ROW, COL, None),
            P(ROW, COL),
            P(),
            P(),
            P(None, None, COL),
            P(COL, None),
            P(None, COL),
            P(COL, None),
            P(COL),
            P(),
            P(),
        ),
        out_specs=(P(ROW, COL, None), P()),
        check_vma=False,
    )
```

```python
import math

import jax
import jax.numpy as jnp
from jax import lax
from jax.experimental import pallas as pl
from jax.experimental.pallas import tpu as pltpu
from jax.sharding import Mesh
from jax.sharding import PartitionSpec as P

COL = ("col_0", "col_1", "col_2")
ROW = ("row_0", "row_1")
ALL = ("row_0", "row_1", "col_0", "col_1", "col_2")
XL, Z, CORE = COL

EPS = 1e-06
F32 = jnp.float32
BF16 = jnp.bfloat16


def permuted(array, axis, by):
    n = lax.axis_size(axis)
    return lax.ppermute(array, axis, [(i, (i + by) % n) for i in range(n)])


def up_z(array):
    return permuted(array, Z, 1)


def down_z(array):
    return permuted(array, Z, -1)


def swap_x(array):
    return permuted(array, XL, 1)


def swap_core(array):
    return permuted(array, CORE, 1)


def next_row(array):
    n = lax.axis_size(ROW)
    return lax.ppermute(array, ROW, [(i, i + 1) for i in range(n - 1)])


def dot(a, b):
    return jnp.dot(a, b, preferred_element_type=F32)


def dot_t(a, b):
    return lax.dot_general(a, b, (((1,), (1,)), ((), ())), preferred_element_type=F32)


def cost(flops, bytes_accessed, exps=0):
    return pl.CostEstimate(flops=flops, bytes_accessed=bytes_accessed, transcendentals=exps)


VMEM = pl.BlockSpec(memory_space=pltpu.VMEM)
SMEM = pl.BlockSpec(memory_space=pltpu.SMEM)
ANY = pl.BlockSpec(memory_space=pl.ANY)
HALF = 16


def laid(column, lanes=256):
    shape = (column.shape[0], lanes)
    hit = lax.broadcasted_iota(jnp.int32, shape, 1) == lax.broadcasted_iota(jnp.int32, shape, 0)
    return jnp.sum(jnp.where(hit, column, 0.0), axis=0, keepdims=True)


def norm_body(x, gain, out):
    v = x[...].astype(F32)
    scale = lax.rsqrt(jnp.sum(v * v, axis=-1, keepdims=True) / v.shape[1] + EPS)
    out[...] = (v * scale * gain[...]).astype(BF16)


def normalize(x, gain):
    return pl.pallas_call(
        norm_body,
        in_specs=[VMEM, VMEM],
        out_specs=VMEM,
        out_shape=jax.ShapeDtypeStruct(x.shape, BF16),
        cost_estimate=cost(5 * x.size, 4 * x.size),
        name="normalize",
    )(x, gain)


def stacked(refs):
    return jnp.concatenate([ref[...] for ref in refs], axis=0)


def project_body(rows, n, *refs):
    mine, theirs, out, edge = refs[n:]
    x = stacked(refs[:n])
    w = jnp.concatenate([mine[0], theirs[0]], axis=1)
    y = dot(x, w).astype(BF16).reshape(4, rows, 2, HALF, w.shape[1])
    for g in range(2):
        out[:, g] = y[:, :, g]
        edge[:, g] = y[:, rows - 1, g]


def project(shards, mine, theirs, rows):
    n = len(shards)
    total = sum(v.shape[0] for v in shards)
    _, width, hs = mine.shape
    whole = [pl.BlockSpec(v.shape, lambda j: (0, 0)) for v in shards]
    weight = pl.BlockSpec((1, width, hs), lambda j: (j, 0, 0))
    return pl.pallas_call(
        lambda *refs: project_body(rows, n, *refs),
        grid=(3,),
        in_specs=whole + [weight] * 2,
        out_specs=[
            pl.BlockSpec((4, 2, rows, HALF, 2 * hs), lambda j: (0, 0, 0, 0, j)),
            pl.BlockSpec((4, 2, HALF, 2 * hs), lambda j: (0, 0, 0, jnp.maximum(j - 1, 0))),
        ],
        out_shape=[
            jax.ShapeDtypeStruct((4, 2, rows, HALF, 6 * hs), BF16),
            jax.ShapeDtypeStruct((4, 2, HALF, 4 * hs), BF16),
        ],
        cost_estimate=cost(2 * total * width * 6 * hs, 2 * total * width + 12 * width * hs),
        name="project",
    )(*shards, mine, theirs)


def forward_body(n, slots, unrolled, *refs):
    shards, (up, their_up, down, their_down) = refs[:n], refs[n : n + 4]
    outs, (x, rise, fall, hidden, done, sems, out_sems) = refs[n + 4 : -7], refs[-7:]
    tokens = x.shape[0] // slots
    width, units = up.shape
    sizes = [ref.shape[0] for ref in shards]
    starts = [sum(sizes[:i]) for i in range(n)]

    def fetch(source, target, i):
        copy = pltpu.make_async_copy(source, target, sems.at[i])
        copy.start()
        return copy

    def shard(i):
        return fetch(shards[i], x.at[starts[i] : starts[i] + sizes[i]], i)

    x_in = [shard(0)]
    ups = [fetch(up, rise.at[:, :units], n), fetch(their_up, rise.at[:, units:], n + 1)]
    x_in += [shard(i) for i in range(1, n)]
    downs = [fetch(down, fall.at[:units], n + 2), fetch(their_down, fall.at[units:], n + 3)]

    def rows_of(s):
        return pl.ds(s * tokens if unrolled else pl.multiple_of(s * tokens, tokens), tokens)

    def each_slot(step):
        if unrolled:
            for s in range(slots):
                step(s, 0)
        else:
            lax.fori_loop(0, slots, step, 0)

    def ascend(s, carry):
        at = rows_of(s)
        for i in range(n):

            @pl.when(s == starts[i] // tokens)
            def _():
                x_in[i].wait()

        total = 0.0
        for c in range(2):

            @pl.when(s == 0)
            def _():
                ups[c].wait()

            lanes = slice(units * c, units * (c + 1))
            h = jax.nn.gelu(dot(x[at, :], rise[:, lanes]), approximate=True).astype(BF16)
            hidden[at, lanes] = h
            h_f = h.astype(F32)
            total = total + jnp.sum(h_f * h_f, axis=-1, keepdims=True)
        done[at, width : width + 128] = jnp.broadcast_to(total, (tokens, 128)).astype(BF16)
        return carry

    each_slot(ascend)
    for copy in downs:
        copy.wait()
    copies = []
    for s in range(slots):
        source = done.at[tokens * s : tokens * (s + 1)]
        copies.append(pltpu.make_async_copy(source, outs[s], out_sems.at[s]))

    def descend(s, carry):
        at = rows_of(s)
        done[at, 0:width] = dot(hidden[at, :], fall[...]).astype(BF16)
        for i in range(slots):

            @pl.when(s == i)
            def _():
                copies[i].start()

        return carry

    each_slot(descend)
    for copy in copies:
        copy.wait()


def feed_forward(shards, slots, up, their_up, down, their_down):
    n = len(shards)
    total = sum(v.shape[0] for v in shards)
    tokens, width = total // slots, shards[0].shape[1]
    units = 2 * up.shape[1]
    return pl.pallas_call(
        lambda *refs: forward_body(n, slots, slots == 4, *refs),
        in_specs=[ANY] * (n + 4),
        out_specs=[ANY] * slots,
        out_shape=[jax.ShapeDtypeStruct((tokens, width + 128), BF16)] * slots,
        scratch_shapes=[
            pltpu.VMEM((total, width), BF16),
            pltpu.VMEM((width, units), BF16),
            pltpu.VMEM((units, width), BF16),
            pltpu.VMEM((total, units), BF16),
            pltpu.VMEM((total, width + 128), BF16),
            pltpu.SemaphoreType.DMA((n + 4,)),
            pltpu.SemaphoreType.DMA((slots,)),
        ],
        cost_estimate=cost(4 * total * width * units, 4 * total * width + 4 * width * units),
        name="feed_forward",
    )(*shards, up, their_up, down, their_down)


def row_body(inv_root, hs, top_ref, qcol, kcol, *refs):
    cur, theirs, edges = refs[:2], refs[2:6], refs[6:10]
    accs, dens, above = refs[10:12], refs[12:14], refs[14:]
    r = pl.program_id(0)
    first = r == 0
    n = qcol.shape[0] // 2
    mask = kcol[...] <= qcol[...]
    closed = jnp.logical_and(first, top_ref[0] == 1)
    same_one = jnp.where(mask, 1.0, 0.0)
    prev_one = jnp.where(closed, 0.0, 1.0 - same_one).astype(BF16)
    same_one = same_one.astype(BF16)
    ones = jnp.ones((kcol.shape[1], hs), BF16)
    scale = inv_root * math.log2(math.e)

    @pl.when(first)
    def _():
        for keep, edge in zip(above, edges):
            keep[...] = edge[...].reshape(n, 4 * hs)

    now = [ref[:, :, 0, :, 2 * hs :].reshape(n, 4 * hs) for ref in cur]
    for i in range(2):
        pair = [ref[:, :, 0].reshape(n, 2 * hs) for ref in theirs[2 * i : 2 * i + 2]]
        now.append(jnp.concatenate(pair, axis=1))
    before = [ref[...] for ref in above]
    for h in range(2):
        at = slice(h * hs, (h + 1) * hs)
        q = jnp.concatenate([ref[:, :, 0, :, at].reshape(n, hs) for ref in cur], axis=0)

        def taken(parts, base):
            lanes = [base + hs * h] * 2 + [base + hs * (1 - h)] * 2
            return jnp.concatenate([p[:, m : m + hs] for p, m in zip(parts, lanes)], axis=0)

        scores = jnp.where(mask, dot_t(q, taken(now, 0)), dot_t(q, taken(before, 0))) * scale
        w = jnp.exp2(scores).astype(BF16)
        out = dot(w * same_one, jnp.concatenate([taken(now, 2 * hs), ones], axis=1))
        out = out + dot(w * prev_one, jnp.concatenate([taken(before, 2 * hs), ones], axis=1))
        shape = (4, 2, HALF, hs)
        for i in range(2):
            half = out[n * i : n * (i + 1)]
            accs[i][:, :, 0, :, at] = half[:, :hs].astype(BF16).reshape(shape)
            dens[i][:, :, 0, :, at] = half[:, hs:].reshape(shape)
    for keep, value in zip(above, now):
        keep[...] = value


def row_attention(top, qcol, kcol, qkv, their_qkv, edge, their_edge, hs, inv_root):
    rows = qkv[0].shape[2]
    now = pl.BlockSpec((4, 2, 1, HALF, 6 * hs), lambda r: (0, 0, r, 0, 0))
    keys = pl.BlockSpec((4, 2, 1, HALF, 2 * hs), lambda r: (0, 0, r, 0, 1))
    values = pl.BlockSpec((4, 2, 1, HALF, 2 * hs), lambda r: (0, 0, r, 0, 2))
    whole = lambda a: pl.BlockSpec(a.shape, lambda r: (0,) * a.ndim)
    out = lambda kind: jax.ShapeDtypeStruct((4, 2, rows, HALF, 2 * hs), kind)
    out_spec = pl.BlockSpec((4, 2, 1, HALF, 2 * hs), lambda r: (0, 0, r, 0, 0))
    n = qcol.shape[0]
    outs = pl.pallas_call(
        lambda *refs: row_body(inv_root, hs, *refs),
        grid=(rows,),
        in_specs=[SMEM, whole(qcol), whole(kcol), now, now, keys, values, keys, values]
        + [whole(e) for e in (*edge, *their_edge)],
        out_specs=[out_spec] * 4,
        out_shape=[out(BF16)] * 2 + [out(F32)] * 2,
        scratch_shapes=[pltpu.VMEM((n // 2, 4 * hs), BF16)] * 4,
        cost_estimate=cost(rows * 32 * n * n * hs, rows * 32 * n * hs, rows * 4 * n * n),
        name="row_attention",
    )(
        top, qcol, kcol, *qkv, their_qkv[0], their_qkv[0], their_qkv[1], their_qkv[1],
        *edge, *their_edge,
    )
    return outs[:2], outs[2:]


def col_body(inv_root, hs, own_rows, bias, their_bias, x, *refs):
    out = refs[-1]
    rows, cols, _ = x.shape
    chunk = 16
    spots = rows * cols
    step = chunk * cols
    log2e = math.log2(math.e)
    lane = lax.broadcasted_iota(jnp.int32, (step, 128), 1)
    spot = lax.broadcasted_iota(jnp.int32, (step, 128), 0) & (cols - 1)
    ones = jnp.ones((spots, hs), BF16)

    def part(at):
        return x[:, :, at * hs : (at + 1) * hs].reshape(spots, hs)

    den_rows = []
    for i in range(rows // chunk):
        n = step * (i + 1)
        qi = lax.broadcasted_iota(jnp.int32, (step, n), 0) + step * i
        ki = lax.broadcasted_iota(jnp.int32, (step, n), 1)
        keep = jnp.logical_and(((qi - ki) & (cols - 1)) == 0, ki < qi)
        laid_out = 0.0
        for h in range(2):
            q, k, v = part(h), part(2 + h), part(4 + h)
            s = dot_t(q[step * i : n], k[:n]) * (inv_root * log2e)
            s = s + (bias, their_bias)[h][0] * log2e
            w = jnp.where(keep, jnp.exp2(s), 0.0).astype(BF16)
            a = dot(w, jnp.concatenate([v[:n], ones[:n]], axis=1))
            laid_out = laid_out + jnp.where(lane == spot + cols * h, a[:, hs:], 0.0)
            a = a[:, :hs].astype(BF16).reshape(chunk, cols, hs)
            for j in range(chunk):
                r = chunk * i + j
                out[r // own_rows, 0, r % own_rows, :, h * hs : (h + 1) * hs] = a[j]
        den_rows.append(jnp.sum(laid_out.reshape(chunk, cols, 128), axis=1))
    den_rows = jnp.concatenate(den_rows, axis=0)
    fill = jnp.zeros((cols - own_rows, 128), F32)
    for b in range(rows // own_rows):
        block = jnp.concatenate([den_rows[own_rows * b : own_rows * (b + 1)], fill], axis=0)
        out[b, 0, own_rows, :, 0:128] = block.astype(BF16)
        out[b, 0, own_rows, :, 128:256] = jnp.zeros((cols, 128), BF16)


def column_attention(group, bias, x, own_rows, hs, inv_root, earlier=()):
    rows, cols, _ = x.shape
    spots = rows * cols
    peers = rows // own_rows
    return pl.pallas_call(
        lambda *refs: col_body(inv_root, hs, own_rows, *refs),
        grid=(1,),
        in_specs=[SMEM, SMEM, pl.BlockSpec(x.shape, lambda i: (0, 0, 0))]
        + [pl.BlockSpec(memory_space=pl.ANY)] * len(earlier),
        out_specs=pl.BlockSpec(
            (peers, 1, own_rows + 1, cols, 2 * hs), lambda i: (0, group, 0, 0, 0)
        ),
        out_shape=jax.ShapeDtypeStruct((peers, 2, own_rows + 1, cols, 2 * hs), BF16),
        input_output_aliases={3: 0} if earlier else {},
        cost_estimate=cost(6 * spots * spots * hs, 16 * spots * hs, 2 * spots * spots),
        name="column_attention",
    )(*bias, x, *earlier)


def term_body(hs, rows, splits, got, acc, den, *refs):
    count = len({slot for slot, _, _ in splits})
    ffs, (w_mine, w_their), outs = refs[:count], refs[count : count + 2], refs[count + 2 :]
    spots = 2 * count * rows * HALF
    lines = 2 * count * HALF
    unit = lax.broadcasted_iota(jnp.int32, (spots, lines), 0) // HALF
    line = lax.broadcasted_iota(jnp.int32, (spots, lines), 1)
    hit = jnp.logical_and(unit == (line // HALF) * rows + line % HALF, line % HALF < rows)
    table = got[:, 0, rows, :, 0:128].reshape(lines, 128)
    table = dot(jnp.where(hit, 1.0, 0.0).astype(BF16), table)
    lane = lax.broadcasted_iota(jnp.int32, (spots, 128), 1)
    spot = lax.broadcasted_iota(jnp.int32, (spots, 128), 0) % HALF
    ones = jnp.ones((128, 128), BF16)
    parts = []
    for h in range(2):
        at = slice(h * hs, (h + 1) * hs)
        col_den = dot(jnp.where(lane == spot + HALF * h, table, 0.0).astype(BF16), ones)
        total = acc[:, :, :, :, at].reshape(spots, hs).astype(F32)
        total = total + got[:, 0, 0:rows, :, at].reshape(spots, hs).astype(F32)
        parts.append((total / (den[:, :, :, :, at].reshape(spots, hs) + col_den)).astype(BF16))
    halves = jnp.concatenate(parts, axis=1).reshape(count, 2, rows, HALF, 2 * hs)
    blocks = [halves[s, g, r] for s in range(count) for r in range(rows) for g in range(2)]
    attended = jnp.concatenate(blocks, axis=0)
    att_f = attended.astype(F32)
    squares = jnp.sum(att_f * att_f, axis=-1, keepdims=True)
    weight = jnp.concatenate([w_mine[...], w_their[...]], axis=0)
    term = dot(attended, weight).astype(BF16)
    width = term.shape[1]
    for out, (slot, low, high) in zip(outs, splits):
        f = ffs[slot]
        tokens = f.shape[0]
        at = slice(tokens * slot + low, tokens * slot + high)
        out[:, 0:width] = f[low:high, 0:width] + term[at]
        out[:, width:] = (f[low:high, width:].astype(F32) + squares[at]).astype(BF16)


def terms(group, base, got, acc, den, ff, w_mine, w_their, hs, rows, splits):
    tokens, full = ff[0].shape
    count = len(ff)
    whole = lambda a: pl.BlockSpec(a.shape, lambda i: (0,) * a.ndim)
    local = pl.BlockSpec((count, 2, rows, HALF, 2 * hs), lambda i: (base // count, 0, 0, 0, 0))
    return pl.pallas_call(
        lambda *refs: term_body(hs, rows, splits, *refs),
        grid=(1,),
        in_specs=[
            pl.BlockSpec(
                (2 * count, 1, rows + 1, HALF, 2 * hs), lambda i: (base // count, group, 0, 0, 0)
            ),
            local,
            local,
        ]
        + [whole(a) for a in (*ff, w_mine, w_their)],
        out_specs=[pl.BlockSpec((b - a, full), lambda i: (0, 0)) for _, a, b in splits],
        out_shape=[jax.ShapeDtypeStruct((b - a, full), BF16) for _, a, b in splits],
        cost_estimate=cost(4 * count * tokens * hs * full, 5 * count * tokens * full),
        name="terms",
    )(got, acc, den, *ff, w_mine, w_their)


def thirds_body(t0, t1, t2, o0, o1, o2):
    o0[...] = t0[...]
    o1[...] = t1[...]
    o2[...] = t2[...]


def thirds_of(arrays):
    rows, width = arrays[0].shape
    third = rows // 3
    block = lambda at: pl.BlockSpec((third, width), lambda i: (at, 0))
    return pl.pallas_call(
        thirds_body,
        grid=(1,),
        in_specs=[block(0), block(1), block(2)],
        out_specs=[block(0)] * 3,
        out_shape=[jax.ShapeDtypeStruct((third, width), BF16)] * 3,
        cost_estimate=cost(0, 4 * rows * width),
        name="thirds",
    )(*arrays)


def far_body(t0, t1, t2, g0, g1, g2, o0, o1, o2):
    for t, g, o in ((t0, g0, o0), (t1, g1, o1), (t2, g2, o2)):
        o[...] = t[...] + g[...]


def add_far(arrays, parts):
    third, width = parts[0].shape
    block = lambda at: pl.BlockSpec((third, width), lambda i: (at, 0))
    spread = [block(0), block(1), block(2)]
    return pl.pallas_call(
        far_body,
        grid=(1,),
        in_specs=spread + [block(0)] * 3,
        out_specs=spread,
        out_shape=[jax.ShapeDtypeStruct(arrays[0].shape, BF16)] * 3,
        input_output_aliases={0: 0, 1: 1, 2: 2},
        cost_estimate=cost(6 * third * width, 18 * third * width),
        name="add_far",
    )(*arrays, *parts)


def near_body(t0, t1, r0, r1, r2, o0, o1):
    o0[...] = t0[...] + (r0[...] + r1[...])
    o1[...] = t1[...] + r2[...]


def add_near(*arrays):
    rows, width = arrays[0].shape
    return pl.pallas_call(
        near_body,
        in_specs=[VMEM] * 5,
        out_specs=[VMEM] * 2,
        out_shape=[jax.ShapeDtypeStruct((rows, width), BF16)] * 2,
        cost_estimate=cost(3 * rows * width, 14 * rows * width),
        name="add_near",
    )(*arrays)


def head_body(x, mine, m0, m1, m2, targets, gain, weight, layer_out, line):
    width = x.shape[1]
    mixed, spread = 0.0, 0.0
    for m in (mine, m0, m1, m2):
        mixed = mixed + m[:, :width].astype(F32)
        spread = spread + m[:, width : width + 1].astype(F32)
    lo = (x[...].astype(F32) + mixed).astype(BF16)
    layer_out[...] = lo
    back = lo.astype(F32)
    inv_norm = lax.rsqrt(jnp.sum(back * back, axis=-1, keepdims=True) / width + EPS)
    head_in = (back * inv_norm * gain[...]).astype(BF16)
    raised = jnp.exp(dot(head_in, weight[...]))
    prob = raised / jnp.sum(raised, axis=-1, keepdims=True)
    levels = lax.broadcasted_iota(jnp.int32, prob.shape, 1)
    grad = prob - jnp.where(levels == targets[...], 1.0, 0.0)
    scaled = gain[...] * dot_t(grad.astype(BF16), weight[...])
    lean = jnp.sum(back * scaled, axis=-1, keepdims=True) / width
    layer_grad = inv_norm * scaled - back * (inv_norm * inv_norm * inv_norm) * lean
    head_f = head_in.astype(F32)
    out_sq = jnp.sum(head_f * head_f, axis=-1, keepdims=True) * jnp.sum(
        grad * grad, axis=-1, keepdims=True
    )
    layer_sq = jnp.sum(layer_grad * layer_grad, axis=-1, keepdims=True)
    norm = jnp.sqrt(laid(out_sq + spread * layer_sq))
    line[...] = jnp.broadcast_to(norm[None], line.shape)


def head(x, mine, m0, m1, m2, targets, gain, weight, devices):
    return pl.pallas_call(
        head_body,
        in_specs=[VMEM] * 8,
        out_specs=[pl.BlockSpec(memory_space=pltpu.VMEM)] * 2,
        out_shape=[
            jax.ShapeDtypeStruct(x.shape, BF16),
            jax.ShapeDtypeStruct((devices, 1, 256), F32),
        ],
        name="head",
    )(x, mine, m0, m1, m2, targets, gain, weight)


def pick_body(table, where, spot, out):
    devices = table.shape[0]
    count = where.shape[1]
    hit = lax.broadcasted_iota(jnp.int32, (devices, count), 0) == where[...]
    hot = jnp.where(hit, 1.0, 0.0).astype(BF16)

    full = table[...]
    high = full.astype(BF16)
    rest = full - high.astype(F32)
    mid = rest.astype(BF16)
    low = (rest - mid.astype(F32)).astype(BF16)
    parts = jnp.concatenate([high, mid, low], axis=0)
    lines = lax.dot_general(
        parts,
        jnp.concatenate([hot, hot, hot], axis=0),
        (((0,), (0,)), ((), ())),
        preferred_element_type=F32,
    )
    mine = lax.broadcasted_iota(jnp.int32, lines.shape, 0) == spot[...]
    picked = jnp.sum(jnp.where(mine, lines, 0.0), axis=0, keepdims=True)
    out[...] = count * picked / jnp.sum(picked, axis=-1, keepdims=True)


def pick(table, where, spot):
    return pl.pallas_call(
        pick_body,
        in_specs=[pl.BlockSpec(memory_space=pltpu.VMEM)] * 3,
        out_specs=pl.BlockSpec(memory_space=pltpu.VMEM),
        out_shape=jax.ShapeDtypeStruct(where.shape, F32),
        name="pick",
    )(table, where, spot)


def per_device(
    activations,
    targets,
    candidates,
    mix_gain,
    project_weight,
    output_weight,
    up_weight,
    down_weight,
    pattern_bias,
    head_gain,
    head_weight,
):
    rows, cols, width = activations.shape
    hs = project_weight.shape[2]
    tokens = rows * cols
    row_peers = lax.axis_size(ROW)
    inv_root = 1.0 / math.sqrt(hs)
    third = tokens // 3

    devices = lax.axis_size(ALL)

    their_project = swap_core(project_weight)
    their_up = swap_core(up_weight)
    their_down = swap_core(down_weight)
    their_output = swap_core(output_weight)
    bias = (pattern_bias, swap_core(pattern_bias))

    x = activations.reshape(tokens, width)
    own = normalize(x, mix_gain[None, :])

    def after(first, values):
        return lax.optimization_barrier((first, values))[1]

    def ffn(shards, slots):
        return feed_forward(shards, slots, up_weight, their_up, down_weight, their_down)

    near = (up_z(own), down_z(own), swap_x(own))
    (ff_own,) = ffn((own,), 1)
    s_a, s_b, s_p = after((ff_own, their_project), near)
    s_aa, s_pb, s_pa = up_z(s_a), down_z(s_p), swap_x(s_a)

    def columns(shards):
        qkv, edge = project(shards, project_weight, their_project, rows)
        got = lax.all_to_all(
            qkv.reshape(row_peers, rows * HALF, 6 * hs), ROW, split_axis=0, concat_axis=0, tiled=True
        )
        return qkv, edge, got

    def attend_columns(group, got, *earlier):
        x = got.reshape(row_peers * rows, HALF, 6 * hs)
        return column_attention(group, bias, x, rows, hs, inv_root, earlier)

    qkv0, edge0, got0 = columns((own, s_a, s_b, s_p))
    edge0 = next_row(edge0)
    their_edge0 = swap_core(edge0)
    their_qkv0 = swap_core(qkv0)
    s_aa, s_pa, s_pb = after(qkv0, (s_aa, s_pa, s_pb))
    h_aa, h_pa, h_pb = thirds_of((s_aa, s_pa, s_pb))
    far = (swap_x(h_aa), up_z(h_pa), down_z(h_pb))
    away = after(their_qkv0, (s_aa, s_pa, s_pb, *far))
    qkv1, edge1, got1 = columns(away)
    back = attend_columns(0, after(qkv1, got0))
    their_qkv1 = swap_core(qkv1)
    edge1 = next_row(edge1)
    their_edge1 = swap_core(edge1)
    ff1 = ffn(after((qkv1, back), away), 4)
    back = attend_columns(1, after((ff1, their_qkv1), got1), back)
    again = lax.all_to_all(back, ROW, split_axis=0, concat_axis=0, tiled=True)

    xl, z, core = lax.axis_index(XL), lax.axis_index(Z), lax.axis_index(CORE)
    n_z = lax.axis_size(Z)
    shift_x = jnp.array([0, 0, 0, 1, 0, 1, 1, 1], jnp.int32)
    shift_z = jnp.array([0, 3, 1, 0, 2, 3, 1, 2], jnp.int32)
    chip = ((xl + shift_x) % 2) * n_z + (z + shift_z) % n_z
    starts = chip * 2 * cols
    offs = jnp.arange(cols, dtype=jnp.int32)
    mine = (starts[:, None] + core * cols + offs[None, :]).reshape(-1)
    theirs = (starts[:, None] + (1 - core) * cols + offs[None, :]).reshape(-1)
    top = (lax.axis_index(ROW) == 0).astype(jnp.int32)[None]
    acc, den = row_attention(
        after(back, top),
        mine[:, None],
        jnp.concatenate([mine, theirs])[None, :],
        (qkv0, qkv1),
        (their_qkv0, their_qkv1),
        (edge0, edge1),
        (their_edge0, their_edge1),
        hs,
        inv_root,
    )
    f0, f1, f2 = terms(
        1, 3, again, acc[1], den[1], ff1[3:], output_weight, their_output, hs, rows,
        [(0, third * i, third * (i + 1)) for i in range(3)],
    )
    g0, g1, g2 = swap_x(f0), down_z(f1), up_z(f2)
    t_aa, t_pa, t_pb = terms(
        1, 0, *after(f0, (again, acc[1], den[1])), ff1[:3], output_weight, their_output, hs, rows,
        [(i, 0, tokens) for i in range(3)],
    )

    t_aa, t_pa, t_pb = add_far((t_aa, t_pa, t_pb), (g0, g1, g2))
    r_aa, r_pa, r_pb = down_z(t_aa), swap_x(t_pa), up_z(t_pb)
    ff0 = ffn(after(t_pb, (s_a, s_b, s_p)), 3)
    t_own, t_a, t_b, t_p = terms(
        0, 0, again, acc[0], den[0], (ff_own, *ff0), output_weight, their_output, hs, rows,
        [(i, 0, tokens) for i in range(4)],
    )
    from_b = up_z(t_b)
    t_a, t_p = add_near(t_a, t_p, r_aa, r_pa, r_pb)
    from_a, from_p = down_z(t_a), swap_x(t_p)

    layer_out, line = head(
        x,
        t_own,
        from_a,
        from_b,
        from_p,
        targets.reshape(tokens, 1),
        head_gain[None, :],
        head_weight,
        devices,
    )
    table = lax.all_to_all(
        line,
        ALL,
        split_axis=0,
        concat_axis=0,
        tiled=True,
    ).reshape(devices, 256)
    full_cols = cols * lax.axis_size(COL)
    c_row, c_col = candidates // full_cols, candidates % full_cols
    where = (c_row // rows) * lax.axis_size(COL) + c_col // cols
    spot = (c_row % rows) * cols + c_col % cols
    chosen = pick(table, where[None, :], spot[None, :])
    return (layer_out.reshape(rows, cols, width), chosen.reshape(-1))


def solution(mesh):
    split = Mesh(mesh.devices.reshape(2, 4, 2, 4, 2), ("row_0", "row_1", "col_0", "col_1", "col_2"))

    return jax.shard_map(
        per_device,
        mesh=split,
        in_specs=(
            P(ROW, COL, None),
            P(ROW, COL),
            P(),
            P(),
            P(None, None, COL),
            P(COL, None),
            P(None, COL),
            P(COL, None),
            P(COL),
            P(),
            P(),
        ),
        out_specs=(P(ROW, COL, None), P()),
        check_vma=False,
    )
```

```python
import math

import jax
import jax.numpy as jnp
from jax import lax
from jax.experimental import pallas as pl
from jax.experimental.pallas import tpu as pltpu
from jax.sharding import Mesh
from jax.sharding import PartitionSpec as P

COL = ("col_0", "col_1", "col_2")
ROW = ("row_0", "row_1")
ALL = ("row_0", "row_1", "col_0", "col_1", "col_2")
XL, Z, CORE = COL

EPS = 1e-06
F32 = jnp.float32
BF16 = jnp.bfloat16


def permuted(array, axis, by):
    n = lax.axis_size(axis)
    return lax.ppermute(array, axis, [(i, (i + by) % n) for i in range(n)])


def up_z(array):
    return permuted(array, Z, 1)


def down_z(array):
    return permuted(array, Z, -1)


def swap_x(array):
    return permuted(array, XL, 1)


def swap_core(array):
    return permuted(array, CORE, 1)


def next_row(array):
    n = lax.axis_size(ROW)
    return lax.ppermute(array, ROW, [(i, i + 1) for i in range(n - 1)])


def dot(a, b):
    return jnp.dot(a, b, preferred_element_type=F32)


def dot_t(a, b):
    return lax.dot_general(a, b, (((1,), (1,)), ((), ())), preferred_element_type=F32)


def cost(flops, bytes_accessed, exps=0):
    return pl.CostEstimate(flops=flops, bytes_accessed=bytes_accessed, transcendentals=exps)


VMEM = pl.BlockSpec(memory_space=pltpu.VMEM)
SMEM = pl.BlockSpec(memory_space=pltpu.SMEM)
ANY = pl.BlockSpec(memory_space=pl.ANY)
HALF = 16


def laid(column, lanes=256):
    shape = (column.shape[0], lanes)
    hit = lax.broadcasted_iota(jnp.int32, shape, 1) == lax.broadcasted_iota(jnp.int32, shape, 0)
    return jnp.sum(jnp.where(hit, column, 0.0), axis=0, keepdims=True)


def norm_body(x, gain, out):
    v = x[...].astype(F32)
    scale = lax.rsqrt(jnp.sum(v * v, axis=-1, keepdims=True) / v.shape[1] + EPS)
    out[...] = (v * scale * gain[...]).astype(BF16)


def normalize(x, gain):
    return pl.pallas_call(
        norm_body,
        in_specs=[VMEM, VMEM],
        out_specs=VMEM,
        out_shape=jax.ShapeDtypeStruct(x.shape, BF16),
        cost_estimate=cost(5 * x.size, 4 * x.size),
        name="normalize",
    )(x, gain)


def stacked(refs):
    return jnp.concatenate([ref[...] for ref in refs], axis=0)


def project_body(rows, n, *refs):
    mine, theirs, out, edge = refs[n:]
    x = stacked(refs[:n])
    w = jnp.concatenate([mine[0], theirs[0]], axis=1)
    y = dot(x, w).astype(BF16).reshape(4, rows, 2, HALF, w.shape[1])
    for g in range(2):
        out[:, g] = y[:, :, g]
        edge[:, g] = y[:, rows - 1, g]


def project(shards, mine, theirs, rows):
    n = len(shards)
    total = sum(v.shape[0] for v in shards)
    _, width, hs = mine.shape
    whole = [pl.BlockSpec(v.shape, lambda j: (0, 0)) for v in shards]
    weight = pl.BlockSpec((1, width, hs), lambda j: (j, 0, 0))
    return pl.pallas_call(
        lambda *refs: project_body(rows, n, *refs),
        grid=(3,),
        in_specs=whole + [weight] * 2,
        out_specs=[
            pl.BlockSpec((4, 2, rows, HALF, 2 * hs), lambda j: (0, 0, 0, 0, j)),
            pl.BlockSpec((4, 2, HALF, 2 * hs), lambda j: (0, 0, 0, jnp.maximum(j - 1, 0))),
        ],
        out_shape=[
            jax.ShapeDtypeStruct((4, 2, rows, HALF, 6 * hs), BF16),
            jax.ShapeDtypeStruct((4, 2, HALF, 4 * hs), BF16),
        ],
        cost_estimate=cost(2 * total * width * 6 * hs, 2 * total * width + 12 * width * hs),
        name="project",
    )(*shards, mine, theirs)


def forward_body(n, slots, unrolled, *refs):
    shards, (up, their_up, down, their_down) = refs[:n], refs[n : n + 4]
    outs, (x, rise, fall, hidden, done, sems, out_sems) = refs[n + 4 : -7], refs[-7:]
    tokens = x.shape[0] // slots
    width, units = up.shape
    sizes = [ref.shape[0] for ref in shards]
    starts = [sum(sizes[:i]) for i in range(n)]

    def fetch(source, target, i):
        copy = pltpu.make_async_copy(source, target, sems.at[i])
        copy.start()
        return copy

    def shard(i):
        return fetch(shards[i], x.at[starts[i] : starts[i] + sizes[i]], i)

    x_in = [shard(0)]
    ups = [fetch(up, rise.at[:, :units], n), fetch(their_up, rise.at[:, units:], n + 1)]
    x_in += [shard(i) for i in range(1, n)]
    downs = [fetch(down, fall.at[:units], n + 2), fetch(their_down, fall.at[units:], n + 3)]

    def rows_of(s):
        return pl.ds(s * tokens if unrolled else pl.multiple_of(s * tokens, tokens), tokens)

    def each_slot(step):
        if unrolled:
            for s in range(slots):
                step(s, 0)
        else:
            lax.fori_loop(0, slots, step, 0)

    def ascend(s, carry):
        at = rows_of(s)
        for i in range(n):

            @pl.when(s == starts[i] // tokens)
            def _():
                x_in[i].wait()

        total = 0.0
        for c in range(2):

            @pl.when(s == 0)
            def _():
                ups[c].wait()

            lanes = slice(units * c, units * (c + 1))
            h = jax.nn.gelu(dot(x[at, :], rise[:, lanes]), approximate=True).astype(BF16)
            hidden[at, lanes] = h
            h_f = h.astype(F32)
            total = total + jnp.sum(h_f * h_f, axis=-1, keepdims=True)
        done[at, width : width + 128] = jnp.broadcast_to(total, (tokens, 128)).astype(BF16)
        return carry

    each_slot(ascend)
    for copy in downs:
        copy.wait()
    copies = []
    for s in range(slots):
        source = done.at[tokens * s : tokens * (s + 1)]
        copies.append(pltpu.make_async_copy(source, outs[s], out_sems.at[s]))

    def descend(s, carry):
        at = rows_of(s)
        done[at, 0:width] = dot(hidden[at, :], fall[...]).astype(BF16)
        for i in range(slots):

            @pl.when(s == i)
            def _():
                copies[i].start()

        return carry

    each_slot(descend)
    for copy in copies:
        copy.wait()


def feed_forward(shards, slots, up, their_up, down, their_down):
    n = len(shards)
    total = sum(v.shape[0] for v in shards)
    tokens, width = total // slots, shards[0].shape[1]
    units = 2 * up.shape[1]
    return pl.pallas_call(
        lambda *refs: forward_body(n, slots, slots == 4, *refs),
        in_specs=[ANY] * (n + 4),
        out_specs=[ANY] * slots,
        out_shape=[jax.ShapeDtypeStruct((tokens, width + 128), BF16)] * slots,
        scratch_shapes=[
            pltpu.VMEM((total, width), BF16),
            pltpu.VMEM((width, units), BF16),
            pltpu.VMEM((units, width), BF16),
            pltpu.VMEM((total, units), BF16),
            pltpu.VMEM((total, width + 128), BF16),
            pltpu.SemaphoreType.DMA((n + 4,)),
            pltpu.SemaphoreType.DMA((slots,)),
        ],
        cost_estimate=cost(4 * total * width * units, 4 * total * width + 4 * width * units),
        name="feed_forward",
    )(*shards, up, their_up, down, their_down)


def row_body(inv_root, hs, top_ref, qcol, kcol, *refs):
    cur, theirs, edges = refs[:2], refs[2:6], refs[6:10]
    accs, dens, above = refs[10:12], refs[12:14], refs[14:]
    r = pl.program_id(0)
    first = r == 0
    n = qcol.shape[0] // 2
    mask = kcol[...] <= qcol[...]
    closed = jnp.logical_and(first, top_ref[0] == 1)
    same_one = jnp.where(mask, 1.0, 0.0)
    prev_one = jnp.where(closed, 0.0, 1.0 - same_one).astype(BF16)
    same_one = same_one.astype(BF16)
    ones = jnp.ones((kcol.shape[1], hs), BF16)
    scale = inv_root * math.log2(math.e)

    @pl.when(first)
    def _():
        for keep, edge in zip(above, edges):
            keep[...] = edge[...].reshape(n, 4 * hs)

    now = [ref[:, :, 0, :, 2 * hs :].reshape(n, 4 * hs) for ref in cur]
    for i in range(2):
        pair = [ref[:, :, 0].reshape(n, 2 * hs) for ref in theirs[2 * i : 2 * i + 2]]
        now.append(jnp.concatenate(pair, axis=1))
    before = [ref[...] for ref in above]
    for h in range(2):
        at = slice(h * hs, (h + 1) * hs)
        q = jnp.concatenate([ref[:, :, 0, :, at].reshape(n, hs) for ref in cur], axis=0)

        def taken(parts, base):
            lanes = [base + hs * h] * 2 + [base + hs * (1 - h)] * 2
            return jnp.concatenate([p[:, m : m + hs] for p, m in zip(parts, lanes)], axis=0)

        scores = jnp.where(mask, dot_t(q, taken(now, 0)), dot_t(q, taken(before, 0))) * scale
        w = jnp.exp2(scores).astype(BF16)
        out = dot(w * same_one, jnp.concatenate([taken(now, 2 * hs), ones], axis=1))
        out = out + dot(w * prev_one, jnp.concatenate([taken(before, 2 * hs), ones], axis=1))
        shape = (4, 2, HALF, hs)
        for i in range(2):
            half = out[n * i : n * (i + 1)]
            accs[i][:, :, 0, :, at] = half[:, :hs].astype(BF16).reshape(shape)
            dens[i][:, :, 0, :, at] = half[:, hs:].reshape(shape)
    for keep, value in zip(above, now):
        keep[...] = value


def row_attention(top, qcol, kcol, qkv, their_qkv, edge, their_edge, hs, inv_root):
    rows = qkv[0].shape[2]
    now = pl.BlockSpec((4, 2, 1, HALF, 6 * hs), lambda r: (0, 0, r, 0, 0))
    keys = pl.BlockSpec((4, 2, 1, HALF, 2 * hs), lambda r: (0, 0, r, 0, 1))
    values = pl.BlockSpec((4, 2, 1, HALF, 2 * hs), lambda r: (0, 0, r, 0, 2))
    whole = lambda a: pl.BlockSpec(a.shape, lambda r: (0,) * a.ndim)
    out = lambda kind: jax.ShapeDtypeStruct((4, 2, rows, HALF, 2 * hs), kind)
    out_spec = pl.BlockSpec((4, 2, 1, HALF, 2 * hs), lambda r: (0, 0, r, 0, 0))
    n = qcol.shape[0]
    outs = pl.pallas_call(
        lambda *refs: row_body(inv_root, hs, *refs),
        grid=(rows,),
        in_specs=[SMEM, whole(qcol), whole(kcol), now, now, keys, values, keys, values]
        + [whole(e) for e in (*edge, *their_edge)],
        out_specs=[out_spec] * 4,
        out_shape=[out(BF16)] * 2 + [out(F32)] * 2,
        scratch_shapes=[pltpu.VMEM((n // 2, 4 * hs), BF16)] * 4,
        cost_estimate=cost(rows * 32 * n * n * hs, rows * 32 * n * hs, rows * 4 * n * n),
        name="row_attention",
    )(
        top, qcol, kcol, *qkv, their_qkv[0], their_qkv[0], their_qkv[1], their_qkv[1],
        *edge, *their_edge,
    )
    return outs[:2], outs[2:]


def col_body(inv_root, hs, own_rows, bias, their_bias, x, *refs):
    out = refs[-1]
    rows, cols, _ = x.shape
    chunk = 16
    spots = rows * cols
    step = chunk * cols
    log2e = math.log2(math.e)
    lane = lax.broadcasted_iota(jnp.int32, (step, 128), 1)
    spot = lax.broadcasted_iota(jnp.int32, (step, 128), 0) & (cols - 1)
    ones = jnp.ones((spots, hs), BF16)

    def part(at):
        return x[:, :, at * hs : (at + 1) * hs].reshape(spots, hs)

    den_rows = []
    for i in range(rows // chunk):
        n = step * (i + 1)
        qi = lax.broadcasted_iota(jnp.int32, (step, n), 0) + step * i
        ki = lax.broadcasted_iota(jnp.int32, (step, n), 1)
        keep = jnp.logical_and(((qi - ki) & (cols - 1)) == 0, ki < qi)
        laid_out = 0.0
        for h in range(2):
            q, k, v = part(h), part(2 + h), part(4 + h)
            s = dot_t(q[step * i : n], k[:n]) * (inv_root * log2e)
            s = s + (bias, their_bias)[h][0] * log2e
            w = jnp.where(keep, jnp.exp2(s), 0.0).astype(BF16)
            a = dot(w, jnp.concatenate([v[:n], ones[:n]], axis=1))
            laid_out = laid_out + jnp.where(lane == spot + cols * h, a[:, hs:], 0.0)
            a = a[:, :hs].astype(BF16).reshape(chunk, cols, hs)
            for j in range(chunk):
                r = chunk * i + j
                out[r // own_rows, 0, r % own_rows, :, h * hs : (h + 1) * hs] = a[j]
        den_rows.append(jnp.sum(laid_out.reshape(chunk, cols, 128), axis=1))
    den_rows = jnp.concatenate(den_rows, axis=0)
    fill = jnp.zeros((cols - own_rows, 128), F32)
    for b in range(rows // own_rows):
        block = jnp.concatenate([den_rows[own_rows * b : own_rows * (b + 1)], fill], axis=0)
        out[b, 0, own_rows, :, 0:128] = block.astype(BF16)
        out[b, 0, own_rows, :, 128:256] = jnp.zeros((cols, 128), BF16)


def column_attention(group, bias, x, own_rows, hs, inv_root, earlier=()):
    rows, cols, _ = x.shape
    spots = rows * cols
    peers = rows // own_rows
    return pl.pallas_call(
        lambda *refs: col_body(inv_root, hs, own_rows, *refs),
        grid=(1,),
        in_specs=[SMEM, SMEM, pl.BlockSpec(x.shape, lambda i: (0, 0, 0))]
        + [pl.BlockSpec(memory_space=pl.ANY)] * len(earlier),
        out_specs=pl.BlockSpec(
            (peers, 1, own_rows + 1, cols, 2 * hs), lambda i: (0, group, 0, 0, 0)
        ),
        out_shape=jax.ShapeDtypeStruct((peers, 2, own_rows + 1, cols, 2 * hs), BF16),
        input_output_aliases={3: 0} if earlier else {},
        cost_estimate=cost(6 * spots * spots * hs, 16 * spots * hs, 2 * spots * spots),
        name="column_attention",
    )(*bias, x, *earlier)


def term_body(hs, rows, splits, got, acc, den, *refs):
    count = len({slot for slot, _, _ in splits})
    ffs, (w_mine, w_their), outs = refs[:count], refs[count : count + 2], refs[count + 2 :]
    spots = 2 * count * rows * HALF
    lines = 2 * count * HALF
    unit = lax.broadcasted_iota(jnp.int32, (spots, lines), 0) // HALF
    line = lax.broadcasted_iota(jnp.int32, (spots, lines), 1)
    hit = jnp.logical_and(unit == (line // HALF) * rows + line % HALF, line % HALF < rows)
    table = got[:, 0, rows, :, 0:128].reshape(lines, 128)
    table = dot(jnp.where(hit, 1.0, 0.0).astype(BF16), table)
    lane = lax.broadcasted_iota(jnp.int32, (spots, 128), 1)
    spot = lax.broadcasted_iota(jnp.int32, (spots, 128), 0) % HALF
    ones = jnp.ones((128, 128), BF16)
    parts = []
    for h in range(2):
        at = slice(h * hs, (h + 1) * hs)
        col_den = dot(jnp.where(lane == spot + HALF * h, table, 0.0).astype(BF16), ones)
        total = acc[:, :, :, :, at].reshape(spots, hs).astype(F32)
        total = total + got[:, 0, 0:rows, :, at].reshape(spots, hs).astype(F32)
        parts.append((total / (den[:, :, :, :, at].reshape(spots, hs) + col_den)).astype(BF16))
    halves = jnp.concatenate(parts, axis=1).reshape(count, 2, rows, HALF, 2 * hs)
    blocks = [halves[s, g, r] for s in range(count) for r in range(rows) for g in range(2)]
    attended = jnp.concatenate(blocks, axis=0)
    att_f = attended.astype(F32)
    squares = jnp.sum(att_f * att_f, axis=-1, keepdims=True)
    weight = jnp.concatenate([w_mine[...], w_their[...]], axis=0)
    term = dot(attended, weight).astype(BF16)
    width = term.shape[1]
    for out, (slot, low, high) in zip(outs, splits):
        f = ffs[slot]
        tokens = f.shape[0]
        at = slice(tokens * slot + low, tokens * slot + high)
        out[:, 0:width] = f[low:high, 0:width] + term[at]
        out[:, width:] = (f[low:high, width:].astype(F32) + squares[at]).astype(BF16)


def terms(group, base, got, acc, den, ff, w_mine, w_their, hs, rows, splits):
    tokens, full = ff[0].shape
    count = len(ff)
    whole = lambda a: pl.BlockSpec(a.shape, lambda i: (0,) * a.ndim)
    local = pl.BlockSpec((count, 2, rows, HALF, 2 * hs), lambda i: (base // count, 0, 0, 0, 0))
    return pl.pallas_call(
        lambda *refs: term_body(hs, rows, splits, *refs),
        grid=(1,),
        in_specs=[
            pl.BlockSpec(
                (2 * count, 1, rows + 1, HALF, 2 * hs), lambda i: (base // count, group, 0, 0, 0)
            ),
            local,
            local,
        ]
        + [whole(a) for a in (*ff, w_mine, w_their)],
        out_specs=[pl.BlockSpec((b - a, full), lambda i: (0, 0)) for _, a, b in splits],
        out_shape=[jax.ShapeDtypeStruct((b - a, full), BF16) for _, a, b in splits],
        cost_estimate=cost(4 * count * tokens * hs * full, 5 * count * tokens * full),
        name="terms",
    )(got, acc, den, *ff, w_mine, w_their)


def halves_body(t0, t1, o0, o1):
    o0[...] = t0[...]
    o1[...] = t1[...]


def halves_of(first, second):
    rows, width = first.shape
    block = lambda at: pl.BlockSpec((rows // 2, width), lambda i: (at, 0))
    return pl.pallas_call(
        halves_body,
        grid=(1,),
        in_specs=[block(0), block(1)],
        out_specs=[block(0)] * 2,
        out_shape=[jax.ShapeDtypeStruct((rows // 2, width), BF16)] * 2,
        cost_estimate=cost(0, 4 * rows * width),
        name="halves",
    )(first, second)


def far_body(t0, t1, t2, g0, g1, g2, o0, o1, o2):
    for t, g, o in ((t0, g0, o0), (t1, g1, o1), (t2, g2, o2)):
        o[...] = t[...] + g[...]


def add_far(arrays, parts):
    third, width = parts[0].shape
    block = lambda at: pl.BlockSpec((third, width), lambda i: (at, 0))
    spread = [block(0), block(1), block(2)]
    return pl.pallas_call(
        far_body,
        grid=(1,),
        in_specs=spread + [block(0)] * 3,
        out_specs=spread,
        out_shape=[jax.ShapeDtypeStruct(arrays[0].shape, BF16)] * 3,
        input_output_aliases={0: 0, 1: 1, 2: 2},
        cost_estimate=cost(6 * third * width, 18 * third * width),
        name="add_far",
    )(*arrays, *parts)


def near_body(t0, t1, r0, r1, r2, o0, o1):
    o0[...] = t0[...] + (r0[...] + r1[...])
    o1[...] = t1[...] + r2[...]


def add_near(*arrays):
    rows, width = arrays[0].shape
    return pl.pallas_call(
        near_body,
        in_specs=[VMEM] * 5,
        out_specs=[VMEM] * 2,
        out_shape=[jax.ShapeDtypeStruct((rows, width), BF16)] * 2,
        cost_estimate=cost(3 * rows * width, 14 * rows * width),
        name="add_near",
    )(*arrays)


def head_body(x, mine, m0, m1, m2, targets, gain, weight, layer_out, line):
    width = x.shape[1]
    mixed, spread = 0.0, 0.0
    for m in (mine, m0, m1, m2):
        mixed = mixed + m[:, :width].astype(F32)
        spread = spread + m[:, width : width + 1].astype(F32)
    lo = (x[...].astype(F32) + mixed).astype(BF16)
    layer_out[...] = lo
    back = lo.astype(F32)
    inv_norm = lax.rsqrt(jnp.sum(back * back, axis=-1, keepdims=True) / width + EPS)
    head_in = (back * inv_norm * gain[...]).astype(BF16)
    raised = jnp.exp(dot(head_in, weight[...]))
    prob = raised / jnp.sum(raised, axis=-1, keepdims=True)
    levels = lax.broadcasted_iota(jnp.int32, prob.shape, 1)
    grad = prob - jnp.where(levels == targets[...], 1.0, 0.0)
    scaled = gain[...] * dot_t(grad.astype(BF16), weight[...])
    lean = jnp.sum(back * scaled, axis=-1, keepdims=True) / width
    layer_grad = inv_norm * scaled - back * (inv_norm * inv_norm * inv_norm) * lean
    head_f = head_in.astype(F32)
    out_sq = jnp.sum(head_f * head_f, axis=-1, keepdims=True) * jnp.sum(
        grad * grad, axis=-1, keepdims=True
    )
    layer_sq = jnp.sum(layer_grad * layer_grad, axis=-1, keepdims=True)
    norm = jnp.sqrt(laid(out_sq + spread * layer_sq))
    line[...] = jnp.broadcast_to(norm[None], line.shape)


def head(x, mine, m0, m1, m2, targets, gain, weight, devices):
    return pl.pallas_call(
        head_body,
        in_specs=[VMEM] * 8,
        out_specs=[pl.BlockSpec(memory_space=pltpu.VMEM)] * 2,
        out_shape=[
            jax.ShapeDtypeStruct(x.shape, BF16),
            jax.ShapeDtypeStruct((devices, 1, 256), F32),
        ],
        name="head",
    )(x, mine, m0, m1, m2, targets, gain, weight)


def pick_body(table, where, spot, out):
    devices = table.shape[0]
    count = where.shape[1]
    hit = lax.broadcasted_iota(jnp.int32, (devices, count), 0) == where[...]
    hot = jnp.where(hit, 1.0, 0.0).astype(BF16)

    full = table[...]
    high = full.astype(BF16)
    rest = full - high.astype(F32)
    mid = rest.astype(BF16)
    low = (rest - mid.astype(F32)).astype(BF16)
    parts = jnp.concatenate([high, mid, low], axis=0)
    lines = lax.dot_general(
        parts,
        jnp.concatenate([hot, hot, hot], axis=0),
        (((0,), (0,)), ((), ())),
        preferred_element_type=F32,
    )
    mine = lax.broadcasted_iota(jnp.int32, lines.shape, 0) == spot[...]
    picked = jnp.sum(jnp.where(mine, lines, 0.0), axis=0, keepdims=True)
    out[...] = count * picked / jnp.sum(picked, axis=-1, keepdims=True)


def pick(table, where, spot):
    return pl.pallas_call(
        pick_body,
        in_specs=[pl.BlockSpec(memory_space=pltpu.VMEM)] * 3,
        out_specs=pl.BlockSpec(memory_space=pltpu.VMEM),
        out_shape=jax.ShapeDtypeStruct(where.shape, F32),
        name="pick",
    )(table, where, spot)


def per_device(
    activations,
    targets,
    candidates,
    mix_gain,
    project_weight,
    output_weight,
    up_weight,
    down_weight,
    pattern_bias,
    head_gain,
    head_weight,
):
    rows, cols, width = activations.shape
    hs = project_weight.shape[2]
    tokens = rows * cols
    row_peers = lax.axis_size(ROW)
    inv_root = 1.0 / math.sqrt(hs)
    third = tokens // 3

    devices = lax.axis_size(ALL)

    their_project = swap_core(project_weight)
    their_up = swap_core(up_weight)
    their_down = swap_core(down_weight)
    their_output = swap_core(output_weight)
    bias = (pattern_bias, swap_core(pattern_bias))

    x = activations.reshape(tokens, width)
    own = normalize(x, mix_gain[None, :])

    def after(first, values):
        return lax.optimization_barrier((first, values))[1]

    def ffn(shards, slots):
        return feed_forward(shards, slots, up_weight, their_up, down_weight, their_down)

    near = (up_z(own), down_z(own), swap_x(own))
    (ff_own,) = ffn((own,), 1)
    s_a, s_b, s_p = after((ff_own, their_project), near)
    s_aa, s_pb, s_pa = up_z(s_a), down_z(s_p), swap_x(s_a)

    def columns(shards):
        qkv, edge = project(shards, project_weight, their_project, rows)
        got = lax.all_to_all(
            qkv.reshape(row_peers, rows * HALF, 6 * hs), ROW, split_axis=0, concat_axis=0, tiled=True
        )
        return qkv, edge, got

    def attend_columns(group, got, *earlier):
        x = got.reshape(row_peers * rows, HALF, 6 * hs)
        return column_attention(group, bias, x, rows, hs, inv_root, earlier)

    qkv0, edge0, got0 = columns((own, s_a, s_b, s_p))
    edge0 = next_row(edge0)
    their_edge0 = swap_core(edge0)
    their_qkv0 = swap_core(qkv0)
    s_aa, s_pa, s_pb = after(qkv0, (s_aa, s_pa, s_pb))
    h_pa, h_pb = halves_of(s_pa, s_pb)
    far = (up_z(h_pa), down_z(h_pb))
    away = after(their_qkv0, (s_aa, s_pa, s_pb, *far))
    qkv1, edge1, got1 = columns(away)
    back = attend_columns(0, after(qkv1, got0))
    their_qkv1 = swap_core(qkv1)
    edge1 = next_row(edge1)
    their_edge1 = swap_core(edge1)
    ff1 = ffn(after((qkv1, back), away), 4)
    back = attend_columns(1, after((ff1, their_qkv1), got1), back)
    again = lax.all_to_all(back, ROW, split_axis=0, concat_axis=0, tiled=True)

    xl, z, core = lax.axis_index(XL), lax.axis_index(Z), lax.axis_index(CORE)
    n_z = lax.axis_size(Z)
    shift_x = jnp.array([0, 0, 0, 1, 0, 1, 1, 1], jnp.int32)
    shift_z = jnp.array([0, 3, 1, 0, 2, 3, 1, 2], jnp.int32)
    chip = ((xl + shift_x) % 2) * n_z + (z + shift_z) % n_z
    starts = chip * 2 * cols
    offs = jnp.arange(cols, dtype=jnp.int32)
    mine = (starts[:, None] + core * cols + offs[None, :]).reshape(-1)
    theirs = (starts[:, None] + (1 - core) * cols + offs[None, :]).reshape(-1)
    top = (lax.axis_index(ROW) == 0).astype(jnp.int32)[None]
    acc, den = row_attention(
        after(back, top),
        mine[:, None],
        jnp.concatenate([mine, theirs])[None, :],
        (qkv0, qkv1),
        (their_qkv0, their_qkv1),
        (edge0, edge1),
        (their_edge0, their_edge1),
        hs,
        inv_root,
    )
    f0, f1, f2 = terms(
        1, 3, again, acc[1], den[1], ff1[3:], output_weight, their_output, hs, rows,
        [(0, third * i, third * (i + 1)) for i in range(3)],
    )
    g0, g1, g2 = swap_x(f0), down_z(f1), up_z(f2)
    t_aa, t_pa, t_pb = terms(
        1, 0, *after(f0, (again, acc[1], den[1])), ff1[:3], output_weight, their_output, hs, rows,
        [(i, 0, tokens) for i in range(3)],
    )

    t_aa, t_pa, t_pb = add_far((t_aa, t_pa, t_pb), (g0, g1, g2))
    r_aa, r_pa, r_pb = down_z(t_aa), swap_x(t_pa), up_z(t_pb)
    ff0 = ffn(after(t_pb, (s_a, s_b, s_p)), 3)
    t_own, t_a, t_b, t_p = terms(
        0, 0, again, acc[0], den[0], (ff_own, *ff0), output_weight, their_output, hs, rows,
        [(i, 0, tokens) for i in range(4)],
    )
    from_b = up_z(t_b)
    t_a, t_p = add_near(t_a, t_p, r_aa, r_pa, r_pb)
    from_a, from_p = down_z(t_a), swap_x(t_p)

    layer_out, line = head(
        x,
        t_own,
        from_a,
        from_b,
        from_p,
        targets.reshape(tokens, 1),
        head_gain[None, :],
        head_weight,
        devices,
    )
    table = lax.all_to_all(
        line,
        ALL,
        split_axis=0,
        concat_axis=0,
        tiled=True,
    ).reshape(devices, 256)
    full_cols = cols * lax.axis_size(COL)
    c_row, c_col = candidates // full_cols, candidates % full_cols
    where = (c_row // rows) * lax.axis_size(COL) + c_col // cols
    spot = (c_row % rows) * cols + c_col % cols
    chosen = pick(table, where[None, :], spot[None, :])
    return (layer_out.reshape(rows, cols, width), chosen.reshape(-1))


def solution(mesh):
    split = Mesh(mesh.devices.reshape(2, 4, 2, 4, 2), ("row_0", "row_1", "col_0", "col_1", "col_2"))

    return jax.shard_map(
        per_device,
        mesh=split,
        in_specs=(
            P(ROW, COL, None),
            P(ROW, COL),
            P(),
            P(),
            P(None, None, COL),
            P(COL, None),
            P(None, COL),
            P(COL, None),
            P(COL),
            P(),
            P(),
        ),
        out_specs=(P(ROW, COL, None), P()),
        check_vma=False,
    )
```

```python
import math

import jax
import jax.numpy as jnp
from jax import lax
from jax.experimental import pallas as pl
from jax.experimental.pallas import tpu as pltpu
from jax.sharding import Mesh
from jax.sharding import PartitionSpec as P

COL = ("col_0", "col_1", "col_2")
ROW = ("row_0", "row_1")
ALL = ("row_0", "row_1", "col_0", "col_1", "col_2")
XL, Z, CORE = COL

EPS = 1e-06
F32 = jnp.float32
BF16 = jnp.bfloat16


def permuted(array, axis, by):
    n = lax.axis_size(axis)
    return lax.ppermute(array, axis, [(i, (i + by) % n) for i in range(n)])


def up_z(array):
    return permuted(array, Z, 1)


def down_z(array):
    return permuted(array, Z, -1)


def swap_x(array):
    return permuted(array, XL, 1)


def swap_core(array):
    return permuted(array, CORE, 1)


def next_row(array):
    n = lax.axis_size(ROW)
    return lax.ppermute(array, ROW, [(i, i + 1) for i in range(n - 1)])


def dot(a, b):
    return jnp.dot(a, b, preferred_element_type=F32)


def dot_t(a, b):
    return lax.dot_general(a, b, (((1,), (1,)), ((), ())), preferred_element_type=F32)


def cost(flops, bytes_accessed, exps=0):
    return pl.CostEstimate(flops=flops, bytes_accessed=bytes_accessed, transcendentals=exps)


VMEM = pl.BlockSpec(memory_space=pltpu.VMEM)
SMEM = pl.BlockSpec(memory_space=pltpu.SMEM)
ANY = pl.BlockSpec(memory_space=pl.ANY)
HALF = 16


def laid(column, lanes=256):
    shape = (column.shape[0], lanes)
    hit = lax.broadcasted_iota(jnp.int32, shape, 1) == lax.broadcasted_iota(jnp.int32, shape, 0)
    return jnp.sum(jnp.where(hit, column, 0.0), axis=0, keepdims=True)


def norm_body(x, gain, out):
    v = x[...].astype(F32)
    scale = lax.rsqrt(jnp.sum(v * v, axis=-1, keepdims=True) / v.shape[1] + EPS)
    out[...] = (v * scale * gain[...]).astype(BF16)


def normalize(x, gain):
    return pl.pallas_call(
        norm_body,
        in_specs=[VMEM, VMEM],
        out_specs=VMEM,
        out_shape=jax.ShapeDtypeStruct(x.shape, BF16),
        cost_estimate=cost(5 * x.size, 4 * x.size),
        name="normalize",
    )(x, gain)


def stacked(refs):
    return jnp.concatenate([ref[...] for ref in refs], axis=0)


def project_body(rows, n, *refs):
    mine, theirs, out, edge = refs[n:]
    x = stacked(refs[:n])
    w = jnp.concatenate([mine[0], theirs[0]], axis=1)
    y = dot(x, w).astype(BF16).reshape(4, rows, 2, HALF, w.shape[1])
    for g in range(2):
        out[:, g] = y[:, :, g]
        edge[:, g] = y[:, rows - 1, g]


def project(shards, mine, theirs, rows):
    n = len(shards)
    total = sum(v.shape[0] for v in shards)
    _, width, hs = mine.shape
    whole = [pl.BlockSpec(v.shape, lambda j: (0, 0)) for v in shards]
    weight = pl.BlockSpec((1, width, hs), lambda j: (j, 0, 0))
    return pl.pallas_call(
        lambda *refs: project_body(rows, n, *refs),
        grid=(3,),
        in_specs=whole + [weight] * 2,
        out_specs=[
            pl.BlockSpec((4, 2, rows, HALF, 2 * hs), lambda j: (0, 0, 0, 0, j)),
            pl.BlockSpec((4, 2, HALF, 2 * hs), lambda j: (0, 0, 0, jnp.maximum(j - 1, 0))),
        ],
        out_shape=[
            jax.ShapeDtypeStruct((4, 2, rows, HALF, 6 * hs), BF16),
            jax.ShapeDtypeStruct((4, 2, HALF, 4 * hs), BF16),
        ],
        cost_estimate=cost(2 * total * width * 6 * hs, 2 * total * width + 12 * width * hs),
        name="project",
    )(*shards, mine, theirs)


def forward_body(n, slots, unrolled, *refs):
    shards, (up, their_up, down, their_down) = refs[:n], refs[n : n + 4]
    outs, (x, rise, fall, hidden, done, sems, out_sems) = refs[n + 4 : -7], refs[-7:]
    tokens = x.shape[0] // slots
    width, units = up.shape
    sizes = [ref.shape[0] for ref in shards]
    starts = [sum(sizes[:i]) for i in range(n)]

    def fetch(source, target, i):
        copy = pltpu.make_async_copy(source, target, sems.at[i])
        copy.start()
        return copy

    def shard(i):
        return fetch(shards[i], x.at[starts[i] : starts[i] + sizes[i]], i)

    x_in = [shard(0)]
    ups = [fetch(up, rise.at[:, :units], n), fetch(their_up, rise.at[:, units:], n + 1)]
    x_in += [shard(i) for i in range(1, n)]
    downs = [fetch(down, fall.at[:units], n + 2), fetch(their_down, fall.at[units:], n + 3)]

    def rows_of(s):
        return pl.ds(s * tokens if unrolled else pl.multiple_of(s * tokens, tokens), tokens)

    def each_slot(step):
        if unrolled:
            for s in range(slots):
                step(s, 0)
        else:
            lax.fori_loop(0, slots, step, 0)

    def ascend(s, carry):
        at = rows_of(s)
        for i in range(n):

            @pl.when(s == starts[i] // tokens)
            def _():
                x_in[i].wait()

        total = 0.0
        for c in range(2):

            @pl.when(s == 0)
            def _():
                ups[c].wait()

            lanes = slice(units * c, units * (c + 1))
            h = jax.nn.gelu(dot(x[at, :], rise[:, lanes]), approximate=True).astype(BF16)
            hidden[at, lanes] = h
            h_f = h.astype(F32)
            total = total + jnp.sum(h_f * h_f, axis=-1, keepdims=True)
        done[at, width : width + 128] = jnp.broadcast_to(total, (tokens, 128)).astype(BF16)
        return carry

    each_slot(ascend)
    for copy in downs:
        copy.wait()
    copies = []
    for s in range(slots):
        source = done.at[tokens * s : tokens * (s + 1)]
        copies.append(pltpu.make_async_copy(source, outs[s], out_sems.at[s]))

    def descend(s, carry):
        at = rows_of(s)
        done[at, 0:width] = dot(hidden[at, :], fall[...]).astype(BF16)
        for i in range(slots):

            @pl.when(s == i)
            def _():
                copies[i].start()

        return carry

    each_slot(descend)
    for copy in copies:
        copy.wait()


def feed_forward(shards, slots, up, their_up, down, their_down):
    n = len(shards)
    total = sum(v.shape[0] for v in shards)
    tokens, width = total // slots, shards[0].shape[1]
    units = 2 * up.shape[1]
    return pl.pallas_call(
        lambda *refs: forward_body(n, slots, slots == 4, *refs),
        in_specs=[ANY] * (n + 4),
        out_specs=[ANY] * slots,
        out_shape=[jax.ShapeDtypeStruct((tokens, width + 128), BF16)] * slots,
        scratch_shapes=[
            pltpu.VMEM((total, width), BF16),
            pltpu.VMEM((width, units), BF16),
            pltpu.VMEM((units, width), BF16),
            pltpu.VMEM((total, units), BF16),
            pltpu.VMEM((total, width + 128), BF16),
            pltpu.SemaphoreType.DMA((n + 4,)),
            pltpu.SemaphoreType.DMA((slots,)),
        ],
        cost_estimate=cost(4 * total * width * units, 4 * total * width + 4 * width * units),
        name="feed_forward",
    )(*shards, up, their_up, down, their_down)


def row_body(inv_root, hs, top_ref, qcol, kcol, *refs):
    cur, theirs, edges = refs[:2], refs[2:6], refs[6:10]
    accs, dens, above = refs[10:12], refs[12:14], refs[14:]
    r = pl.program_id(0)
    first = r == 0
    n = qcol.shape[0] // 2
    mask = kcol[...] <= qcol[...]
    closed = jnp.logical_and(first, top_ref[0] == 1)
    same_one = jnp.where(mask, 1.0, 0.0)
    prev_one = jnp.where(closed, 0.0, 1.0 - same_one).astype(BF16)
    same_one = same_one.astype(BF16)
    ones = jnp.ones((kcol.shape[1], hs), BF16)
    scale = inv_root * math.log2(math.e)

    @pl.when(first)
    def _():
        for keep, edge in zip(above, edges):
            keep[...] = edge[...].reshape(n, 4 * hs)

    now = [ref[:, :, 0, :, 2 * hs :].reshape(n, 4 * hs) for ref in cur]
    for i in range(2):
        pair = [ref[:, :, 0].reshape(n, 2 * hs) for ref in theirs[2 * i : 2 * i + 2]]
        now.append(jnp.concatenate(pair, axis=1))
    before = [ref[...] for ref in above]
    for h in range(2):
        at = slice(h * hs, (h + 1) * hs)
        q = jnp.concatenate([ref[:, :, 0, :, at].reshape(n, hs) for ref in cur], axis=0)

        def taken(parts, base):
            lanes = [base + hs * h] * 2 + [base + hs * (1 - h)] * 2
            return jnp.concatenate([p[:, m : m + hs] for p, m in zip(parts, lanes)], axis=0)

        scores = jnp.where(mask, dot_t(q, taken(now, 0)), dot_t(q, taken(before, 0))) * scale
        w = jnp.exp2(scores).astype(BF16)
        out = dot(w * same_one, jnp.concatenate([taken(now, 2 * hs), ones], axis=1))
        out = out + dot(w * prev_one, jnp.concatenate([taken(before, 2 * hs), ones], axis=1))
        shape = (4, 2, HALF, hs)
        for i in range(2):
            half = out[n * i : n * (i + 1)]
            accs[i][:, :, 0, :, at] = half[:, :hs].astype(BF16).reshape(shape)
            dens[i][:, :, 0, :, at] = half[:, hs:].reshape(shape)
    for keep, value in zip(above, now):
        keep[...] = value


def row_attention(top, qcol, kcol, qkv, their_qkv, edge, their_edge, hs, inv_root):
    rows = qkv[0].shape[2]
    now = pl.BlockSpec((4, 2, 1, HALF, 6 * hs), lambda r: (0, 0, r, 0, 0))
    keys = pl.BlockSpec((4, 2, 1, HALF, 2 * hs), lambda r: (0, 0, r, 0, 1))
    values = pl.BlockSpec((4, 2, 1, HALF, 2 * hs), lambda r: (0, 0, r, 0, 2))
    whole = lambda a: pl.BlockSpec(a.shape, lambda r: (0,) * a.ndim)
    out = lambda kind: jax.ShapeDtypeStruct((4, 2, rows, HALF, 2 * hs), kind)
    out_spec = pl.BlockSpec((4, 2, 1, HALF, 2 * hs), lambda r: (0, 0, r, 0, 0))
    n = qcol.shape[0]
    outs = pl.pallas_call(
        lambda *refs: row_body(inv_root, hs, *refs),
        grid=(rows,),
        in_specs=[SMEM, whole(qcol), whole(kcol), now, now, keys, values, keys, values]
        + [whole(e) for e in (*edge, *their_edge)],
        out_specs=[out_spec] * 4,
        out_shape=[out(BF16)] * 2 + [out(F32)] * 2,
        scratch_shapes=[pltpu.VMEM((n // 2, 4 * hs), BF16)] * 4,
        cost_estimate=cost(rows * 32 * n * n * hs, rows * 32 * n * hs, rows * 4 * n * n),
        name="row_attention",
    )(
        top, qcol, kcol, *qkv, their_qkv[0], their_qkv[0], their_qkv[1], their_qkv[1],
        *edge, *their_edge,
    )
    return outs[:2], outs[2:]


def col_body(inv_root, hs, own_rows, bias, their_bias, x, *refs):
    out = refs[-1]
    rows, cols, _ = x.shape
    chunk = 16
    spots = rows * cols
    step = chunk * cols
    log2e = math.log2(math.e)
    lane = lax.broadcasted_iota(jnp.int32, (step, 128), 1)
    spot = lax.broadcasted_iota(jnp.int32, (step, 128), 0) & (cols - 1)
    ones = jnp.ones((spots, hs), BF16)

    def part(at):
        return x[:, :, at * hs : (at + 1) * hs].reshape(spots, hs)

    den_rows = []
    for i in range(rows // chunk):
        n = step * (i + 1)
        qi = lax.broadcasted_iota(jnp.int32, (step, n), 0) + step * i
        ki = lax.broadcasted_iota(jnp.int32, (step, n), 1)
        keep = jnp.logical_and(((qi - ki) & (cols - 1)) == 0, ki < qi)
        laid_out = 0.0
        for h in range(2):
            q, k, v = part(h), part(2 + h), part(4 + h)
            s = dot_t(q[step * i : n], k[:n]) * (inv_root * log2e)
            s = s + (bias, their_bias)[h][0] * log2e
            w = jnp.where(keep, jnp.exp2(s), 0.0).astype(BF16)
            a = dot(w, jnp.concatenate([v[:n], ones[:n]], axis=1))
            laid_out = laid_out + jnp.where(lane == spot + cols * h, a[:, hs:], 0.0)
            a = a[:, :hs].astype(BF16).reshape(chunk, cols, hs)
            for j in range(chunk):
                r = chunk * i + j
                out[r // own_rows, 0, r % own_rows, :, h * hs : (h + 1) * hs] = a[j]
        den_rows.append(jnp.sum(laid_out.reshape(chunk, cols, 128), axis=1))
    den_rows = jnp.concatenate(den_rows, axis=0)
    fill = jnp.zeros((cols - own_rows, 128), F32)
    for b in range(rows // own_rows):
        block = jnp.concatenate([den_rows[own_rows * b : own_rows * (b + 1)], fill], axis=0)
        out[b, 0, own_rows, :, 0:128] = block.astype(BF16)
        out[b, 0, own_rows, :, 128:256] = jnp.zeros((cols, 128), BF16)


def column_attention(group, bias, x, own_rows, hs, inv_root, earlier=()):
    rows, cols, _ = x.shape
    spots = rows * cols
    peers = rows // own_rows
    return pl.pallas_call(
        lambda *refs: col_body(inv_root, hs, own_rows, *refs),
        grid=(1,),
        in_specs=[SMEM, SMEM, pl.BlockSpec(x.shape, lambda i: (0, 0, 0))]
        + [pl.BlockSpec(memory_space=pl.ANY)] * len(earlier),
        out_specs=pl.BlockSpec(
            (peers, 1, own_rows + 1, cols, 2 * hs), lambda i: (0, group, 0, 0, 0)
        ),
        out_shape=jax.ShapeDtypeStruct((peers, 2, own_rows + 1, cols, 2 * hs), BF16),
        input_output_aliases={3: 0} if earlier else {},
        cost_estimate=cost(6 * spots * spots * hs, 16 * spots * hs, 2 * spots * spots),
        name="column_attention",
    )(*bias, x, *earlier)


def term_body(hs, rows, splits, got, acc, den, *refs):
    count = len({slot for slot, _, _ in splits})
    ffs, (w_mine, w_their), outs = refs[:count], refs[count : count + 2], refs[count + 2 :]
    spots = 2 * count * rows * HALF
    lines = 2 * count * HALF
    unit = lax.broadcasted_iota(jnp.int32, (spots, lines), 0) // HALF
    line = lax.broadcasted_iota(jnp.int32, (spots, lines), 1)
    hit = jnp.logical_and(unit == (line // HALF) * rows + line % HALF, line % HALF < rows)
    table = got[:, 0, rows, :, 0:128].reshape(lines, 128)
    table = dot(jnp.where(hit, 1.0, 0.0).astype(BF16), table)
    lane = lax.broadcasted_iota(jnp.int32, (spots, 128), 1)
    spot = lax.broadcasted_iota(jnp.int32, (spots, 128), 0) % HALF
    ones = jnp.ones((128, 128), BF16)
    parts = []
    for h in range(2):
        at = slice(h * hs, (h + 1) * hs)
        col_den = dot(jnp.where(lane == spot + HALF * h, table, 0.0).astype(BF16), ones)
        total = acc[:, :, :, :, at].reshape(spots, hs).astype(F32)
        total = total + got[:, 0, 0:rows, :, at].reshape(spots, hs).astype(F32)
        parts.append((total / (den[:, :, :, :, at].reshape(spots, hs) + col_den)).astype(BF16))
    halves = jnp.concatenate(parts, axis=1).reshape(count, 2, rows, HALF, 2 * hs)
    blocks = [halves[s, g, r] for s in range(count) for r in range(rows) for g in range(2)]
    attended = jnp.concatenate(blocks, axis=0)
    att_f = attended.astype(F32)
    squares = jnp.sum(att_f * att_f, axis=-1, keepdims=True)
    weight = jnp.concatenate([w_mine[...], w_their[...]], axis=0)
    term = dot(attended, weight).astype(BF16)
    width = term.shape[1]
    for out, (slot, low, high) in zip(outs, splits):
        f = ffs[slot]
        tokens = f.shape[0]
        at = slice(tokens * slot + low, tokens * slot + high)
        out[:, 0:width] = f[low:high, 0:width] + term[at]
        out[:, width:] = (f[low:high, width:].astype(F32) + squares[at]).astype(BF16)


def terms(group, base, got, acc, den, ff, w_mine, w_their, hs, rows, splits):
    tokens, full = ff[0].shape
    count = len(ff)
    whole = lambda a: pl.BlockSpec(a.shape, lambda i: (0,) * a.ndim)
    local = pl.BlockSpec((count, 2, rows, HALF, 2 * hs), lambda i: (base // count, 0, 0, 0, 0))
    return pl.pallas_call(
        lambda *refs: term_body(hs, rows, splits, *refs),
        grid=(1,),
        in_specs=[
            pl.BlockSpec(
                (2 * count, 1, rows + 1, HALF, 2 * hs), lambda i: (base // count, group, 0, 0, 0)
            ),
            local,
            local,
        ]
        + [whole(a) for a in (*ff, w_mine, w_their)],
        out_specs=[pl.BlockSpec((b - a, full), lambda i: (0, 0)) for _, a, b in splits],
        out_shape=[jax.ShapeDtypeStruct((b - a, full), BF16) for _, a, b in splits],
        cost_estimate=cost(4 * count * tokens * hs * full, 5 * count * tokens * full),
        name="terms",
    )(got, acc, den, *ff, w_mine, w_their)


def halves_body(t0, t1, o0, o1):
    o0[...] = t0[...]
    o1[...] = t1[...]


def halves_of(first, second):
    rows, width = first.shape
    block = lambda at: pl.BlockSpec((rows // 2, width), lambda i: (at, 0))
    return pl.pallas_call(
        halves_body,
        grid=(1,),
        in_specs=[block(0), block(1)],
        out_specs=[block(0)] * 2,
        out_shape=[jax.ShapeDtypeStruct((rows // 2, width), BF16)] * 2,
        cost_estimate=cost(0, 4 * rows * width),
        name="halves",
    )(first, second)


def far_body(t0, t1, t2, g0, g1, g2, o0, o1, o2):
    for t, g, o in ((t0, g0, o0), (t1, g1, o1), (t2, g2, o2)):
        o[...] = t[...] + g[...]


def add_far(arrays, parts):
    third, width = parts[0].shape
    block = lambda at: pl.BlockSpec((third, width), lambda i: (at, 0))
    spread = [block(0), block(1), block(2)]
    return pl.pallas_call(
        far_body,
        grid=(1,),
        in_specs=spread + [block(0)] * 3,
        out_specs=spread,
        out_shape=[jax.ShapeDtypeStruct(arrays[0].shape, BF16)] * 3,
        input_output_aliases={0: 0, 1: 1, 2: 2},
        cost_estimate=cost(6 * third * width, 18 * third * width),
        name="add_far",
    )(*arrays, *parts)


def near_body(t0, t1, r0, r1, r2, o0, o1):
    o0[...] = t0[...] + (r0[...] + r1[...])
    o1[...] = t1[...] + r2[...]


def add_near(*arrays):
    rows, width = arrays[0].shape
    return pl.pallas_call(
        near_body,
        in_specs=[VMEM] * 5,
        out_specs=[VMEM] * 2,
        out_shape=[jax.ShapeDtypeStruct((rows, width), BF16)] * 2,
        cost_estimate=cost(3 * rows * width, 14 * rows * width),
        name="add_near",
    )(*arrays)


def head_body(x, mine, m0, m1, m2, targets, gain, weight, layer_out, line):
    width = x.shape[1]
    mixed, spread = 0.0, 0.0
    for m in (mine, m0, m1, m2):
        mixed = mixed + m[:, :width].astype(F32)
        spread = spread + m[:, width : width + 1].astype(F32)
    lo = (x[...].astype(F32) + mixed).astype(BF16)
    layer_out[...] = lo
    back = lo.astype(F32)
    inv_norm = lax.rsqrt(jnp.sum(back * back, axis=-1, keepdims=True) / width + EPS)
    head_in = (back * inv_norm * gain[...]).astype(BF16)
    raised = jnp.exp(dot(head_in, weight[...]))
    prob = raised / jnp.sum(raised, axis=-1, keepdims=True)
    levels = lax.broadcasted_iota(jnp.int32, prob.shape, 1)
    grad = prob - jnp.where(levels == targets[...], 1.0, 0.0)
    scaled = gain[...] * dot_t(grad.astype(BF16), weight[...])
    lean = jnp.sum(back * scaled, axis=-1, keepdims=True) / width
    layer_grad = inv_norm * scaled - back * (inv_norm * inv_norm * inv_norm) * lean
    head_f = head_in.astype(F32)
    out_sq = jnp.sum(head_f * head_f, axis=-1, keepdims=True) * jnp.sum(
        grad * grad, axis=-1, keepdims=True
    )
    layer_sq = jnp.sum(layer_grad * layer_grad, axis=-1, keepdims=True)
    norm = jnp.sqrt(laid(out_sq + spread * layer_sq))
    line[...] = jnp.broadcast_to(norm[None], line.shape)


def head(x, mine, m0, m1, m2, targets, gain, weight, devices):
    return pl.pallas_call(
        head_body,
        in_specs=[VMEM] * 8,
        out_specs=[pl.BlockSpec(memory_space=pltpu.VMEM)] * 2,
        out_shape=[
            jax.ShapeDtypeStruct(x.shape, BF16),
            jax.ShapeDtypeStruct((devices, 1, 256), F32),
        ],
        name="head",
    )(x, mine, m0, m1, m2, targets, gain, weight)


def pick_body(table, where, spot, out):
    devices = table.shape[0]
    count = where.shape[1]
    hit = lax.broadcasted_iota(jnp.int32, (devices, count), 0) == where[...]
    hot = jnp.where(hit, 1.0, 0.0).astype(BF16)

    full = table[...]
    high = full.astype(BF16)
    rest = full - high.astype(F32)
    mid = rest.astype(BF16)
    low = (rest - mid.astype(F32)).astype(BF16)
    parts = jnp.concatenate([high, mid, low], axis=0)
    lines = lax.dot_general(
        parts,
        jnp.concatenate([hot, hot, hot], axis=0),
        (((0,), (0,)), ((), ())),
        preferred_element_type=F32,
    )
    mine = lax.broadcasted_iota(jnp.int32, lines.shape, 0) == spot[...]
    picked = jnp.sum(jnp.where(mine, lines, 0.0), axis=0, keepdims=True)
    out[...] = count * picked / jnp.sum(picked, axis=-1, keepdims=True)


def pick(table, where, spot):
    return pl.pallas_call(
        pick_body,
        in_specs=[pl.BlockSpec(memory_space=pltpu.VMEM)] * 3,
        out_specs=pl.BlockSpec(memory_space=pltpu.VMEM),
        out_shape=jax.ShapeDtypeStruct(where.shape, F32),
        name="pick",
    )(table, where, spot)


def per_device(
    activations,
    targets,
    candidates,
    mix_gain,
    project_weight,
    output_weight,
    up_weight,
    down_weight,
    pattern_bias,
    head_gain,
    head_weight,
):
    rows, cols, width = activations.shape
    hs = project_weight.shape[2]
    tokens = rows * cols
    row_peers = lax.axis_size(ROW)
    inv_root = 1.0 / math.sqrt(hs)
    third = tokens // 3

    devices = lax.axis_size(ALL)

    their_project = swap_core(project_weight)
    their_up = swap_core(up_weight)
    their_down = swap_core(down_weight)
    their_output = swap_core(output_weight)
    bias = (pattern_bias, swap_core(pattern_bias))

    x = activations.reshape(tokens, width)
    own = normalize(x, mix_gain[None, :])

    def after(first, values):
        return lax.optimization_barrier((first, values))[1]

    def ffn(shards, slots):
        return feed_forward(shards, slots, up_weight, their_up, down_weight, their_down)

    xl, z, core = lax.axis_index(XL), lax.axis_index(Z), lax.axis_index(CORE)
    n_z = lax.axis_size(Z)
    shift_x = jnp.array([0, 0, 0, 1, 0, 1, 1, 1], jnp.int32)
    shift_z = jnp.array([0, 3, 1, 0, 2, 3, 1, 2], jnp.int32)
    chip = ((xl + shift_x) % 2) * n_z + (z + shift_z) % n_z
    starts = chip * 2 * cols
    offs = jnp.arange(cols, dtype=jnp.int32)
    mine = (starts[:, None] + core * cols + offs[None, :]).reshape(-1)
    theirs = (starts[:, None] + (1 - core) * cols + offs[None, :]).reshape(-1)
    columns_of = (mine[:, None], jnp.concatenate([mine, theirs])[None, :])

    near = (up_z(own), down_z(own), swap_x(own))
    (ff_own,) = ffn((own,), 1)
    s_a, s_b, s_p = after((ff_own, their_project, columns_of), near)
    s_aa, s_pb, s_pa = up_z(s_a), down_z(s_p), swap_x(s_a)

    def columns(shards):
        qkv, edge = project(shards, project_weight, their_project, rows)
        got = lax.all_to_all(
            qkv.reshape(row_peers, rows * HALF, 6 * hs), ROW, split_axis=0, concat_axis=0, tiled=True
        )
        return qkv, edge, got

    def attend_columns(group, got, *earlier):
        x = got.reshape(row_peers * rows, HALF, 6 * hs)
        return column_attention(group, bias, x, rows, hs, inv_root, earlier)

    qkv0, edge0, got0 = columns((own, s_a, s_b, s_p))
    edge0 = next_row(edge0)
    their_edge0 = swap_core(edge0)
    their_qkv0 = swap_core(qkv0)
    s_aa, s_pa, s_pb = after(qkv0, (s_aa, s_pa, s_pb))
    h_pa, h_pb = halves_of(s_pa, s_pb)
    far = (up_z(h_pa), down_z(h_pb))
    away = after(their_qkv0, (s_aa, s_pa, s_pb, *far))
    qkv1, edge1, got1 = columns(away)
    back = attend_columns(0, after(qkv1, got0))
    their_qkv1 = swap_core(qkv1)
    edge1 = next_row(edge1)
    their_edge1 = swap_core(edge1)
    ff1 = ffn(after((qkv1, back), away), 4)
    back = attend_columns(1, after((ff1, their_qkv1), got1), back)
    again = lax.all_to_all(back, ROW, split_axis=0, concat_axis=0, tiled=True)

    top = (lax.axis_index(ROW) == 0).astype(jnp.int32)[None]
    acc, den = row_attention(
        after(back, top),
        *columns_of,
        (qkv0, qkv1),
        (their_qkv0, their_qkv1),
        (edge0, edge1),
        (their_edge0, their_edge1),
        hs,
        inv_root,
    )
    f0, f1, f2 = terms(
        1, 3, again, acc[1], den[1], ff1[3:], output_weight, their_output, hs, rows,
        [(0, third * i, third * (i + 1)) for i in range(3)],
    )
    g0, g1, g2 = swap_x(f0), down_z(f1), up_z(f2)
    t_aa, t_pa, t_pb = terms(
        1, 0, *after(f0, (again, acc[1], den[1])), ff1[:3], output_weight, their_output, hs, rows,
        [(i, 0, tokens) for i in range(3)],
    )

    t_aa, t_pa, t_pb = add_far((t_aa, t_pa, t_pb), (g0, g1, g2))
    r_aa, r_pa, r_pb = down_z(t_aa), swap_x(t_pa), up_z(t_pb)
    ff0 = ffn(after(t_pb, (s_a, s_b, s_p)), 3)
    t_own, t_a, t_b, t_p = terms(
        0, 0, again, acc[0], den[0], (ff_own, *ff0), output_weight, their_output, hs, rows,
        [(i, 0, tokens) for i in range(4)],
    )
    from_b = up_z(t_b)
    t_a, t_p = add_near(t_a, t_p, r_aa, r_pa, r_pb)
    from_a, from_p = down_z(t_a), swap_x(t_p)

    layer_out, line = head(
        x,
        t_own,
        from_a,
        from_b,
        from_p,
        targets.reshape(tokens, 1),
        head_gain[None, :],
        head_weight,
        devices,
    )
    table = lax.all_to_all(
        line,
        ALL,
        split_axis=0,
        concat_axis=0,
        tiled=True,
    ).reshape(devices, 256)
    full_cols = cols * lax.axis_size(COL)
    c_row, c_col = candidates // full_cols, candidates % full_cols
    where = (c_row // rows) * lax.axis_size(COL) + c_col // cols
    spot = (c_row % rows) * cols + c_col % cols
    chosen = pick(table, where[None, :], spot[None, :])
    return (layer_out.reshape(rows, cols, width), chosen.reshape(-1))


def solution(mesh):
    split = Mesh(mesh.devices.reshape(2, 4, 2, 4, 2), ("row_0", "row_1", "col_0", "col_1", "col_2"))

    return jax.shard_map(
        per_device,
        mesh=split,
        in_specs=(
            P(ROW, COL, None),
            P(ROW, COL),
            P(),
            P(),
            P(None, None, COL),
            P(COL, None),
            P(None, COL),
            P(COL, None),
            P(COL),
            P(),
            P(),
        ),
        out_specs=(P(ROW, COL, None), P()),
        check_vma=False,
    )
```

```python
import math

import jax
import jax.numpy as jnp
from jax import lax
from jax.experimental import pallas as pl
from jax.experimental.pallas import tpu as pltpu
from jax.sharding import Mesh
from jax.sharding import PartitionSpec as P

COL = ("col_0", "col_1", "col_2")
ROW = ("row_0", "row_1")
ALL = ("row_0", "row_1", "col_0", "col_1", "col_2")
XL, Z, CORE = COL

EPS = 1e-06
F32 = jnp.float32
BF16 = jnp.bfloat16


def permuted(array, axis, by):
    n = lax.axis_size(axis)
    return lax.ppermute(array, axis, [(i, (i + by) % n) for i in range(n)])


def up_z(array):
    return permuted(array, Z, 1)


def down_z(array):
    return permuted(array, Z, -1)


def swap_x(array):
    return permuted(array, XL, 1)


def swap_core(array):
    return permuted(array, CORE, 1)


def next_row(array):
    n = lax.axis_size(ROW)
    return lax.ppermute(array, ROW, [(i, i + 1) for i in range(n - 1)])


def dot(a, b):
    return jnp.dot(a, b, preferred_element_type=F32)


def dot_t(a, b):
    return lax.dot_general(a, b, (((1,), (1,)), ((), ())), preferred_element_type=F32)


def cost(flops, bytes_accessed, exps=0):
    return pl.CostEstimate(flops=flops, bytes_accessed=bytes_accessed, transcendentals=exps)


VMEM = pl.BlockSpec(memory_space=pltpu.VMEM)
SMEM = pl.BlockSpec(memory_space=pltpu.SMEM)
ANY = pl.BlockSpec(memory_space=pl.ANY)
HALF = 16


def laid(column, lanes=256):
    shape = (column.shape[0], lanes)
    hit = lax.broadcasted_iota(jnp.int32, shape, 1) == lax.broadcasted_iota(jnp.int32, shape, 0)
    return jnp.sum(jnp.where(hit, column, 0.0), axis=0, keepdims=True)


def norm_body(x, gain, out):
    v = x[...].astype(F32)
    scale = lax.rsqrt(jnp.sum(v * v, axis=-1, keepdims=True) / v.shape[1] + EPS)
    out[...] = (v * scale * gain[...]).astype(BF16)


def normalize(x, gain):
    return pl.pallas_call(
        norm_body,
        in_specs=[VMEM, VMEM],
        out_specs=VMEM,
        out_shape=jax.ShapeDtypeStruct(x.shape, BF16),
        cost_estimate=cost(5 * x.size, 4 * x.size),
        name="normalize",
    )(x, gain)


def stacked(refs):
    return jnp.concatenate([ref[...] for ref in refs], axis=0)


def project_body(rows, n, *refs):
    mine, theirs, out, edge = refs[n:]
    x = stacked(refs[:n])
    w = jnp.concatenate([mine[0], theirs[0]], axis=1)
    y = dot(x, w).astype(BF16).reshape(4, rows, 2, HALF, w.shape[1])
    for g in range(2):
        out[:, g] = y[:, :, g]
        edge[:, g] = y[:, rows - 1, g]


def project(shards, mine, theirs, rows):
    n = len(shards)
    total = sum(v.shape[0] for v in shards)
    _, width, hs = mine.shape
    whole = [pl.BlockSpec(v.shape, lambda j: (0, 0)) for v in shards]
    weight = pl.BlockSpec((1, width, hs), lambda j: (j, 0, 0))
    return pl.pallas_call(
        lambda *refs: project_body(rows, n, *refs),
        grid=(3,),
        in_specs=whole + [weight] * 2,
        out_specs=[
            pl.BlockSpec((4, 2, rows, HALF, 2 * hs), lambda j: (0, 0, 0, 0, j)),
            pl.BlockSpec((4, 2, HALF, 2 * hs), lambda j: (0, 0, 0, jnp.maximum(j - 1, 0))),
        ],
        out_shape=[
            jax.ShapeDtypeStruct((4, 2, rows, HALF, 6 * hs), BF16),
            jax.ShapeDtypeStruct((4, 2, HALF, 4 * hs), BF16),
        ],
        cost_estimate=cost(2 * total * width * 6 * hs, 2 * total * width + 12 * width * hs),
        name="project",
    )(*shards, mine, theirs)


def forward_body(n, slots, unrolled, *refs):
    shards, (up, their_up, down, their_down) = refs[:n], refs[n : n + 4]
    outs, (x, rise, fall, hidden, done, sems, out_sems) = refs[n + 4 : -7], refs[-7:]
    tokens = x.shape[0] // slots
    width, units = up.shape
    sizes = [ref.shape[0] for ref in shards]
    starts = [sum(sizes[:i]) for i in range(n)]

    def fetch(source, target, i):
        copy = pltpu.make_async_copy(source, target, sems.at[i])
        copy.start()
        return copy

    def shard(i):
        return fetch(shards[i], x.at[starts[i] : starts[i] + sizes[i]], i)

    x_in = [shard(0)]
    ups = [fetch(up, rise.at[:, :units], n), fetch(their_up, rise.at[:, units:], n + 1)]
    x_in += [shard(i) for i in range(1, n)]
    downs = [fetch(down, fall.at[:units], n + 2), fetch(their_down, fall.at[units:], n + 3)]

    def rows_of(s):
        return pl.ds(s * tokens if unrolled else pl.multiple_of(s * tokens, tokens), tokens)

    def each_slot(step):
        if unrolled:
            for s in range(slots):
                step(s, 0)
        else:
            lax.fori_loop(0, slots, step, 0)

    def ascend(s, carry):
        at = rows_of(s)
        for i in range(n):

            @pl.when(s == starts[i] // tokens)
            def _():
                x_in[i].wait()

        total = 0.0
        for c in range(2):

            @pl.when(s == 0)
            def _():
                ups[c].wait()

            lanes = slice(units * c, units * (c + 1))
            h = jax.nn.gelu(dot(x[at, :], rise[:, lanes]), approximate=True).astype(BF16)
            hidden[at, lanes] = h
            h_f = h.astype(F32)
            total = total + jnp.sum(h_f * h_f, axis=-1, keepdims=True)
        done[at, width : width + 128] = jnp.broadcast_to(total, (tokens, 128)).astype(BF16)
        return carry

    each_slot(ascend)
    for copy in downs:
        copy.wait()
    copies = []
    for s in range(slots):
        source = done.at[tokens * s : tokens * (s + 1)]
        copies.append(pltpu.make_async_copy(source, outs[s], out_sems.at[s]))

    def descend(s, carry):
        at = rows_of(s)
        done[at, 0:width] = dot(hidden[at, :], fall[...]).astype(BF16)
        for i in range(slots):

            @pl.when(s == i)
            def _():
                copies[i].start()

        return carry

    each_slot(descend)
    for copy in copies:
        copy.wait()


def feed_forward(shards, slots, up, their_up, down, their_down):
    n = len(shards)
    total = sum(v.shape[0] for v in shards)
    tokens, width = total // slots, shards[0].shape[1]
    units = 2 * up.shape[1]
    return pl.pallas_call(
        lambda *refs: forward_body(n, slots, slots == 4, *refs),
        in_specs=[ANY] * (n + 4),
        out_specs=[ANY] * slots,
        out_shape=[jax.ShapeDtypeStruct((tokens, width + 128), BF16)] * slots,
        scratch_shapes=[
            pltpu.VMEM((total, width), BF16),
            pltpu.VMEM((width, units), BF16),
            pltpu.VMEM((units, width), BF16),
            pltpu.VMEM((total, units), BF16),
            pltpu.VMEM((total, width + 128), BF16),
            pltpu.SemaphoreType.DMA((n + 4,)),
            pltpu.SemaphoreType.DMA((slots,)),
        ],
        cost_estimate=cost(4 * total * width * units, 4 * total * width + 4 * width * units),
        name="feed_forward",
    )(*shards, up, their_up, down, their_down)


def row_body(inv_root, hs, top_ref, kcol, *refs):
    cur, theirs, edges = refs[:2], refs[2:6], refs[6:10]
    accs, dens, above, qcol = refs[10:12], refs[12:14], refs[14:18], refs[18]
    r = pl.program_id(0)
    first = r == 0
    n = qcol.shape[0] // 2

    @pl.when(first)
    def _():
        shape = (2 * n, 2 * n)
        row, col = (lax.broadcasted_iota(jnp.int32, shape, i) for i in range(2))
        here = jnp.where(row == col, kcol[:, : 2 * n].astype(F32), 0.0)
        qcol[...] = jnp.broadcast_to(jnp.sum(here, axis=-1, keepdims=True), qcol.shape)

    mask = kcol[...].astype(F32) <= qcol[:, 0:1]
    closed = jnp.logical_and(first, top_ref[0] == 1)
    same_one = jnp.where(mask, 1.0, 0.0)
    prev_one = jnp.where(closed, 0.0, 1.0 - same_one).astype(BF16)
    same_one = same_one.astype(BF16)
    ones = jnp.ones((kcol.shape[1], hs), BF16)
    scale = inv_root * math.log2(math.e)

    @pl.when(first)
    def _():
        for keep, edge in zip(above, edges):
            keep[...] = edge[...].reshape(n, 4 * hs)

    now = [ref[:, :, 0, :, 2 * hs :].reshape(n, 4 * hs) for ref in cur]
    for i in range(2):
        pair = [ref[:, :, 0].reshape(n, 2 * hs) for ref in theirs[2 * i : 2 * i + 2]]
        now.append(jnp.concatenate(pair, axis=1))
    before = [ref[...] for ref in above]
    for h in range(2):
        at = slice(h * hs, (h + 1) * hs)
        q = jnp.concatenate([ref[:, :, 0, :, at].reshape(n, hs) for ref in cur], axis=0)

        def taken(parts, base):
            lanes = [base + hs * h] * 2 + [base + hs * (1 - h)] * 2
            return jnp.concatenate([p[:, m : m + hs] for p, m in zip(parts, lanes)], axis=0)

        scores = jnp.where(mask, dot_t(q, taken(now, 0)), dot_t(q, taken(before, 0))) * scale
        w = jnp.exp2(scores).astype(BF16)
        out = dot(w * same_one, jnp.concatenate([taken(now, 2 * hs), ones], axis=1))
        out = out + dot(w * prev_one, jnp.concatenate([taken(before, 2 * hs), ones], axis=1))
        shape = (4, 2, HALF, hs)
        for i in range(2):
            half = out[n * i : n * (i + 1)]
            accs[i][:, :, 0, :, at] = half[:, :hs].astype(BF16).reshape(shape)
            dens[i][:, :, 0, :, at] = half[:, hs:].reshape(shape)
    for keep, value in zip(above, now):
        keep[...] = value


def row_attention(top, kcol, qkv, their_qkv, edge, their_edge, hs, inv_root):
    rows = qkv[0].shape[2]
    now = pl.BlockSpec((4, 2, 1, HALF, 6 * hs), lambda r: (0, 0, r, 0, 0))
    keys = pl.BlockSpec((4, 2, 1, HALF, 2 * hs), lambda r: (0, 0, r, 0, 1))
    values = pl.BlockSpec((4, 2, 1, HALF, 2 * hs), lambda r: (0, 0, r, 0, 2))
    whole = lambda a: pl.BlockSpec(a.shape, lambda r: (0,) * a.ndim)
    out = lambda kind: jax.ShapeDtypeStruct((4, 2, rows, HALF, 2 * hs), kind)
    out_spec = pl.BlockSpec((4, 2, 1, HALF, 2 * hs), lambda r: (0, 0, r, 0, 0))
    n = kcol.shape[1] // 2
    outs = pl.pallas_call(
        lambda *refs: row_body(inv_root, hs, *refs),
        grid=(rows,),
        in_specs=[SMEM, whole(kcol), now, now, keys, values, keys, values]
        + [whole(e) for e in (*edge, *their_edge)],
        out_specs=[out_spec] * 4,
        out_shape=[out(BF16)] * 2 + [out(F32)] * 2,
        scratch_shapes=[pltpu.VMEM((n // 2, 4 * hs), BF16)] * 4 + [pltpu.VMEM((n, 128), F32)],
        cost_estimate=cost(rows * 32 * n * n * hs, rows * 32 * n * hs, rows * 4 * n * n),
        name="row_attention",
    )(
        top, kcol, *qkv, their_qkv[0], their_qkv[0], their_qkv[1], their_qkv[1],
        *edge, *their_edge,
    )
    return outs[:2], outs[2:]


def col_body(inv_root, hs, own_rows, bias, their_bias, x, *refs):
    out = refs[-1]
    rows, cols, _ = x.shape
    chunk = 16
    spots = rows * cols
    step = chunk * cols
    log2e = math.log2(math.e)
    lane = lax.broadcasted_iota(jnp.int32, (step, 128), 1)
    spot = lax.broadcasted_iota(jnp.int32, (step, 128), 0) & (cols - 1)
    ones = jnp.ones((spots, hs), BF16)

    def part(at):
        return x[:, :, at * hs : (at + 1) * hs].reshape(spots, hs)

    den_rows = []
    for i in range(rows // chunk):
        n = step * (i + 1)
        qi = lax.broadcasted_iota(jnp.int32, (step, n), 0) + step * i
        ki = lax.broadcasted_iota(jnp.int32, (step, n), 1)
        keep = jnp.logical_and(((qi - ki) & (cols - 1)) == 0, ki < qi)
        laid_out = 0.0
        for h in range(2):
            q, k, v = part(h), part(2 + h), part(4 + h)
            s = dot_t(q[step * i : n], k[:n]) * (inv_root * log2e)
            s = s + (bias, their_bias)[h][0] * log2e
            w = jnp.where(keep, jnp.exp2(s), 0.0).astype(BF16)
            a = dot(w, jnp.concatenate([v[:n], ones[:n]], axis=1))
            laid_out = laid_out + jnp.where(lane == spot + cols * h, a[:, hs:], 0.0)
            a = a[:, :hs].astype(BF16).reshape(chunk, cols, hs)
            for j in range(chunk):
                r = chunk * i + j
                out[r // own_rows, 0, r % own_rows, :, h * hs : (h + 1) * hs] = a[j]
        den_rows.append(jnp.sum(laid_out.reshape(chunk, cols, 128), axis=1))
    den_rows = jnp.concatenate(den_rows, axis=0)
    fill = jnp.zeros((cols - own_rows, 128), F32)
    for b in range(rows // own_rows):
        block = jnp.concatenate([den_rows[own_rows * b : own_rows * (b + 1)], fill], axis=0)
        out[b, 0, own_rows, :, 0:128] = block.astype(BF16)
        out[b, 0, own_rows, :, 128:256] = jnp.zeros((cols, 128), BF16)


def column_attention(group, bias, x, own_rows, hs, inv_root, earlier=()):
    rows, cols, _ = x.shape
    spots = rows * cols
    peers = rows // own_rows
    return pl.pallas_call(
        lambda *refs: col_body(inv_root, hs, own_rows, *refs),
        grid=(1,),
        in_specs=[SMEM, SMEM, pl.BlockSpec(x.shape, lambda i: (0, 0, 0))]
        + [pl.BlockSpec(memory_space=pl.ANY)] * len(earlier),
        out_specs=pl.BlockSpec(
            (peers, 1, own_rows + 1, cols, 2 * hs), lambda i: (0, group, 0, 0, 0)
        ),
        out_shape=jax.ShapeDtypeStruct((peers, 2, own_rows + 1, cols, 2 * hs), BF16),
        input_output_aliases={3: 0} if earlier else {},
        cost_estimate=cost(6 * spots * spots * hs, 16 * spots * hs, 2 * spots * spots),
        name="column_attention",
    )(*bias, x, *earlier)


def term_body(hs, rows, splits, got, acc, den, *refs):
    count = len({slot for slot, _, _ in splits})
    ffs, (w_mine, w_their), outs = refs[:count], refs[count : count + 2], refs[count + 2 :]
    spots = 2 * count * rows * HALF
    lines = 2 * count * HALF
    unit = lax.broadcasted_iota(jnp.int32, (spots, lines), 0) // HALF
    line = lax.broadcasted_iota(jnp.int32, (spots, lines), 1)
    hit = jnp.logical_and(unit == (line // HALF) * rows + line % HALF, line % HALF < rows)
    table = got[:, 0, rows, :, 0:128].reshape(lines, 128)
    table = dot(jnp.where(hit, 1.0, 0.0).astype(BF16), table)
    lane = lax.broadcasted_iota(jnp.int32, (spots, 128), 1)
    spot = lax.broadcasted_iota(jnp.int32, (spots, 128), 0) % HALF
    ones = jnp.ones((128, 128), BF16)
    parts = []
    for h in range(2):
        at = slice(h * hs, (h + 1) * hs)
        col_den = dot(jnp.where(lane == spot + HALF * h, table, 0.0).astype(BF16), ones)
        total = acc[:, :, :, :, at].reshape(spots, hs).astype(F32)
        total = total + got[:, 0, 0:rows, :, at].reshape(spots, hs).astype(F32)
        parts.append((total / (den[:, :, :, :, at].reshape(spots, hs) + col_den)).astype(BF16))
    halves = jnp.concatenate(parts, axis=1).reshape(count, 2, rows, HALF, 2 * hs)
    blocks = [halves[s, g, r] for s in range(count) for r in range(rows) for g in range(2)]
    attended = jnp.concatenate(blocks, axis=0)
    att_f = attended.astype(F32)
    squares = jnp.sum(att_f * att_f, axis=-1, keepdims=True)
    weight = jnp.concatenate([w_mine[...], w_their[...]], axis=0)
    term = dot(attended, weight).astype(BF16)
    width = term.shape[1]
    for out, (slot, low, high) in zip(outs, splits):
        f = ffs[slot]
        tokens = f.shape[0]
        at = slice(tokens * slot + low, tokens * slot + high)
        out[:, 0:width] = f[low:high, 0:width] + term[at]
        out[:, width:] = (f[low:high, width:].astype(F32) + squares[at]).astype(BF16)


def terms(group, base, got, acc, den, ff, w_mine, w_their, hs, rows, splits):
    tokens, full = ff[0].shape
    count = len(ff)
    whole = lambda a: pl.BlockSpec(a.shape, lambda i: (0,) * a.ndim)
    local = pl.BlockSpec((count, 2, rows, HALF, 2 * hs), lambda i: (base // count, 0, 0, 0, 0))
    return pl.pallas_call(
        lambda *refs: term_body(hs, rows, splits, *refs),
        grid=(1,),
        in_specs=[
            pl.BlockSpec(
                (2 * count, 1, rows + 1, HALF, 2 * hs), lambda i: (base // count, group, 0, 0, 0)
            ),
            local,
            local,
        ]
        + [whole(a) for a in (*ff, w_mine, w_their)],
        out_specs=[pl.BlockSpec((b - a, full), lambda i: (0, 0)) for _, a, b in splits],
        out_shape=[jax.ShapeDtypeStruct((b - a, full), BF16) for _, a, b in splits],
        cost_estimate=cost(4 * count * tokens * hs * full, 5 * count * tokens * full),
        name="terms",
    )(got, acc, den, *ff, w_mine, w_their)


def halves_body(t0, t1, o0, o1):
    o0[...] = t0[...]
    o1[...] = t1[...]


def halves_of(first, second):
    rows, width = first.shape
    block = lambda at: pl.BlockSpec((rows // 2, width), lambda i: (at, 0))
    return pl.pallas_call(
        halves_body,
        grid=(1,),
        in_specs=[block(0), block(1)],
        out_specs=[block(0)] * 2,
        out_shape=[jax.ShapeDtypeStruct((rows // 2, width), BF16)] * 2,
        cost_estimate=cost(0, 4 * rows * width),
        name="halves",
    )(first, second)


def far_body(t0, t1, t2, g0, g1, g2, o0, o1, o2):
    for t, g, o in ((t0, g0, o0), (t1, g1, o1), (t2, g2, o2)):
        o[...] = t[...] + g[...]


def add_far(arrays, parts):
    third, width = parts[0].shape
    block = lambda at: pl.BlockSpec((third, width), lambda i: (at, 0))
    spread = [block(0), block(1), block(2)]
    return pl.pallas_call(
        far_body,
        grid=(1,),
        in_specs=spread + [block(0)] * 3,
        out_specs=spread,
        out_shape=[jax.ShapeDtypeStruct(arrays[0].shape, BF16)] * 3,
        input_output_aliases={0: 0, 1: 1, 2: 2},
        cost_estimate=cost(6 * third * width, 18 * third * width),
        name="add_far",
    )(*arrays, *parts)


def near_body(t0, t1, r0, r1, r2, o0, o1):
    o0[...] = t0[...] + (r0[...] + r1[...])
    o1[...] = t1[...] + r2[...]


def add_near(*arrays):
    rows, width = arrays[0].shape
    return pl.pallas_call(
        near_body,
        in_specs=[VMEM] * 5,
        out_specs=[VMEM] * 2,
        out_shape=[jax.ShapeDtypeStruct((rows, width), BF16)] * 2,
        cost_estimate=cost(3 * rows * width, 14 * rows * width),
        name="add_near",
    )(*arrays)


def head_body(x, mine, m0, m1, m2, targets, gain, weight, layer_out, line):
    width = x.shape[1]
    mixed, spread = 0.0, 0.0
    for m in (mine, m0, m1, m2):
        mixed = mixed + m[:, :width].astype(F32)
        spread = spread + m[:, width : width + 1].astype(F32)
    lo = (x[...].astype(F32) + mixed).astype(BF16)
    layer_out[...] = lo
    back = lo.astype(F32)
    inv_norm = lax.rsqrt(jnp.sum(back * back, axis=-1, keepdims=True) / width + EPS)
    head_in = (back * inv_norm * gain[...]).astype(BF16)
    raised = jnp.exp(dot(head_in, weight[...]))
    prob = raised / jnp.sum(raised, axis=-1, keepdims=True)
    levels = lax.broadcasted_iota(jnp.int32, prob.shape, 1)
    grad = prob - jnp.where(levels == targets[...], 1.0, 0.0)
    scaled = gain[...] * dot_t(grad.astype(BF16), weight[...])
    lean = jnp.sum(back * scaled, axis=-1, keepdims=True) / width
    layer_grad = inv_norm * scaled - back * (inv_norm * inv_norm * inv_norm) * lean
    head_f = head_in.astype(F32)
    out_sq = jnp.sum(head_f * head_f, axis=-1, keepdims=True) * jnp.sum(
        grad * grad, axis=-1, keepdims=True
    )
    layer_sq = jnp.sum(layer_grad * layer_grad, axis=-1, keepdims=True)
    norm = jnp.sqrt(laid(out_sq + spread * layer_sq))
    line[...] = jnp.broadcast_to(norm[None], line.shape)


def head(x, mine, m0, m1, m2, targets, gain, weight, devices):
    return pl.pallas_call(
        head_body,
        in_specs=[VMEM] * 8,
        out_specs=[pl.BlockSpec(memory_space=pltpu.VMEM)] * 2,
        out_shape=[
            jax.ShapeDtypeStruct(x.shape, BF16),
            jax.ShapeDtypeStruct((devices, 1, 256), F32),
        ],
        name="head",
    )(x, mine, m0, m1, m2, targets, gain, weight)


def pick_body(table, where, spot, out):
    devices = table.shape[0]
    count = where.shape[1]
    hit = lax.broadcasted_iota(jnp.int32, (devices, count), 0) == where[...]
    hot = jnp.where(hit, 1.0, 0.0).astype(BF16)

    full = table[...]
    high = full.astype(BF16)
    rest = full - high.astype(F32)
    mid = rest.astype(BF16)
    low = (rest - mid.astype(F32)).astype(BF16)
    parts = jnp.concatenate([high, mid, low], axis=0)
    lines = lax.dot_general(
        parts,
        jnp.concatenate([hot, hot, hot], axis=0),
        (((0,), (0,)), ((), ())),
        preferred_element_type=F32,
    )
    mine = lax.broadcasted_iota(jnp.int32, lines.shape, 0) == spot[...]
    picked = jnp.sum(jnp.where(mine, lines, 0.0), axis=0, keepdims=True)
    out[...] = count * picked / jnp.sum(picked, axis=-1, keepdims=True)


def pick(table, where, spot):
    return pl.pallas_call(
        pick_body,
        in_specs=[pl.BlockSpec(memory_space=pltpu.VMEM)] * 3,
        out_specs=pl.BlockSpec(memory_space=pltpu.VMEM),
        out_shape=jax.ShapeDtypeStruct(where.shape, F32),
        name="pick",
    )(table, where, spot)


def per_device(
    activations,
    targets,
    candidates,
    mix_gain,
    project_weight,
    output_weight,
    up_weight,
    down_weight,
    pattern_bias,
    head_gain,
    head_weight,
):
    rows, cols, width = activations.shape
    hs = project_weight.shape[2]
    tokens = rows * cols
    row_peers = lax.axis_size(ROW)
    inv_root = 1.0 / math.sqrt(hs)
    third = tokens // 3

    devices = lax.axis_size(ALL)

    their_project = swap_core(project_weight)
    their_up = swap_core(up_weight)
    their_down = swap_core(down_weight)
    their_output = swap_core(output_weight)
    bias = (pattern_bias, swap_core(pattern_bias))

    x = activations.reshape(tokens, width)
    own = normalize(x, mix_gain[None, :])

    def after(first, values):
        return lax.optimization_barrier((first, values))[1]

    def ffn(shards, slots):
        return feed_forward(shards, slots, up_weight, their_up, down_weight, their_down)

    xl, z, core = lax.axis_index(XL), lax.axis_index(Z), lax.axis_index(CORE)
    n_z = lax.axis_size(Z)
    shift_x = jnp.array([0, 0, 0, 1, 0, 1, 1, 1], jnp.int32)
    shift_z = jnp.array([0, 3, 1, 0, 2, 3, 1, 2], jnp.int32)
    chip = ((xl + shift_x) % 2) * n_z + (z + shift_z) % n_z
    starts = chip * 2 * cols
    offs = jnp.arange(cols, dtype=jnp.int32)
    mine = (starts[:, None] + core * cols + offs[None, :]).reshape(-1)
    theirs = (starts[:, None] + (1 - core) * cols + offs[None, :]).reshape(-1)
    columns_of = jnp.concatenate([mine, theirs])[None, :]

    near = (up_z(own), down_z(own), swap_x(own))
    (ff_own,) = ffn((own,), 1)
    s_a, s_b, s_p = after((ff_own, their_project, columns_of), near)
    s_aa, s_pb, s_pa = up_z(s_a), down_z(s_p), swap_x(s_a)

    def columns(shards):
        qkv, edge = project(shards, project_weight, their_project, rows)
        got = lax.all_to_all(
            qkv.reshape(row_peers, rows * HALF, 6 * hs), ROW, split_axis=0, concat_axis=0, tiled=True
        )
        return qkv, edge, got

    def attend_columns(group, got, *earlier):
        x = got.reshape(row_peers * rows, HALF, 6 * hs)
        return column_attention(group, bias, x, rows, hs, inv_root, earlier)

    qkv0, edge0, got0 = columns((own, s_a, s_b, s_p))
    edge0 = next_row(edge0)
    their_edge0 = swap_core(edge0)
    their_qkv0 = swap_core(qkv0)
    s_aa, s_pa, s_pb = after(qkv0, (s_aa, s_pa, s_pb))
    h_pa, h_pb = halves_of(s_pa, s_pb)
    far = (up_z(h_pa), down_z(h_pb))
    away = after(their_qkv0, (s_aa, s_pa, s_pb, *far))
    qkv1, edge1, got1 = columns(away)
    back = attend_columns(0, after(qkv1, got0))
    their_qkv1 = swap_core(qkv1)
    edge1 = next_row(edge1)
    their_edge1 = swap_core(edge1)
    ff1 = ffn(after((qkv1, back), away), 4)
    back = attend_columns(1, after((ff1, their_qkv1), got1), back)
    again = lax.all_to_all(back, ROW, split_axis=0, concat_axis=0, tiled=True)

    top = (lax.axis_index(ROW) == 0).astype(jnp.int32)[None]
    acc, den = row_attention(
        after(back, top),
        columns_of,
        (qkv0, qkv1),
        (their_qkv0, their_qkv1),
        (edge0, edge1),
        (their_edge0, their_edge1),
        hs,
        inv_root,
    )
    f0, f1, f2 = terms(
        1, 3, again, acc[1], den[1], ff1[3:], output_weight, their_output, hs, rows,
        [(0, third * i, third * (i + 1)) for i in range(3)],
    )
    g0, g1, g2 = swap_x(f0), down_z(f1), up_z(f2)
    t_aa, t_pa, t_pb = terms(
        1, 0, *after(f0, (again, acc[1], den[1])), ff1[:3], output_weight, their_output, hs, rows,
        [(i, 0, tokens) for i in range(3)],
    )

    t_aa, t_pa, t_pb = add_far((t_aa, t_pa, t_pb), (g0, g1, g2))
    r_aa, r_pa, r_pb = down_z(t_aa), swap_x(t_pa), up_z(t_pb)
    ff0 = ffn(after(t_pb, (s_a, s_b, s_p)), 3)
    t_own, t_a, t_b, t_p = terms(
        0, 0, again, acc[0], den[0], (ff_own, *ff0), output_weight, their_output, hs, rows,
        [(i, 0, tokens) for i in range(4)],
    )
    from_b = up_z(t_b)
    t_a, t_p = add_near(t_a, t_p, r_aa, r_pa, r_pb)
    from_a, from_p = down_z(t_a), swap_x(t_p)

    layer_out, line = head(
        x,
        t_own,
        from_a,
        from_b,
        from_p,
        targets.reshape(tokens, 1),
        head_gain[None, :],
        head_weight,
        devices,
    )
    table = lax.all_to_all(
        line,
        ALL,
        split_axis=0,
        concat_axis=0,
        tiled=True,
    ).reshape(devices, 256)
    full_cols = cols * lax.axis_size(COL)
    c_row, c_col = candidates // full_cols, candidates % full_cols
    where = (c_row // rows) * lax.axis_size(COL) + c_col // cols
    spot = (c_row % rows) * cols + c_col % cols
    chosen = pick(table, where[None, :], spot[None, :])
    return (layer_out.reshape(rows, cols, width), chosen.reshape(-1))


def solution(mesh):
    split = Mesh(mesh.devices.reshape(2, 4, 2, 4, 2), ("row_0", "row_1", "col_0", "col_1", "col_2"))

    return jax.shard_map(
        per_device,
        mesh=split,
        in_specs=(
            P(ROW, COL, None),
            P(ROW, COL),
            P(),
            P(),
            P(None, None, COL),
            P(COL, None),
            P(None, COL),
            P(COL, None),
            P(COL),
            P(),
            P(),
        ),
        out_specs=(P(ROW, COL, None), P()),
        check_vma=False,
    )
```
